32 devices in a mesh: wide: 8 (over z, y), narrow: 4 (over x, core).
Axes of the slice: x: 2, y: 2, z: 4, core: 2. Of those that a mesh axis runs over, the one named last changes fastest.
Arguments:
- inputs: bfloat16 [16384, 1024], P(('wide', 'narrow')), may hold values from -6 to 6
- segment_ids: int32 [16384], P(('wide', 'narrow')), may hold values from -1 to 7, as said below
- cotangent: bfloat16 [16384, 1024], P(('wide', 'narrow')), may hold values from -6 to 6
- ln1_gain: bfloat16 [1024], P(('wide', 'narrow')), may hold values from 0.5 to 1.5
- ln1_shift: bfloat16 [1024], P(('wide', 'narrow')), may hold values from -3 to 3
- w_qkv: bfloat16 [1024, 3072], P(('wide', 'narrow')), may hold values from -0.1875 to 0.1875
- query_bias: bfloat16 [1024], P(('wide', 'narrow')), may hold values from -3 to 3
- value_bias: bfloat16 [1024], P(('wide', 'narrow')), may hold values from -3 to 3
- w_out: bfloat16 [1024, 1024], P(('wide', 'narrow')), may hold values from -1.5 to 1.5
- out_bias: bfloat16 [1024], P(('wide', 'narrow')), may hold values from -3 to 3
- ln2_gain: bfloat16 [1024], P(('wide', 'narrow')), may hold values from 0.5 to 1.5
- ln2_shift: bfloat16 [1024], P(('wide', 'narrow')), may hold values from -3 to 3
- w_in: bfloat16 [1024, 4096], P(('wide', 'narrow')), may hold values from -0.1875 to 0.1875
- in_bias: bfloat16 [4096], P(('wide', 'narrow')), may hold values from -3 to 3
- w_down: bfloat16 [4096, 1024], P(('wide', 'narrow')), may hold values from -0.125 to 0.125
- down_bias: bfloat16 [1024], P(('wide', 'narrow')), may hold values from -3 to 3
Outputs:
- layer_out: float32 [16384, 1024], P(('wide', 'narrow'))
- grad_input: float32 [16384, 1024], P(('wide', 'narrow'))
- grad_ln1_gain: float32 [1024], P(('wide', 'narrow'))
- grad_ln1_shift: float32 [1024], P(('wide', 'narrow'))
- grad_w_qkv: float32 [1024, 3072], P(('wide', 'narrow'))
- grad_query_bias: float32 [1024], P(('wide', 'narrow'))
- grad_value_bias: float32 [1024], P(('wide', 'narrow'))
- grad_w_out: float32 [1024, 1024], P(('wide', 'narrow'))
- grad_out_bias: float32 [1024], P(('wide', 'narrow'))
- grad_ln2_gain: float32 [1024], P(('wide', 'narrow'))
- grad_ln2_shift: float32 [1024], P(('wide', 'narrow'))
- grad_w_in: float32 [1024, 4096], P(('wide', 'narrow'))
- grad_in_bias: float32 [4096], P(('wide', 'narrow'))
- grad_w_down: float32 [4096, 1024], P(('wide', 'narrow'))
- grad_down_bias: float32 [1024], P(('wide', 'narrow'))
The draws below stay inside these ranges and needn't reach their ends.
Inputs may be any that keep to these rules, and one draw needn't show every extreme that they name: `segment_ids`: within each sequence of 512 slots the live slots come first, with ids 0 to 7 that start at 0 and never fall, every id present; the last 1 to 64 slots are padding with id -1.
All inputs are finite; a program needn't handle non-finite values.
Results may differ from the reference program's by a relative error of at most 0.012.
Values may be sent and summed in bfloat16 or wider, within the bound.
A program may use at most 192 MiB of HBM per device.

```python
import jax
import jax.numpy as jnp
from jax import lax

D = 1024
HD = 64
FF = 4096
TOK_DEV = 512
TOKENS = 16384


def draw_segment_ids(key, part):
    seq_count = TOKENS // TOK_DEV
    key_jitter = jax.random.fold_in(key, 11)
    key_padding = jax.random.fold_in(key, 23)
    spacing = TOK_DEV // 9
    jitter_range = max(TOK_DEV // 18, 1)
    position = jnp.arange(TOK_DEV, dtype=jnp.int32)[None, None, :]
    steps = jnp.arange(1, 8, dtype=jnp.int32)[None, :]
    bounds = steps * spacing + jax.random.randint(key_jitter, (seq_count, 7), 0, jitter_range)
    labels = jnp.sum((position >= bounds[:, :, None]).astype(jnp.int32), axis=1).astype(jnp.int32)
    padding = jax.random.randint(key_padding, (seq_count, 1), 1, TOK_DEV // 8 + 1)
    labels = jnp.where(position[0] >= TOK_DEV - padding, -1, labels)
    return labels.reshape(-1).astype(jnp.int32)


def block_scale(own_key, dims, cuts, low, high):
    level = 1.0
    for dim, shards_of in cuts:
        steps = jax.random.uniform(jax.random.fold_in(jax.random.fold_in(own_key, 6), dim), (shards_of,), jnp.float32, low / len(cuts), high / len(cuts))
        level = level * jnp.repeat(jnp.exp(steps), dims[dim] // shards_of).reshape((-1,) + (1,) * (len(dims) - 1 - dim))
    return level


def gaussian(rng, shape, width, bound, cuts=(), held_as=jnp.bfloat16):
    values = width * jax.random.normal(rng, shape, jnp.float32)
    if cuts:
        values = values * block_scale(rng, shape, cuts, -0.22, 0.18)
    return jnp.clip(values, -bound, bound).astype(held_as)


def setup_inputs(seed: int = 0) -> dict:
    streams_of = jax.random.split(jax.random.key(seed), 17)
    inputs = gaussian(streams_of[0], (TOKENS, D), 1.0, 6.0, ((0, 32),))
    segment_ids = draw_segment_ids(jax.random.fold_in(streams_of[16], 71), 0)
    cotangent = gaussian(streams_of[2], (TOKENS, D), 1.0, 6.0, ((0, 32),))
    ln1_gain = jnp.clip(1.0 + 0.1 * jax.random.normal(streams_of[3], (D,), jnp.float32), 0.5, 1.5).astype(jnp.bfloat16)
    ln1_shift = gaussian(streams_of[4], (D,), 0.3, 3.0, ((0, 32),))
    w_qkv = gaussian(streams_of[5], (D, 3 * D), D ** -0.5, 0.1875, ((0, 32),))
    query_bias = gaussian(streams_of[6], (D,), 0.3, 3.0, ((0, 32),))
    value_bias = gaussian(streams_of[7], (D,), 0.3, 3.0, ((0, 32),))
    w_out = gaussian(streams_of[8], (D, D), (D // 64) ** -0.5, 1.5, ((0, 32),))
    out_bias = gaussian(streams_of[9], (D,), 0.3, 3.0, ((0, 32),))
    ln2_gain = jnp.clip(1.0 + 0.1 * jax.random.normal(streams_of[10], (D,), jnp.float32), 0.5, 1.5).astype(jnp.bfloat16)
    ln2_shift = gaussian(streams_of[11], (D,), 0.3, 3.0, ((0, 32),))
    w_in = gaussian(streams_of[12], (D, FF), D ** -0.5, 0.1875, ((0, 32),))
    in_bias = gaussian(streams_of[13], (FF,), 0.5, 3.0, ((0, 32),))
    w_down = gaussian(streams_of[14], (FF, D), (FF // 2) ** -0.5, 0.125, ((0, 32),))
    down_bias = gaussian(streams_of[15], (D,), 0.3, 3.0, ((0, 32),))
    return {"inputs": inputs, "segment_ids": segment_ids, "cotangent": cotangent, "ln1_gain": ln1_gain, "ln1_shift": ln1_shift, "w_qkv": w_qkv, "query_bias": query_bias, "value_bias": value_bias, "w_out": w_out, "out_bias": out_bias, "ln2_gain": ln2_gain, "ln2_shift": ln2_shift, "w_in": w_in, "in_bias": in_bias, "w_down": w_down, "down_bias": down_bias}


EPS = 1e-05
HIGH = lax.Precision.HIGHEST

@jax.custom_vjp
def low(v):
    return lax.optimization_barrier(v.astype(jnp.bfloat16)).astype(jnp.float32)

@jax.custom_vjp
def low_back(v):
    return v

def low_keep(v):
    return (low(v), None)

def low_pass(kept, grad):
    return (grad,)

def back_keep(v):
    return (v, None)

def back_low(kept, grad):
    return (low(grad),)
low.defvjp(low_keep, low_pass)
low_back.defvjp(back_keep, back_low)

def layer_norm(values, gain, shift):
    average = lax.optimization_barrier(jnp.mean(values, -1, keepdims=True))
    centred = values - average
    variance = lax.optimization_barrier(jnp.mean(centred * centred, -1, keepdims=True))
    return centred * lax.rsqrt(variance + EPS) * gain + shift

def block_forward(tokens, labels, params):
    ln1_gain, ln1_shift, w_qkv, query_bias, value_bias, w_out, out_bias, ln2_gain, ln2_shift, w_in, in_bias, w_down, down_bias = params
    length = tokens.shape[0]
    heads = D // HD
    norm_one = low(layer_norm(tokens, ln1_gain, ln1_shift))
    shifts = jnp.concatenate([query_bias, jnp.zeros_like(query_bias), value_bias])
    triple = low(low_back(jnp.dot(norm_one, w_qkv, precision=HIGH) + shifts))
    queries = triple[:, :D].reshape(length, heads, HD)
    key_rows = triple[:, D:2 * D].reshape(length, heads, HD)
    values = triple[:, 2 * D:].reshape(length, heads, HD)
    position = jnp.arange(length, dtype=jnp.int32)
    allowed = (labels[:, None] == labels[None, :]) & (labels[:, None] >= 0) | (position[:, None] == position[None, :])
    scores = low_back(jnp.einsum('qhd,khd->hqk', queries, key_rows, precision=HIGH) * HD ** (-0.5))
    scores = jnp.where(allowed[None], scores, -1000000000.0)
    attn_probs = low(jax.nn.softmax(scores, axis=-1))
    attended = low(low_back(jnp.einsum('hqk,khd->qhd', attn_probs, values, precision=HIGH).reshape(length, D)))
    middle = tokens + low_back(jnp.dot(attended, w_out, precision=HIGH) + out_bias)
    norm_two = low(layer_norm(middle, ln2_gain, ln2_shift))
    pre_act = low_back(jnp.dot(norm_two, w_in, precision=HIGH) + in_bias)
    hidden = low(jax.nn.gelu(pre_act, approximate=False))
    return middle + low_back(jnp.dot(hidden, w_down, precision=HIGH) + down_bias)

def reference(inputs, segment_ids, cotangent, ln1_gain, ln1_shift, w_qkv, query_bias, value_bias, w_out, out_bias, ln2_gain, ln2_shift, w_in, in_bias, w_down, down_bias):
    params = (ln1_gain.astype(jnp.float32), ln1_shift.astype(jnp.float32), w_qkv.astype(jnp.float32), query_bias.astype(jnp.float32), value_bias.astype(jnp.float32), w_out.astype(jnp.float32), out_bias.astype(jnp.float32), ln2_gain.astype(jnp.float32), ln2_shift.astype(jnp.float32), w_in.astype(jnp.float32), in_bias.astype(jnp.float32), w_down.astype(jnp.float32), down_bias.astype(jnp.float32))
    seq_count = inputs.shape[0] // TOK_DEV
    tokens = inputs.astype(jnp.float32).reshape(seq_count, TOK_DEV, D)
    labels = segment_ids.reshape(seq_count, TOK_DEV)
    grads_out = cotangent.astype(jnp.float32).reshape(seq_count, TOK_DEV, D)

    def one_sequence(totals, items):
        tok_seq, lab_seq, grad_seq = items

        def apply_block(tok_arg, param_arg):
            return block_forward(tok_arg, lab_seq, param_arg)
        result, pull = jax.vjp(apply_block, tok_seq, params)
        grad_tok, grad_params = pull(grad_seq)
        summed = jax.tree.map(jnp.add, totals, grad_params)
        return (summed, (result, grad_tok))
    zeros = jax.tree.map(jnp.zeros_like, params)
    totals, outputs = lax.scan(one_sequence, zeros, (tokens, labels, grads_out))
    results, grad_tokens = outputs
    return (results.reshape(-1, D), grad_tokens.reshape(-1, D), totals[0], totals[1], totals[2], totals[3], totals[4], totals[5], totals[6], totals[7], totals[8], totals[9], totals[10], totals[11], totals[12])
```

```python
import jax
import jax.numpy as jnp
from jax import lax
from jax.experimental import pallas as pl
from jax.experimental.pallas import tpu as pltpu
from jax.sharding import Mesh
from jax.sharding import PartitionSpec as P

HD = 64


EPS = 1e-05
ROOT_HALF = 0.7071067811865476
INV_ROOT_TAU = 0.3989422804014327
NEG_FILL = -1000000000.0


def normalize(values, gain, shift):
    average = jnp.mean(values, -1, keepdims=True)
    centred = values - average
    inverse = lax.rsqrt(jnp.mean(centred * centred, -1, keepdims=True) + EPS)
    normed = centred * inverse
    return (normed * gain + shift, normed, inverse)


def normalize_back(grad_norm, normed, inverse, gain):
    scaled = grad_norm * gain
    return inverse * (
        scaled
        - jnp.mean(scaled, -1, keepdims=True)
        - normed * jnp.mean(scaled * normed, -1, keepdims=True)
    )


def gelu_value(pre_act):
    return 0.5 * pre_act * (1.0 + lax.erf(pre_act * ROOT_HALF))


def gelu_slope(pre_act):
    return (
        0.5 * (1.0 + lax.erf(pre_act * ROOT_HALF))
        + pre_act * jnp.exp(-0.5 * pre_act * pre_act) * INV_ROOT_TAU
    )


def gather_forward(shards):
    return (
        lax.all_gather(shards[0], ("wide", "narrow"), axis=0, tiled=True),
        lax.all_gather(shards[1], ("wide", "narrow"), axis=0, tiled=True),
        lax.all_gather(shards[2], ("wide", "narrow"), axis=0, tiled=True),
        lax.all_gather(shards[3], ("wide", "narrow"), axis=0, tiled=True),
        lax.all_gather(shards[4], ("wide", "narrow"), axis=0, tiled=True),
        lax.all_gather(shards[5], ("wide", "narrow"), axis=0, tiled=True),
        lax.all_gather(shards[6], ("wide", "narrow"), axis=0, tiled=True),
        lax.all_gather(shards[7], ("wide", "narrow"), axis=0, tiled=True),
        lax.all_gather(shards[8], ("wide", "narrow"), axis=0, tiled=True),
        lax.all_gather(shards[9], ("wide", "narrow"), axis=0, tiled=True),
        lax.all_gather(shards[10], ("wide", "narrow"), axis=0, tiled=True),
        lax.all_gather(shards[11], ("wide", "narrow"), axis=0, tiled=True),
        lax.all_gather(shards[12], ("wide", "narrow"), axis=0, tiled=True),
    )


def gather_backward(shards):
    return (
        lax.all_gather(shards[0], ("wide", "narrow"), axis=0, tiled=True),
        lax.all_gather(shards[1], ("wide", "narrow"), axis=0, tiled=True),
        lax.all_gather(shards[2], ("wide", "narrow"), axis=0, tiled=True),
        lax.all_gather(shards[3], ("wide", "narrow"), axis=0, tiled=True),
        lax.all_gather(shards[4], ("wide", "narrow"), axis=0, tiled=True),
        lax.all_gather(shards[5], ("wide", "narrow"), axis=0, tiled=True),
        lax.all_gather(shards[6], ("wide", "narrow"), axis=0, tiled=True),
        lax.all_gather(shards[7], ("wide", "narrow"), axis=0, tiled=True),
        lax.all_gather(shards[8], ("wide", "narrow"), axis=0, tiled=True),
        lax.all_gather(shards[9], ("wide", "narrow"), axis=0, tiled=True),
        lax.all_gather(shards[10], ("wide", "narrow"), axis=0, tiled=True),
        lax.all_gather(shards[11], ("wide", "narrow"), axis=0, tiled=True),
        lax.all_gather(shards[12], ("wide", "narrow"), axis=0, tiled=True),
    )


def reduce_grads(grads):
    return (
        lax.psum_scatter(grads[0], ("wide", "narrow"), scatter_dimension=0, tiled=True),
        lax.psum_scatter(grads[1], ("wide", "narrow"), scatter_dimension=0, tiled=True),
        lax.psum_scatter(grads[2], ("wide", "narrow"), scatter_dimension=0, tiled=True),
        lax.psum_scatter(grads[3], ("wide", "narrow"), scatter_dimension=0, tiled=True),
        lax.psum_scatter(grads[4], ("wide", "narrow"), scatter_dimension=0, tiled=True),
        lax.psum_scatter(grads[5], ("wide", "narrow"), scatter_dimension=0, tiled=True),
        lax.psum_scatter(grads[6], ("wide", "narrow"), scatter_dimension=0, tiled=True),
        lax.psum_scatter(grads[7], ("wide", "narrow"), scatter_dimension=0, tiled=True),
        lax.psum_scatter(grads[8], ("wide", "narrow"), scatter_dimension=0, tiled=True),
        lax.psum_scatter(grads[9], ("wide", "narrow"), scatter_dimension=0, tiled=True),
        lax.psum_scatter(grads[10], ("wide", "narrow"), scatter_dimension=0, tiled=True),
        lax.psum_scatter(grads[11], ("wide", "narrow"), scatter_dimension=0, tiled=True),
        lax.psum_scatter(grads[12], ("wide", "narrow"), scatter_dimension=0, tiled=True),
    )


def head_block(triple_b, offset, group_width, d_model):
    length = triple_b.shape[0]
    queries = triple_b[:, offset : offset + group_width].reshape(length, group_width // HD, HD)
    key_rows = triple_b[:, d_model + offset : d_model + offset + group_width].reshape(
        length, group_width // HD, HD
    )
    values = triple_b[:, 2 * d_model + offset : 2 * d_model + offset + group_width].reshape(
        length, group_width // HD, HD
    )
    return (queries, key_rows, values)


def block_scores(queries, key_rows, allowed):
    scores = jnp.einsum(
        "qhd,khd->hqk", queries, key_rows, preferred_element_type=jnp.float32
    ) * HD ** (-0.5)
    return jnp.where(allowed[None], scores, NEG_FILL)


def attend(triple_b, allowed, d_model):
    length = triple_b.shape[0]
    group_width = 4 * HD
    pieces = []
    log_totals = []
    for offset in range(0, d_model, group_width):
        queries, key_rows, values = head_block(triple_b, offset, group_width, d_model)
        scores = block_scores(queries, key_rows, allowed)
        highest = jnp.max(scores, -1, keepdims=True)
        exponent = jnp.exp(scores - highest)
        row_total = jnp.sum(exponent, -1, keepdims=True)
        probs_low = (exponent / row_total).astype(jnp.bfloat16)
        mixed = jnp.einsum("hqk,khd->qhd", probs_low, values, preferred_element_type=jnp.float32)
        pieces.append(mixed.reshape(length, group_width))
        log_totals.append(highest + jnp.log(row_total))
    return (jnp.concatenate(pieces, 1), log_totals)


def attend_back(triple_b, grad_att_b, allowed, log_totals, d_model):
    length = triple_b.shape[0]
    group_width = 4 * HD
    query_parts = []
    key_parts = []
    value_parts = []
    for index, offset in enumerate(range(0, d_model, group_width)):
        queries, key_rows, values = head_block(triple_b, offset, group_width, d_model)
        scores = block_scores(queries, key_rows, allowed)
        attn_probs = jnp.exp(scores - log_totals[index])
        probs_low = attn_probs.astype(jnp.bfloat16)
        grad_heads = grad_att_b[:, offset : offset + group_width].reshape(
            length, group_width // HD, HD
        )
        grad_probs = jnp.einsum(
            "qhd,khd->hqk", grad_heads, values, preferred_element_type=jnp.float32
        )
        inner_sum = jnp.sum(attn_probs * grad_probs, -1, keepdims=True)
        grad_scores = (attn_probs * (grad_probs - inner_sum)).astype(jnp.bfloat16)
        grad_query = jnp.einsum(
            "hqk,khd->qhd", grad_scores, key_rows, preferred_element_type=jnp.float32
        ) * HD ** (-0.5)
        grad_key = jnp.einsum(
            "hqk,qhd->khd", grad_scores, queries, preferred_element_type=jnp.float32
        ) * HD ** (-0.5)
        grad_value = jnp.einsum(
            "hqk,qhd->khd", probs_low, grad_heads, preferred_element_type=jnp.float32
        )
        query_parts.append(grad_query.reshape(length, group_width))
        key_parts.append(grad_key.reshape(length, group_width))
        value_parts.append(grad_value.reshape(length, group_width))
    return jnp.concatenate(query_parts + key_parts + value_parts, 1).astype(jnp.bfloat16)


def local(
    inputs,
    segment_ids,
    cotangent,
    ln1_gain,
    ln1_shift,
    w_qkv,
    query_bias,
    value_bias,
    w_out,
    out_bias,
    ln2_gain,
    ln2_shift,
    w_in,
    in_bias,
    w_down,
    down_bias,
):
    shards = (
        ln1_gain,
        ln1_shift,
        w_qkv,
        query_bias,
        value_bias,
        w_out,
        out_bias,
        ln2_gain,
        ln2_shift,
        w_in,
        in_bias,
        w_down,
        down_bias,
    )
    fwd_weights = gather_forward(shards)
    (
        gain_one,
        shift_one,
        qkv_full,
        qbias_full,
        vbias_full,
        outw_full,
        outb_full,
        gain_two,
        shift_two,
        inw_full,
        inb_full,
        downw_full,
        downb_full,
    ) = fwd_weights
    d_model = inputs.shape[1]
    length = inputs.shape[0]
    tokens = inputs.astype(jnp.float32)
    position = jnp.arange(length, dtype=jnp.int32)
    allowed = (segment_ids[:, None] == segment_ids[None, :]) & (segment_ids[:, None] >= 0) | (
        position[:, None] == position[None, :]
    )
    normed_out, normed_one, inverse_one = normalize(
        tokens, gain_one.astype(jnp.float32), shift_one.astype(jnp.float32)
    )
    norm_one = normed_out.astype(jnp.bfloat16)
    shifts = jnp.concatenate(
        [
            qbias_full.astype(jnp.float32),
            jnp.zeros((d_model,), jnp.float32),
            vbias_full.astype(jnp.float32),
        ]
    )
    triple_b = (jnp.dot(norm_one, qkv_full, preferred_element_type=jnp.float32) + shifts).astype(
        jnp.bfloat16
    )
    attended_f, log_totals = attend(triple_b, allowed, d_model)
    attended = attended_f.astype(jnp.bfloat16)
    middle = (
        tokens
        + jnp.dot(attended, outw_full, preferred_element_type=jnp.float32)
        + outb_full.astype(jnp.float32)
    )
    normed_out_two, normed_two, inverse_two = normalize(
        middle, gain_two.astype(jnp.float32), shift_two.astype(jnp.float32)
    )
    norm_two = normed_out_two.astype(jnp.bfloat16)
    pre_act = jnp.dot(norm_two, inw_full, preferred_element_type=jnp.float32) + inb_full.astype(
        jnp.float32
    )
    hidden = gelu_value(pre_act).astype(jnp.bfloat16)
    layer_out = (
        middle
        + jnp.dot(hidden, downw_full, preferred_element_type=jnp.float32)
        + downb_full.astype(jnp.float32)
    )
    back_weights = gather_backward(shards)
    (
        gain_one_b,
        shift_one_b,
        qkv_back,
        qbias_back,
        vbias_back,
        outw_back,
        outb_back,
        gain_two_b,
        shift_two_b,
        inw_back,
        inb_back,
        downw_back,
        downb_back,
    ) = back_weights
    grad_top = cotangent.astype(jnp.float32)
    grad_w_down = jnp.einsum("sf,sd->fd", hidden, cotangent, preferred_element_type=jnp.float32)
    grad_down_bias = jnp.sum(grad_top, 0)
    grad_hidden = jnp.einsum("sd,fd->sf", cotangent, downw_back, preferred_element_type=jnp.float32)
    grad_pre = (grad_hidden * gelu_slope(pre_act)).astype(jnp.bfloat16)
    grad_w_in = jnp.einsum("sd,sf->df", norm_two, grad_pre, preferred_element_type=jnp.float32)
    grad_in_bias = jnp.sum(grad_pre.astype(jnp.float32), 0)
    grad_norm_two = jnp.einsum("sf,df->sd", grad_pre, inw_back, preferred_element_type=jnp.float32)
    grad_ln2_gain = jnp.sum(grad_norm_two * normed_two, 0)
    grad_ln2_shift = jnp.sum(grad_norm_two, 0)
    grad_middle = grad_top + normalize_back(
        grad_norm_two, normed_two, inverse_two, gain_two_b.astype(jnp.float32)
    )
    grad_mixed = grad_middle.astype(jnp.bfloat16)
    grad_w_out = jnp.einsum("sd,se->de", attended, grad_mixed, preferred_element_type=jnp.float32)
    grad_out_bias = jnp.sum(grad_mixed.astype(jnp.float32), 0)
    grad_attended = jnp.einsum(
        "se,de->sd", grad_mixed, outw_back, preferred_element_type=jnp.float32
    ).astype(jnp.bfloat16)
    grad_triple = attend_back(triple_b, grad_attended, allowed, log_totals, d_model)
    grad_w_qkv = jnp.einsum("sd,st->dt", norm_one, grad_triple, preferred_element_type=jnp.float32)
    grad_query_bias = jnp.sum(grad_triple[:, :d_model].astype(jnp.float32), 0)
    grad_value_bias = jnp.sum(grad_triple[:, 2 * d_model :].astype(jnp.float32), 0)
    grad_norm_one = jnp.einsum(
        "st,dt->sd", grad_triple, qkv_back, preferred_element_type=jnp.float32
    )
    grad_ln1_gain = jnp.sum(grad_norm_one * normed_one, 0)
    grad_ln1_shift = jnp.sum(grad_norm_one, 0)
    grad_input = grad_middle + normalize_back(
        grad_norm_one, normed_one, inverse_one, gain_one_b.astype(jnp.float32)
    )
    owned = reduce_grads(
        (
            grad_ln1_gain,
            grad_ln1_shift,
            grad_w_qkv,
            grad_query_bias,
            grad_value_bias,
            grad_w_out,
            grad_out_bias,
            grad_ln2_gain,
            grad_ln2_shift,
            grad_w_in,
            grad_in_bias,
            grad_w_down,
            grad_down_bias,
        )
    )
    return (
        layer_out,
        grad_input,
        owned[0],
        owned[1],
        owned[2],
        owned[3],
        owned[4],
        owned[5],
        owned[6],
        owned[7],
        owned[8],
        owned[9],
        owned[10],
        owned[11],
        owned[12],
    )


MESH_ID = pl.DeviceIdType.MESH
ROWS = 32


def chip_index(z, y, x):
    return (z * 2 + y) * 2 + x


class Place:
    def __init__(self):
        self.z = lax.axis_index("z")
        self.y = lax.axis_index("y")
        self.x = lax.axis_index("x")
        self.c = lax.axis_index("c")

    def chip(self, dz=0, dy=0, dx=0):
        z = self.z
        if dz == 2:
            z = lax.rem(z + 2, 4)
        elif dz == 1:
            z = z + 1 - 2 * lax.rem(z, 2)
        elif dz == 3:
            z = 3 - z
        y = 1 - self.y if dy else self.y
        x = 1 - self.x if dx else self.x
        return z, y, x

    def index(self, dz=0, dy=0, dx=0):
        return chip_index(*self.chip(dz, dy, dx))

    def device(self, dz=0, dy=0, dx=0):
        z, y, x = self.chip(dz, dy, dx)
        return {"z": z, "y": y, "x": x, "c": self.c}

    def partner(self):
        return {"z": self.z, "y": self.y, "x": self.x, "c": 1 - self.c}

    def greet(self):
        barrier = pltpu.get_barrier_semaphore()
        peers = [self.device(dz=1), self.device(dz=2), self.device(dz=3)]
        peers += [self.device(dy=1), self.device(dx=1), self.partner()]
        for peer in peers:
            pl.semaphore_signal(barrier, inc=1, device_id=peer, device_id_type=MESH_ID)
        pl.semaphore_wait(barrier, len(peers))


Z_AT, X_AT, Y_AT, D_AT = -1, 3, 7, 11


class Gather:
    def __init__(self, place, blocks, sent, came):
        self.p, self.blocks, self.sent, self.came = place, blocks, sent, came
        self.out = []

    def copy(self, block, slot, device):
        return pltpu.make_async_remote_copy(
            src_ref=self.blocks.at[block],
            dst_ref=self.blocks.at[block],
            send_sem=self.sent.at[slot],
            recv_sem=self.came.at[slot],
            device_id=device,
            device_id_type=MESH_ID,
        )

    def send(self, block, slot, device):
        copy = self.copy(block, slot, device)
        copy.start()
        self.out.append(copy)

    def wait(self, block, slot):
        self.copy(block, slot, self.p.device(dx=1)).wait_recv()

    def begin(self):
        own = self.p.index()
        for dz in (3, 2, 1):
            self.send(own, Z_AT + dz, self.p.device(dz=dz))
        self.send(own, X_AT, self.p.device(dx=1))
        self.send(own, Y_AT, self.p.device(dy=1))

    def along(self, dz):
        block = self.p.index(dz=dz)
        self.wait(block, Z_AT + dz)
        self.send(block, X_AT + dz, self.p.device(dx=1))
        self.send(block, Y_AT + dz, self.p.device(dy=1))

    def across(self, dz):
        if dz < 2:
            block = self.p.index(dz=dz, dx=1)
            self.wait(block, X_AT + dz)
            self.send(block, D_AT + dz, self.p.device(dy=1))
        else:
            block = self.p.index(dz=dz, dy=1)
            self.wait(block, Y_AT + dz)
            self.send(block, D_AT + dz, self.p.device(dx=1))

    def finish(self):
        for dz in range(4):
            if dz < 2:
                self.wait(self.p.index(dz=dz, dy=1), Y_AT + dz)
            else:
                self.wait(self.p.index(dz=dz, dx=1), X_AT + dz)
        for dz in range(4):
            self.wait(self.p.index(dz=dz, dy=1, dx=1), D_AT + dz)

    def drain(self):
        for copy in self.out:
            copy.wait_send()


class Scatter:
    def __init__(self, place, blocks, landed, sent, came):
        self.p, self.blocks, self.landed = place, blocks, landed
        self.sent, self.came = sent, came
        self.out = []

    def copy(self, block, slot, device):
        return pltpu.make_async_remote_copy(
            src_ref=self.blocks.at[block],
            dst_ref=self.landed.at[slot],
            send_sem=self.sent.at[slot],
            recv_sem=self.came.at[slot],
            device_id=device,
            device_id_type=MESH_ID,
        )

    def send(self, block, slot, device):
        copy = self.copy(block, slot, device)
        copy.start()
        self.out.append(copy)

    def wait(self, slot):
        self.copy(0, slot, self.p.device(dx=1)).wait_recv()

    def add(self, block, slots):
        rows = self.blocks.shape[1]
        step = 16

        def body(i, carry):
            at = pl.ds(pl.multiple_of(i * step, step), step)
            total = self.blocks[block, at, :].astype(jnp.float32)
            for slot in slots:
                total = total + self.landed[slot, at, :].astype(jnp.float32)
            self.blocks[block, at, :] = total.astype(self.blocks.dtype)
            return carry

        lax.fori_loop(0, rows // step, body, 0)

    def begin(self):
        for dz in (1, 2, 3, 0):
            diagonal = self.p.index(dz=dz, dy=1, dx=1)
            if dz < 2:
                self.send(diagonal, D_AT + dz, self.p.device(dy=1))
                self.send(self.p.index(dz=dz, dy=1), Y_AT + dz, self.p.device(dy=1))
            else:
                self.send(diagonal, D_AT + dz, self.p.device(dx=1))
                self.send(self.p.index(dz=dz, dx=1), X_AT + dz, self.p.device(dx=1))

    def across(self, dz):
        self.wait(D_AT + dz)
        if dz < 2:
            block = self.p.index(dz=dz, dx=1)
            self.add(block, (D_AT + dz,))
            self.send(block, X_AT + dz, self.p.device(dx=1))
        else:
            block = self.p.index(dz=dz, dy=1)
            self.add(block, (D_AT + dz,))
            self.send(block, Y_AT + dz, self.p.device(dy=1))

    def along(self, dz):
        self.wait(X_AT + dz)
        self.wait(Y_AT + dz)
        block = self.p.index(dz=dz)
        if dz:
            self.add(block, (X_AT + dz, Y_AT + dz))
            self.send(block, Z_AT + dz, self.p.device(dz=dz))

    def total(self, write):
        for dz in (1, 2, 3):
            self.wait(Z_AT + dz)
        own = self.p.index()
        rows = self.blocks.shape[1]
        step = 16

        def body(i, carry):
            at = pl.ds(pl.multiple_of(i * step, step), step)
            total = self.blocks[own, at, :].astype(jnp.float32)
            for slot in (X_AT, Y_AT, Z_AT + 1, Z_AT + 2, Z_AT + 3):
                total = total + self.landed[slot, at, :].astype(jnp.float32)
            write(at, total)
            return carry

        lax.fori_loop(0, rows // step, body, 0)

    def drain(self):
        for copy in self.out:
            copy.wait_send()


def gather_kernel(
    wqkv_ref, wout_ref, win_ref, wdown_ref, vec_ref, tok_ref, cot_ref,
    qkv_o, out_o, in_o, down_o, vec_o, tok_o, cot_o,
    w_qkv, w_nat, w_out, w_in, w_down, vec, tok, cot,
    sent, came, pair_sent, pair_came, local,
):
    p = Place()
    own = p.index()
    c = p.c
    mine = pl.ds(pl.multiple_of(ROWS * c, ROWS), ROWS)
    loads = [
        pltpu.make_async_copy(wqkv_ref.at[c], w_qkv.at[own, mine], local.at[0]),
        pltpu.make_async_copy(win_ref.at[c], w_in.at[own, mine], local.at[1]),
        pltpu.make_async_copy(wout_ref, w_nat.at[own], local.at[2]),
        pltpu.make_async_copy(wdown_ref, w_down.at[own], local.at[3]),
        pltpu.make_async_copy(vec_ref, vec.at[own], local.at[4]),
        pltpu.make_async_copy(tok_ref, tok.at[c], local.at[5]),
        pltpu.make_async_copy(cot_ref, cot.at[c], local.at[6]),
    ]
    for load in loads:
        load.start()
    p.greet()

    def to_partner(src, dst, slot):
        return pltpu.make_async_remote_copy(
            src_ref=src, dst_ref=dst, send_sem=pair_sent.at[slot], recv_sem=pair_came.at[slot],
            device_id=p.partner(), device_id_type=MESH_ID,
        )

    pair = [
        to_partner(wqkv_ref.at[1 - c], w_qkv.at[own, mine], 0),
        to_partner(win_ref.at[1 - c], w_in.at[own, mine], 1),
        to_partner(tok_ref, tok.at[c], 2),
        to_partner(cot_ref, cot.at[c], 3),
    ]
    for copy in pair:
        copy.start()
    g_qkv, g_out, g_in, g_down, g_vec = (
        Gather(p, blocks, sent.at[i], came.at[i])
        for i, blocks in enumerate((w_qkv, w_nat, w_in, w_down, vec))
    )
    loads[4].wait()
    g_vec.begin()
    loads[0].wait()
    pair[0].wait_recv()
    g_qkv.begin()
    loads[2].wait()
    g_out.begin()
    loads[1].wait()
    pair[1].wait_recv()
    g_in.begin()
    loads[3].wait()
    g_down.begin()
    for g in (g_vec, g_qkv, g_out, g_in, g_down):
        for dz in (1, 2, 3):
            g.along(dz)
        for dz in (0, 1, 2, 3):
            g.across(dz)
    for g in (g_vec, g_qkv, g_out):
        g.finish()
    half = to_partner(w_nat.at[pl.ds(8 * (1 - c), 8)], w_out.at[:, mine], 4)
    half.start()
    keep = pltpu.make_async_copy(w_nat.at[pl.ds(8 * c, 8)], w_out.at[:, mine], local.at[7])
    keep.start()
    for g in (g_in, g_down):
        g.finish()
    loads[5].wait()
    loads[6].wait()
    pair[2].wait_recv()
    pair[3].wait_recv()
    keep.wait()
    half.wait_recv()
    stores = [
        pltpu.make_async_copy(a, b, local.at[8 + i])
        for i, (a, b) in enumerate(
            ((w_qkv, qkv_o), (w_out, out_o), (w_in, in_o), (w_down, down_o), (vec, vec_o), (tok, tok_o), (cot, cot_o))
        )
    ]
    for store in stores:
        store.start()
    for g in (g_vec, g_qkv, g_out, g_in, g_down):
        g.drain()
    for copy in pair:
        copy.wait_send()
    half.wait_send()
    for store in stores:
        store.wait()


def gather_all(wqkv2, w_out, win2, w_down, tile, inputs, cotangent):
    bf, f32 = jnp.bfloat16, jnp.float32
    dq, do, di = wqkv2.shape[2], w_out.shape[1], win2.shape[2]
    shapes = [
        ((16, 64, dq), bf), ((8, 64, do), bf), ((16, 64, di), bf), ((16,) + w_down.shape, bf),
        ((16, 16, 128), f32), ((2,) + inputs.shape, bf), ((2,) + cotangent.shape, bf),
    ]
    scratch = list(shapes)
    scratch.insert(1, ((16, 32, do), bf))
    return pl.pallas_call(
        gather_kernel,
        out_shape=[jax.ShapeDtypeStruct(s, d) for s, d in shapes],
        in_specs=[pl.BlockSpec(memory_space=pl.ANY)] * 7,
        out_specs=[pl.BlockSpec(memory_space=pl.ANY)] * 7,
        scratch_shapes=[pltpu.VMEM(s, d) for s, d in scratch]
        + [
            pltpu.SemaphoreType.DMA((5, 15)),
            pltpu.SemaphoreType.DMA((5, 15)),
            pltpu.SemaphoreType.DMA((5,)),
            pltpu.SemaphoreType.DMA((5,)),
            pltpu.SemaphoreType.DMA((15,)),
        ],
        compiler_params=pltpu.CompilerParams(
            collective_id=0, has_side_effects=True, vmem_limit_bytes=60 * 1024 * 1024
        ),
        name="weights_gather",
    )(wqkv2, w_out, win2, w_down, tile, inputs, cotangent)


def scatter_kernel(
    qkv_ref, out_ref, in_ref, down_ref, vec_ref,
    qkv_o, out_o, in_o, down_o, vec_o,
    b_qkv, b_out, b_in, b_down, b_vec,
    l_qkv, l_out, l_in, l_down, l_vec,
    f_qkv, f_out, f_in, f_down, f_vec, n_vec,
    sent, came, pair_sent, pair_came, local,
):
    p = Place()
    c = p.c
    mine = pl.ds(pl.multiple_of(ROWS * c, ROWS), ROWS)
    theirs = pl.ds(pl.multiple_of(ROWS * (1 - c), ROWS), ROWS)
    loads = [
        pltpu.make_async_copy(a, b, local.at[i])
        for i, (a, b) in enumerate(
            ((down_ref, b_down), (in_ref, b_in), (out_ref.at[:, mine], b_out.at[pl.ds(8 * c, 8)]), (qkv_ref, b_qkv), (vec_ref, b_vec))
        )
    ]
    for load in loads:
        load.start()
    p.greet()

    def to_partner(src, dst, slot):
        return pltpu.make_async_remote_copy(
            src_ref=src, dst_ref=dst, send_sem=pair_sent.at[slot], recv_sem=pair_came.at[slot],
            device_id=p.partner(), device_id_type=MESH_ID,
        )

    half = to_partner(out_ref.at[:, theirs], b_out.at[pl.ds(8 * c, 8)], 0)
    half.start()
    s_down, s_in, s_out, s_qkv, s_vec = (
        Scatter(p, blocks, landed, sent.at[i], came.at[i])
        for i, (blocks, landed) in enumerate(
            ((b_down, l_down), (b_in, l_in), (b_out, l_out), (b_qkv, l_qkv), (b_vec, l_vec))
        )
    )
    for i, s in enumerate((s_down, s_in, s_out, s_qkv, s_vec)):
        loads[i].wait()
        if i == 2:
            half.wait_recv()
        s.begin()

    def put(ref):
        def write(at, value):
            ref[at, :] = value

        return write

    finals = {0: f_down, 1: f_in, 2: f_out, 3: f_qkv, 4: f_vec}
    every = (s_down, s_in, s_out, s_qkv, s_vec)
    for s in every:
        for dz in (1, 2, 3, 0):
            s.across(dz)
        for dz in (1, 2, 3, 0):
            s.along(dz)
    for i, s in enumerate(every):
        s.total(put(finals[i]))
    pair = [
        to_partner(f_qkv.at[theirs], qkv_o.at[c], 1),
        to_partner(f_in.at[theirs], in_o.at[c], 2),
        to_partner(f_vec, n_vec, 3),
    ]
    for copy in pair:
        copy.start()
    stores = [
        pltpu.make_async_copy(f_down, down_o, local.at[5]),
        pltpu.make_async_copy(f_out, out_o, local.at[6]),
        pltpu.make_async_copy(f_qkv.at[mine], qkv_o.at[c], local.at[7]),
        pltpu.make_async_copy(f_in.at[mine], in_o.at[c], local.at[8]),
        pltpu.make_async_copy(f_vec, vec_o.at[0], local.at[9]),
    ]
    for store in stores:
        store.start()
    pair[2].wait_recv()
    other = pltpu.make_async_copy(n_vec, vec_o.at[1], local.at[10])
    other.start()
    for s in every:
        s.drain()
    half.wait_send()
    pair[0].wait()
    pair[1].wait()
    pair[2].wait_send()
    for store in stores:
        store.wait()
    other.wait()


def scatter_all(g_qkv, g_out, g_in, g_down, g_vec):
    bf, f32 = jnp.bfloat16, jnp.float32
    dq, do, di, dd = g_qkv.shape[2], g_out.shape[2], g_in.shape[2], g_down.shape[2]
    down = g_down.shape[1]
    outs = [((2, 32, dq), f32), ((32, do), f32), ((2, 32, di), f32), ((down, dd), f32), ((2, 16, 128), f32)]
    blocks = [((64, dq), bf), ((32, do), bf), ((64, di), bf), ((down, dd), bf), ((16, 128), f32)]
    return pl.pallas_call(
        scatter_kernel,
        out_shape=[jax.ShapeDtypeStruct(s, d) for s, d in outs],
        in_specs=[pl.BlockSpec(memory_space=pl.ANY)] * 5,
        out_specs=[pl.BlockSpec(memory_space=pl.ANY)] * 5,
        scratch_shapes=[pltpu.VMEM((16,) + s, d) for s, d in blocks]
        + [pltpu.VMEM((15,) + s, d) for s, d in blocks]
        + [pltpu.VMEM(s, f32) for s, d in blocks]
        + [pltpu.VMEM((16, 128), f32)]
        + [
            pltpu.SemaphoreType.DMA((5, 15)),
            pltpu.SemaphoreType.DMA((5, 15)),
            pltpu.SemaphoreType.DMA((4,)),
            pltpu.SemaphoreType.DMA((4,)),
            pltpu.SemaphoreType.DMA((11,)),
        ],
        compiler_params=pltpu.CompilerParams(
            collective_id=1, has_side_effects=True, vmem_limit_bytes=60 * 1024 * 1024
        ),
        name="gradients_scatter",
    )(g_qkv, g_out, g_in, g_down, g_vec)


def swap(value):
    return lax.ppermute(value, "c", [(0, 1), (1, 0)])


def local_split(
    inputs, segment_ids, cotangent, ln1_gain, ln1_shift, w_qkv, query_bias, value_bias, w_out, out_bias,
    ln2_gain, ln2_shift, w_in, in_bias, w_down, down_bias,
):
    f32, bf = jnp.float32, jnp.bfloat16
    c = lax.axis_index("c")
    narrow = lax.axis_index("x") * 2 + c
    wide = lax.axis_index("z") * 2 + lax.axis_index("y")
    length, d_model = inputs.shape
    rows = ln1_gain.shape[0]
    small = jnp.stack(
        [ln1_gain, ln1_shift, query_bias, value_bias, out_bias, ln2_gain, ln2_shift, down_bias]
    ).astype(f32)
    quarter = jnp.arange(4)[None, :, None] == narrow
    tile = jnp.where(quarter, small[:, None, :], 0.0).reshape(8, 128)
    tile = jnp.concatenate([tile, in_bias.astype(f32)[None], jnp.zeros((7, 128), f32)])
    wqkv2 = w_qkv.reshape(rows, 3, 2, d_model // 2).transpose(2, 0, 1, 3).reshape(2, rows, -1)
    win2 = w_in.reshape(rows, 16, 2, 128).transpose(2, 0, 1, 3).reshape(2, rows, -1)
    qkv_f, out_f, in_f, down_f, vec_f, tok2, cot2 = gather_all(wqkv2, w_out, win2, w_down, tile, inputs, cotangent)
    mates = swap(vec_f)
    vecs = (vec_f + mates)[:, :8].reshape(8, 2, 8, 128).sum(1).transpose(1, 0, 2).reshape(8, d_model)
    g1, b1, qb, vb, ob, g2, b2, db = [vecs[i] for i in range(8)]
    inb = vec_f[:, 8].reshape(-1)
    qkv_m = qkv_f.reshape(d_model, -1)
    out_m = out_f.reshape(-1, d_model)
    in_m = in_f.reshape(d_model, -1)
    down_m = down_f.reshape(-1, d_model)
    half = d_model // 2
    cut = lambda v: lax.dynamic_slice(v, (c * half,), (half,))
    seg2 = jnp.where(c == 0, jnp.stack([segment_ids, swap(segment_ids)]), jnp.stack([swap(segment_ids), segment_ids]))
    tokens = tok2.astype(f32).reshape(2 * length, d_model)
    position = jnp.arange(length, dtype=jnp.int32)
    allowed = ((seg2[:, :, None] == seg2[:, None, :]) & (seg2[:, :, None] >= 0)) | (
        position[:, None] == position[None, :]
    )
    n1, x1, r1 = normalize(tokens, g1, b1)
    norm_one = n1.astype(bf)
    shifts = jnp.concatenate([cut(qb), jnp.zeros((half,), f32), cut(vb)])
    triple = (jnp.dot(norm_one, qkv_m, preferred_element_type=f32) + shifts).astype(bf)
    t5 = triple.reshape(2, length, 3, half // HD, HD)
    q, k, v = t5[:, :, 0], t5[:, :, 1], t5[:, :, 2]
    scores = jnp.einsum("sqhd,skhd->shqk", q, k, preferred_element_type=f32) * HD ** (-0.5)
    scores = jnp.where(allowed[:, None], scores, NEG_FILL)
    probs = jax.nn.softmax(scores, axis=-1)
    probs_low = probs.astype(bf)
    attended = jnp.einsum("shqk,skhd->sqhd", probs_low, v, preferred_element_type=f32)
    attended = attended.reshape(2 * length, half).astype(bf)
    part = jnp.dot(attended, out_m, preferred_element_type=f32)
    middle = tokens + part + swap(part) + ob
    n2, x2, r2 = normalize(middle, g2, b2)
    norm_two = n2.astype(bf)
    pre_act = jnp.dot(norm_two, in_m, preferred_element_type=f32) + inb
    hidden = gelu_value(pre_act).astype(bf)
    cot = cot2.reshape(2 * length, d_model)
    grad_down = jnp.einsum("sf,sd->fd", hidden, cot, preferred_element_type=f32).astype(bf)
    outp = jnp.dot(hidden, down_m, preferred_element_type=f32).reshape(2, length, d_model)
    pick = lambda a, i: lax.dynamic_index_in_dim(a, i, 0, False)
    layer_out = pick(middle.reshape(2, length, d_model), c) + pick(outp, c) + swap(pick(outp, 1 - c)) + db
    grad_hidden = jnp.einsum("sd,fd->sf", cot, down_m, preferred_element_type=f32)
    grad_pre = (grad_hidden * gelu_slope(pre_act)).astype(bf)
    grad_in = jnp.einsum("sd,sf->df", norm_two, grad_pre, preferred_element_type=f32).astype(bf)
    grad_in_bias = jnp.sum(grad_pre.astype(f32), 0)
    gn2 = jnp.einsum("sf,df->sd", grad_pre, in_m, preferred_element_type=f32)
    gn2 = gn2 + swap(gn2)
    gm = cot.astype(f32) + normalize_back(gn2, x2, r2, g2)
    grad_mixed = gm.astype(bf)
    grad_out = jnp.einsum("sd,se->de", attended, grad_mixed, preferred_element_type=f32).astype(bf)
    grad_att = jnp.einsum("se,de->sd", grad_mixed, out_m, preferred_element_type=f32).astype(bf)
    ga = grad_att.reshape(2, length, half // HD, HD)
    gp = jnp.einsum("sqhd,skhd->shqk", ga, v, preferred_element_type=f32)
    gs = (probs * (gp - jnp.sum(probs * gp, -1, keepdims=True))).astype(bf)
    gq = jnp.einsum("shqk,skhd->sqhd", gs, k, preferred_element_type=f32) * HD ** (-0.5)
    gk = jnp.einsum("shqk,sqhd->skhd", gs, q, preferred_element_type=f32) * HD ** (-0.5)
    gv = jnp.einsum("shqk,sqhd->skhd", probs_low, ga, preferred_element_type=f32)
    gt = jnp.stack([gq, gk, gv], 2).reshape(2 * length, 3 * half).astype(bf)
    grad_qkv = jnp.einsum("sd,st->dt", norm_one, gt, preferred_element_type=f32).astype(bf)
    gqb = jnp.sum(gt[:, :half].astype(f32), 0)
    gvb = jnp.sum(gt[:, 2 * half :].astype(f32), 0)
    gn1 = jnp.einsum("st,dt->sd", gt, qkv_m, preferred_element_type=f32).reshape(2, length, d_model)
    gn1 = pick(gn1, c) + swap(pick(gn1, 1 - c))
    own = lambda a: pick(a.reshape(2, length, d_model), c)
    r1o = pick(r1.reshape(2, length, 1), c)
    grad_input = own(gm) + normalize_back(gn1, own(x1), r1o, g1)
    put = lambda v: lax.dynamic_update_slice(jnp.zeros((d_model,), f32), v, (c * half,))
    sums = jnp.stack(
        [
            jnp.sum(gn1 * own(x1), 0), jnp.sum(gn1, 0), put(gqb), put(gvb), jnp.sum(own(grad_mixed).astype(f32), 0),
            jnp.sum(own(gn2 * x2), 0), jnp.sum(own(gn2), 0), jnp.sum(own(cot).astype(f32), 0),
        ]
    )
    gvec = jnp.repeat(sums.reshape(8, 8, 128).transpose(1, 0, 2), 2, 0)
    gvec = jnp.concatenate([gvec, grad_in_bias.reshape(16, 1, 128), jnp.zeros((16, 7, 128), f32)], 1)
    d_qkv, d_out, d_in, d_down, d_vec = scatter_all(
        grad_qkv.reshape(16, 64, -1), grad_out.reshape(8, 64, -1), grad_in.reshape(16, 64, -1),
        grad_down.reshape(16, 128, -1), gvec,
    )
    d_qkv = d_qkv.reshape(2, rows, 3, half).transpose(1, 2, 0, 3).reshape(rows, -1)
    d_in = d_in.reshape(2, rows, 16, 128).transpose(1, 2, 0, 3).reshape(rows, -1)
    eight = (d_vec[0, :8] + d_vec[1, :8]).reshape(8, 4, 32)
    eight = lax.dynamic_index_in_dim(eight, narrow, 1, False)
    return (
        layer_out, grad_input, eight[0], eight[1], d_qkv, eight[2], eight[3], d_out, eight[4],
        eight[5], eight[6], d_in, d_vec[0, 8], d_down, eight[7],
    )


def solution(mesh):
    sizes = tuple(mesh.shape.values())
    step, names = local, (("wide", "narrow"),)
    if sizes == (8, 4):
        mesh = Mesh(mesh.devices.reshape(4, 2, 2, 2), ("z", "y", "x", "c"))
        step, names = local_split, (("z", "y", "x", "c"),)
    line, plane = P(names[0]), P(names[0], None)
    return jax.shard_map(
        step,
        mesh=mesh,
        in_specs=(plane, line, plane, line, line, plane, line, line, plane, line, line, line, plane, line, plane, line),
        out_specs=(plane, plane, line, line, plane, line, line, plane, line, line, line, plane, line, plane, line),
        check_vma=False,
    )
```

```python
import functools

import jax
import jax.numpy as jnp
from jax import lax
from jax.experimental import pallas as pl
from jax.experimental.pallas import tpu as pltpu
from jax.sharding import Mesh
from jax.sharding import PartitionSpec as P

HD = 64


EPS = 1e-05
ROOT_HALF = 0.7071067811865476
INV_ROOT_TAU = 0.3989422804014327
NEG_FILL = -1000000000.0


def normalize(values, gain, shift):
    average = jnp.mean(values, -1, keepdims=True)
    centred = values - average
    inverse = lax.rsqrt(jnp.mean(centred * centred, -1, keepdims=True) + EPS)
    normed = centred * inverse
    return (normed * gain + shift, normed, inverse)


def normalize_back(grad_norm, normed, inverse, gain):
    scaled = grad_norm * gain
    return inverse * (
        scaled
        - jnp.mean(scaled, -1, keepdims=True)
        - normed * jnp.mean(scaled * normed, -1, keepdims=True)
    )


def gelu_value(pre_act):
    return 0.5 * pre_act * (1.0 + lax.erf(pre_act * ROOT_HALF))


def gelu_slope(pre_act):
    return (
        0.5 * (1.0 + lax.erf(pre_act * ROOT_HALF))
        + pre_act * jnp.exp(-0.5 * pre_act * pre_act) * INV_ROOT_TAU
    )


def gather_forward(shards):
    return (
        lax.all_gather(shards[0], ("wide", "narrow"), axis=0, tiled=True),
        lax.all_gather(shards[1], ("wide", "narrow"), axis=0, tiled=True),
        lax.all_gather(shards[2], ("wide", "narrow"), axis=0, tiled=True),
        lax.all_gather(shards[3], ("wide", "narrow"), axis=0, tiled=True),
        lax.all_gather(shards[4], ("wide", "narrow"), axis=0, tiled=True),
        lax.all_gather(shards[5], ("wide", "narrow"), axis=0, tiled=True),
        lax.all_gather(shards[6], ("wide", "narrow"), axis=0, tiled=True),
        lax.all_gather(shards[7], ("wide", "narrow"), axis=0, tiled=True),
        lax.all_gather(shards[8], ("wide", "narrow"), axis=0, tiled=True),
        lax.all_gather(shards[9], ("wide", "narrow"), axis=0, tiled=True),
        lax.all_gather(shards[10], ("wide", "narrow"), axis=0, tiled=True),
        lax.all_gather(shards[11], ("wide", "narrow"), axis=0, tiled=True),
        lax.all_gather(shards[12], ("wide", "narrow"), axis=0, tiled=True),
    )


def gather_backward(shards):
    return (
        lax.all_gather(shards[0], ("wide", "narrow"), axis=0, tiled=True),
        lax.all_gather(shards[1], ("wide", "narrow"), axis=0, tiled=True),
        lax.all_gather(shards[2], ("wide", "narrow"), axis=0, tiled=True),
        lax.all_gather(shards[3], ("wide", "narrow"), axis=0, tiled=True),
        lax.all_gather(shards[4], ("wide", "narrow"), axis=0, tiled=True),
        lax.all_gather(shards[5], ("wide", "narrow"), axis=0, tiled=True),
        lax.all_gather(shards[6], ("wide", "narrow"), axis=0, tiled=True),
        lax.all_gather(shards[7], ("wide", "narrow"), axis=0, tiled=True),
        lax.all_gather(shards[8], ("wide", "narrow"), axis=0, tiled=True),
        lax.all_gather(shards[9], ("wide", "narrow"), axis=0, tiled=True),
        lax.all_gather(shards[10], ("wide", "narrow"), axis=0, tiled=True),
        lax.all_gather(shards[11], ("wide", "narrow"), axis=0, tiled=True),
        lax.all_gather(shards[12], ("wide", "narrow"), axis=0, tiled=True),
    )


def reduce_grads(grads):
    return (
        lax.psum_scatter(grads[0], ("wide", "narrow"), scatter_dimension=0, tiled=True),
        lax.psum_scatter(grads[1], ("wide", "narrow"), scatter_dimension=0, tiled=True),
        lax.psum_scatter(grads[2], ("wide", "narrow"), scatter_dimension=0, tiled=True),
        lax.psum_scatter(grads[3], ("wide", "narrow"), scatter_dimension=0, tiled=True),
        lax.psum_scatter(grads[4], ("wide", "narrow"), scatter_dimension=0, tiled=True),
        lax.psum_scatter(grads[5], ("wide", "narrow"), scatter_dimension=0, tiled=True),
        lax.psum_scatter(grads[6], ("wide", "narrow"), scatter_dimension=0, tiled=True),
        lax.psum_scatter(grads[7], ("wide", "narrow"), scatter_dimension=0, tiled=True),
        lax.psum_scatter(grads[8], ("wide", "narrow"), scatter_dimension=0, tiled=True),
        lax.psum_scatter(grads[9], ("wide", "narrow"), scatter_dimension=0, tiled=True),
        lax.psum_scatter(grads[10], ("wide", "narrow"), scatter_dimension=0, tiled=True),
        lax.psum_scatter(grads[11], ("wide", "narrow"), scatter_dimension=0, tiled=True),
        lax.psum_scatter(grads[12], ("wide", "narrow"), scatter_dimension=0, tiled=True),
    )


def head_block(triple_b, offset, group_width, d_model):
    length = triple_b.shape[0]
    queries = triple_b[:, offset : offset + group_width].reshape(length, group_width // HD, HD)
    key_rows = triple_b[:, d_model + offset : d_model + offset + group_width].reshape(
        length, group_width // HD, HD
    )
    values = triple_b[:, 2 * d_model + offset : 2 * d_model + offset + group_width].reshape(
        length, group_width // HD, HD
    )
    return (queries, key_rows, values)


def block_scores(queries, key_rows, allowed):
    scores = jnp.einsum(
        "qhd,khd->hqk", queries, key_rows, preferred_element_type=jnp.float32
    ) * HD ** (-0.5)
    return jnp.where(allowed[None], scores, NEG_FILL)


def attend(triple_b, allowed, d_model):
    length = triple_b.shape[0]
    group_width = 4 * HD
    pieces = []
    log_totals = []
    for offset in range(0, d_model, group_width):
        queries, key_rows, values = head_block(triple_b, offset, group_width, d_model)
        scores = block_scores(queries, key_rows, allowed)
        highest = jnp.max(scores, -1, keepdims=True)
        exponent = jnp.exp(scores - highest)
        row_total = jnp.sum(exponent, -1, keepdims=True)
        probs_low = (exponent / row_total).astype(jnp.bfloat16)
        mixed = jnp.einsum("hqk,khd->qhd", probs_low, values, preferred_element_type=jnp.float32)
        pieces.append(mixed.reshape(length, group_width))
        log_totals.append(highest + jnp.log(row_total))
    return (jnp.concatenate(pieces, 1), log_totals)


def attend_back(triple_b, grad_att_b, allowed, log_totals, d_model):
    length = triple_b.shape[0]
    group_width = 4 * HD
    query_parts = []
    key_parts = []
    value_parts = []
    for index, offset in enumerate(range(0, d_model, group_width)):
        queries, key_rows, values = head_block(triple_b, offset, group_width, d_model)
        scores = block_scores(queries, key_rows, allowed)
        attn_probs = jnp.exp(scores - log_totals[index])
        probs_low = attn_probs.astype(jnp.bfloat16)
        grad_heads = grad_att_b[:, offset : offset + group_width].reshape(
            length, group_width // HD, HD
        )
        grad_probs = jnp.einsum(
            "qhd,khd->hqk", grad_heads, values, preferred_element_type=jnp.float32
        )
        inner_sum = jnp.sum(attn_probs * grad_probs, -1, keepdims=True)
        grad_scores = (attn_probs * (grad_probs - inner_sum)).astype(jnp.bfloat16)
        grad_query = jnp.einsum(
            "hqk,khd->qhd", grad_scores, key_rows, preferred_element_type=jnp.float32
        ) * HD ** (-0.5)
        grad_key = jnp.einsum(
            "hqk,qhd->khd", grad_scores, queries, preferred_element_type=jnp.float32
        ) * HD ** (-0.5)
        grad_value = jnp.einsum(
            "hqk,qhd->khd", probs_low, grad_heads, preferred_element_type=jnp.float32
        )
        query_parts.append(grad_query.reshape(length, group_width))
        key_parts.append(grad_key.reshape(length, group_width))
        value_parts.append(grad_value.reshape(length, group_width))
    return jnp.concatenate(query_parts + key_parts + value_parts, 1).astype(jnp.bfloat16)


def local(
    inputs,
    segment_ids,
    cotangent,
    ln1_gain,
    ln1_shift,
    w_qkv,
    query_bias,
    value_bias,
    w_out,
    out_bias,
    ln2_gain,
    ln2_shift,
    w_in,
    in_bias,
    w_down,
    down_bias,
):
    shards = (
        ln1_gain,
        ln1_shift,
        w_qkv,
        query_bias,
        value_bias,
        w_out,
        out_bias,
        ln2_gain,
        ln2_shift,
        w_in,
        in_bias,
        w_down,
        down_bias,
    )
    fwd_weights = gather_forward(shards)
    (
        gain_one,
        shift_one,
        qkv_full,
        qbias_full,
        vbias_full,
        outw_full,
        outb_full,
        gain_two,
        shift_two,
        inw_full,
        inb_full,
        downw_full,
        downb_full,
    ) = fwd_weights
    d_model = inputs.shape[1]
    length = inputs.shape[0]
    tokens = inputs.astype(jnp.float32)
    position = jnp.arange(length, dtype=jnp.int32)
    allowed = (segment_ids[:, None] == segment_ids[None, :]) & (segment_ids[:, None] >= 0) | (
        position[:, None] == position[None, :]
    )
    normed_out, normed_one, inverse_one = normalize(
        tokens, gain_one.astype(jnp.float32), shift_one.astype(jnp.float32)
    )
    norm_one = normed_out.astype(jnp.bfloat16)
    shifts = jnp.concatenate(
        [
            qbias_full.astype(jnp.float32),
            jnp.zeros((d_model,), jnp.float32),
            vbias_full.astype(jnp.float32),
        ]
    )
    triple_b = (jnp.dot(norm_one, qkv_full, preferred_element_type=jnp.float32) + shifts).astype(
        jnp.bfloat16
    )
    attended_f, log_totals = attend(triple_b, allowed, d_model)
    attended = attended_f.astype(jnp.bfloat16)
    middle = (
        tokens
        + jnp.dot(attended, outw_full, preferred_element_type=jnp.float32)
        + outb_full.astype(jnp.float32)
    )
    normed_out_two, normed_two, inverse_two = normalize(
        middle, gain_two.astype(jnp.float32), shift_two.astype(jnp.float32)
    )
    norm_two = normed_out_two.astype(jnp.bfloat16)
    pre_act = jnp.dot(norm_two, inw_full, preferred_element_type=jnp.float32) + inb_full.astype(
        jnp.float32
    )
    hidden = gelu_value(pre_act).astype(jnp.bfloat16)
    layer_out = (
        middle
        + jnp.dot(hidden, downw_full, preferred_element_type=jnp.float32)
        + downb_full.astype(jnp.float32)
    )
    back_weights = gather_backward(shards)
    (
        gain_one_b,
        shift_one_b,
        qkv_back,
        qbias_back,
        vbias_back,
        outw_back,
        outb_back,
        gain_two_b,
        shift_two_b,
        inw_back,
        inb_back,
        downw_back,
        downb_back,
    ) = back_weights
    grad_top = cotangent.astype(jnp.float32)
    grad_w_down = jnp.einsum("sf,sd->fd", hidden, cotangent, preferred_element_type=jnp.float32)
    grad_down_bias = jnp.sum(grad_top, 0)
    grad_hidden = jnp.einsum("sd,fd->sf", cotangent, downw_back, preferred_element_type=jnp.float32)
    grad_pre = (grad_hidden * gelu_slope(pre_act)).astype(jnp.bfloat16)
    grad_w_in = jnp.einsum("sd,sf->df", norm_two, grad_pre, preferred_element_type=jnp.float32)
    grad_in_bias = jnp.sum(grad_pre.astype(jnp.float32), 0)
    grad_norm_two = jnp.einsum("sf,df->sd", grad_pre, inw_back, preferred_element_type=jnp.float32)
    grad_ln2_gain = jnp.sum(grad_norm_two * normed_two, 0)
    grad_ln2_shift = jnp.sum(grad_norm_two, 0)
    grad_middle = grad_top + normalize_back(
        grad_norm_two, normed_two, inverse_two, gain_two_b.astype(jnp.float32)
    )
    grad_mixed = grad_middle.astype(jnp.bfloat16)
    grad_w_out = jnp.einsum("sd,se->de", attended, grad_mixed, preferred_element_type=jnp.float32)
    grad_out_bias = jnp.sum(grad_mixed.astype(jnp.float32), 0)
    grad_attended = jnp.einsum(
        "se,de->sd", grad_mixed, outw_back, preferred_element_type=jnp.float32
    ).astype(jnp.bfloat16)
    grad_triple = attend_back(triple_b, grad_attended, allowed, log_totals, d_model)
    grad_w_qkv = jnp.einsum("sd,st->dt", norm_one, grad_triple, preferred_element_type=jnp.float32)
    grad_query_bias = jnp.sum(grad_triple[:, :d_model].astype(jnp.float32), 0)
    grad_value_bias = jnp.sum(grad_triple[:, 2 * d_model :].astype(jnp.float32), 0)
    grad_norm_one = jnp.einsum(
        "st,dt->sd", grad_triple, qkv_back, preferred_element_type=jnp.float32
    )
    grad_ln1_gain = jnp.sum(grad_norm_one * normed_one, 0)
    grad_ln1_shift = jnp.sum(grad_norm_one, 0)
    grad_input = grad_middle + normalize_back(
        grad_norm_one, normed_one, inverse_one, gain_one_b.astype(jnp.float32)
    )
    owned = reduce_grads(
        (
            grad_ln1_gain,
            grad_ln1_shift,
            grad_w_qkv,
            grad_query_bias,
            grad_value_bias,
            grad_w_out,
            grad_out_bias,
            grad_ln2_gain,
            grad_ln2_shift,
            grad_w_in,
            grad_in_bias,
            grad_w_down,
            grad_down_bias,
        )
    )
    return (
        layer_out,
        grad_input,
        owned[0],
        owned[1],
        owned[2],
        owned[3],
        owned[4],
        owned[5],
        owned[6],
        owned[7],
        owned[8],
        owned[9],
        owned[10],
        owned[11],
        owned[12],
    )


MESH_ID = pl.DeviceIdType.MESH
ROWS = 32
BF, F32 = jnp.bfloat16, jnp.float32


class Place:
    def __init__(self):
        self.z = lax.axis_index("z")
        self.y = lax.axis_index("y")
        self.x = lax.axis_index("x")
        self.c = lax.axis_index("c")

    def chip(self, dz=0, dy=0, dx=0):
        z = self.z
        if dz == 2:
            z = lax.rem(z + 2, 4)
        elif dz == 1:
            z = z + 1 - 2 * lax.rem(z, 2)
        elif dz == 3:
            z = 3 - z
        y = 1 - self.y if dy else self.y
        x = 1 - self.x if dx else self.x
        return z, y, x

    def index(self, dz=0, dy=0, dx=0):
        z, y, x = self.chip(dz, dy, dx)
        return (z * 2 + y) * 2 + x

    def device(self, dz=0, dy=0, dx=0):
        z, y, x = self.chip(dz, dy, dx)
        return {"z": z, "y": y, "x": x, "c": self.c}

    def partner(self):
        return {"z": self.z, "y": self.y, "x": self.x, "c": 1 - self.c}

    def greet(self):
        barrier = pltpu.get_barrier_semaphore()
        peers = [self.device(dz=1), self.device(dz=2), self.device(dz=3)]
        peers += [self.device(dy=1), self.device(dx=1), self.partner()]
        for peer in peers:
            pl.semaphore_signal(barrier, inc=1, device_id=peer, device_id_type=MESH_ID)
        pl.semaphore_wait(barrier, len(peers))


class Pair:
    def __init__(self, place, sent, came):
        self.p, self.sent, self.came = place, sent, came

    def copy(self, src, dst, slot):
        return pltpu.make_async_remote_copy(
            src_ref=src,
            dst_ref=dst,
            send_sem=self.sent.at[slot],
            recv_sem=self.came.at[slot],
            device_id=self.p.partner(),
            device_id_type=MESH_ID,
        )


Z_AT, X_AT, Y_AT, D_AT = -1, 3, 7, 11


class Gather:
    def __init__(self, place, blocks, sent, came):
        self.p, self.blocks, self.sent, self.came = place, blocks, sent, came
        self.left = []

    def copy(self, block, slot, to):
        at = self.p.index(**block)
        return pltpu.make_async_remote_copy(
            src_ref=self.blocks.at[at],
            dst_ref=self.blocks.at[at],
            send_sem=self.sent.at[slot],
            recv_sem=self.came.at[slot],
            device_id=self.p.device(**to),
            device_id_type=MESH_ID,
        )

    def send(self, block, slot, to):
        self.copy(block, slot, to).start()
        self.left.append((block, slot, to))

    def wait(self, block, slot):
        self.copy(block, slot, dict(dx=1)).wait_recv()

    def begin(self):
        for dz in (3, 2, 1):
            self.send({}, Z_AT + dz, dict(dz=dz))
        self.send({}, X_AT, dict(dx=1))
        self.send({}, Y_AT, dict(dy=1))

    def along(self, dz):
        self.wait(dict(dz=dz), Z_AT + dz)
        self.send(dict(dz=dz), X_AT + dz, dict(dx=1))
        self.send(dict(dz=dz), Y_AT + dz, dict(dy=1))

    def across(self, dz):
        if dz < 2:
            self.wait(dict(dz=dz, dx=1), X_AT + dz)
            self.send(dict(dz=dz, dx=1), D_AT + dz, dict(dy=1))
        else:
            self.wait(dict(dz=dz, dy=1), Y_AT + dz)
            self.send(dict(dz=dz, dy=1), D_AT + dz, dict(dx=1))

    def finish(self):
        for dz in range(4):
            if dz < 2:
                self.wait(dict(dz=dz, dy=1), Y_AT + dz)
            else:
                self.wait(dict(dz=dz, dx=1), X_AT + dz)
        for dz in range(4):
            self.wait(dict(dz=dz, dy=1, dx=1), D_AT + dz)

    def steps(self):
        for dz in (1, 2, 3):
            yield functools.partial(self.along, dz)
        for dz in (0, 1, 2, 3):
            yield functools.partial(self.across, dz)

    def drain(self):
        for block, slot, to in self.left:
            self.copy(block, slot, to).wait_send()


class Scatter:
    def __init__(self, place, blocks, landed, sent, came):
        self.p, self.blocks, self.landed = place, blocks, landed
        self.sent, self.came = sent, came
        self.left = []

    def copy(self, block, slot, to):
        return pltpu.make_async_remote_copy(
            src_ref=self.blocks.at[self.p.index(**block)],
            dst_ref=self.landed.at[slot],
            send_sem=self.sent.at[slot],
            recv_sem=self.came.at[slot],
            device_id=self.p.device(**to),
            device_id_type=MESH_ID,
        )

    def send(self, block, slot, to):
        self.copy(block, slot, to).start()
        self.left.append((block, slot, to))

    def wait(self, slot):
        self.copy({}, slot, dict(dx=1)).wait_recv()

    def add(self, at, slots, write):
        rows = self.blocks.shape[1]
        step = 16

        def body(i, carry):
            some = pl.ds(pl.multiple_of(i * step, step), step)
            total = self.blocks[at, some, :].astype(F32)
            for slot in slots:
                total = total + self.landed[slot, some, :].astype(F32)
            write(some, total)
            return carry

        lax.fori_loop(0, rows // step, body, 0)

    def merge(self, block, slots):
        at = self.p.index(**block)

        def write(some, total):
            self.blocks[at, some, :] = total.astype(self.blocks.dtype)

        self.add(at, slots, write)

    def begin(self):
        for dz in (1, 2, 3, 0):
            if dz < 2:
                self.send(dict(dz=dz, dy=1, dx=1), D_AT + dz, dict(dy=1))
                self.send(dict(dz=dz, dy=1), Y_AT + dz, dict(dy=1))
            else:
                self.send(dict(dz=dz, dy=1, dx=1), D_AT + dz, dict(dx=1))
                self.send(dict(dz=dz, dx=1), X_AT + dz, dict(dx=1))

    def across(self, dz):
        self.wait(D_AT + dz)
        if dz < 2:
            self.merge(dict(dz=dz, dx=1), (D_AT + dz,))
            self.send(dict(dz=dz, dx=1), X_AT + dz, dict(dx=1))
        else:
            self.merge(dict(dz=dz, dy=1), (D_AT + dz,))
            self.send(dict(dz=dz, dy=1), Y_AT + dz, dict(dy=1))

    def along(self, dz):
        self.wait(X_AT + dz)
        self.wait(Y_AT + dz)
        if dz:
            self.merge(dict(dz=dz), (X_AT + dz, Y_AT + dz))
            self.send(dict(dz=dz), Z_AT + dz, dict(dz=dz))

    def total(self, write):
        for dz in (1, 2, 3):
            self.wait(Z_AT + dz)
        self.add(self.p.index(), (X_AT, Y_AT, Z_AT + 1, Z_AT + 2, Z_AT + 3), write)

    def steps(self):
        for dz in (1, 2, 3, 0):
            yield functools.partial(self.across, dz)
        for dz in (1, 2, 3, 0):
            yield functools.partial(self.along, dz)

    def drain(self):
        for block, slot, to in self.left:
            self.copy(block, slot, to).wait_send()


class Pump:
    def __init__(self):
        self.queue = []

    def add(self, steps):
        self.queue.extend(steps)

    def take(self, count):
        now, self.queue = self.queue[:count], self.queue[count:]
        for step in now:
            step()

    def loop(self, trips, body, per_trip=0):
        groups = []
        for i in range(trips):
            groups.append(self.queue[:per_trip])
            self.queue = self.queue[per_trip:]

        def trip(i, carry):
            body(i)
            for k, group in enumerate(groups):
                if group:

                    @pl.when(i == k)
                    def _(group=group):
                        for step in group:
                            step()

            return carry

        lax.fori_loop(0, trips, trip, 0)


NN = (((1,), (0,)), ((), ()))
NT = (((1,), (1,)), ((), ()))
TN = (((0,), (0,)), ((), ()))


def mm(a, b, dims=NN):
    return lax.dot_general(a, b, dims, preferred_element_type=F32)


def span(i, size):
    return pl.ds(pl.multiple_of(i * size, size), size)


def stats(v):
    average = jnp.mean(v, -1, keepdims=True)
    centred = v - average
    inverse = lax.rsqrt(jnp.mean(centred * centred, -1, keepdims=True) + EPS)
    return centred * inverse, inverse


def build_mask(mask, seg_col, seg_row):
    size = mask.shape[1]
    for s in range(2):

        def body(i, carry, s=s):
            rows = span(i, 128)
            col = seg_col[s, rows, :][:, :1]
            row = seg_row[s, :1, :]
            here = lax.broadcasted_iota(jnp.int32, (128, size), 0) + i * 128
            there = lax.broadcasted_iota(jnp.int32, (128, size), 1)
            fine = ((col == row) & (col >= 0)) | (here == there)
            mask[s, rows, :] = jnp.where(fine, 0.0, NEG_FILL)
            return carry

        lax.fori_loop(0, size // 128, body, 0)


def build_vectors(vecs, hidden_shift, triple_shift, tiles, c):
    for w in range(8):
        vecs[0:8, 128 * w : 128 * (w + 1)] = tiles[2 * w, 0:8, :] + tiles[2 * w + 1, 0:8, :]
    for j in range(16):
        hidden_shift[0:1, 128 * j : 128 * (j + 1)] = tiles[j, 8:9, :]
    half = vecs.shape[1] // 2
    first = c == 0
    triple_shift[0:1, 0:half] = jnp.where(first, vecs[2:3, 0:half], vecs[2:3, half:])
    triple_shift[0:1, half : 2 * half] = jnp.zeros((1, half), F32)
    triple_shift[0:1, 2 * half :] = jnp.where(first, vecs[3:4, 0:half], vecs[3:4, half:])


G1, B1, QB, VB, OB, G2, B2, DB = range(8)


def attend_pair(i, triple, mask, attended, lse):
    length = mask.shape[1]
    half = attended.shape[1]
    pairs = half // 128
    s, pair = i // pairs, lax.rem(i, pairs)
    rows = span(s, length)
    q = triple[rows, pl.ds(pl.multiple_of(pair * 128, 128), 128)]
    k = triple[rows, pl.ds(pl.multiple_of(half + pair * 128, 128), 128)]
    v = triple[rows, pl.ds(pl.multiple_of(2 * half + pair * 128, 128), 128)]
    lane = lax.broadcasted_iota(jnp.int32, (length, 128), 1)
    low = lane < HD
    outs = []
    kept = lse[s]
    for h in range(2):
        mine = low if h == 0 else ~low
        scores = mm(jnp.where(mine, q, jnp.zeros_like(q)), k, NT) * HD ** (-0.5) + mask[s]
        highest = jnp.max(scores, -1, keepdims=True)
        exponent = jnp.exp(scores - highest)
        total = jnp.sum(exponent, -1, keepdims=True)
        probs = (exponent * (1.0 / total)).astype(BF)
        outs.append(mm(probs, v))
        kept = jnp.where(lane == pair * 2 + h, highest + jnp.log(total), kept)
    lse[s] = kept
    attended[rows, pl.ds(pl.multiple_of(pair * 128, 128), 128)] = jnp.where(low, outs[0], outs[1]).astype(BF)


def forward_kernel(
    wqkv_ref, wout_ref, win_ref, wdown_ref, tile_ref, tok_ref, cot_ref, col_ref, row_ref,
    qkv_o, out_o, in_o, down_o, vecs_o, norm1_o, triple_o, att_o, lse_o, xhat_o, inv_o, norm2_o, slope_o, cot_o,
    mask_o, gdown_o, layer_o,
    w_qkv, w_nat, w_out, w_in, w_down, tiles, tile, tile_in, tok, cot, col, row, mask,
    vecs, hshift, tshift, norm1, triple, att, lse, mid, part, part_in, last_in, norm2, xhat, inv, hidden, slope, gdown,
    sent, came, pair_sent, pair_came, local,
):
    p = Place()
    own, c = p.index(), p.c
    length = tok.shape[1]
    mine = pl.ds(pl.multiple_of(ROWS * c, ROWS), ROWS)
    slots = iter(range(local.shape[0]))

    def load(src, dst):
        copy = pltpu.make_async_copy(src, dst, local.at[next(slots)])
        copy.start()
        return copy

    loads = [
        load(wqkv_ref.at[c], w_qkv.at[own, mine]),
        load(wout_ref, w_nat.at[own]),
        load(win_ref.at[c], w_in.at[own, mine]),
        load(wdown_ref, w_down.at[own]),
        load(tile_ref, tile),
        load(tok_ref, tok.at[c]),
        load(cot_ref, cot.at[c]),
        load(col_ref, col.at[c]),
        load(row_ref, row.at[c]),
    ]
    p.greet()
    pair = Pair(p, pair_sent, pair_came)
    swaps = [
        pair.copy(tile_ref, tile_in, 0),
        pair.copy(wqkv_ref.at[1 - c], w_qkv.at[own, mine], 1),
        pair.copy(win_ref.at[1 - c], w_in.at[own, mine], 2),
        pair.copy(row_ref, row.at[c], 3),
        pair.copy(col_ref, col.at[c], 4),
        pair.copy(tok_ref, tok.at[c], 5),
        pair.copy(cot_ref, cot.at[c], 6),
    ]
    for copy in swaps:
        copy.start()
    g_qkv, g_out, g_in, g_down, g_vec = (
        Gather(p, blocks, sent.at[i], came.at[i])
        for i, blocks in enumerate((w_qkv, w_nat, w_in, w_down, tiles))
    )
    loads[0].wait()
    swaps[1].wait_recv()
    g_qkv.begin()
    loads[4].wait()
    swaps[0].wait_recv()
    tiles[own, 0:8, :] = tile[0:8, :] + tile_in[0:8, :]
    tiles[own, 8:16, :] = tile[8:16, :]
    g_vec.begin()
    loads[1].wait()
    g_out.begin()
    loads[2].wait()
    swaps[2].wait_recv()
    g_in.begin()
    loads[3].wait()
    g_down.begin()
    pump = Pump()
    for g in (g_vec, g_qkv, g_out, g_in, g_down):
        pump.add(g.steps())
    for i in (7, 8, 5):
        loads[i].wait()
    for i in (3, 4, 5):
        swaps[i].wait_recv()
    build_mask(mask, col, row)
    pump.take(7)
    g_vec.finish()
    build_vectors(vecs, hshift, tshift, tiles, c)
    tokens = tok.shape[0] * length

    def first_norm(i):
        rows = span(i, 128)
        v = tok[i // 4, span(lax.rem(i, 4), 128), :].astype(F32)
        normed, _ = stats(v)
        norm1[rows, :] = (normed * vecs[G1 : G1 + 1, :] + vecs[B1 : B1 + 1, :]).astype(BF)

    pump.loop(tokens // 128, first_norm, 0)
    pump.take(7)
    g_qkv.finish()
    stores = [load(w_qkv, qkv_o), load(norm1, norm1_o), load(vecs, vecs_o), load(mask, mask_o)]
    depth = norm1.shape[1]

    def project(i):
        cols = span(i, 256)
        w = w_qkv[:, :, cols].reshape(depth, 256)
        triple[:, cols] = (mm(norm1[...], w) + tshift[0:1, cols]).astype(BF)

    pump.loop(triple.shape[1] // 256, project, 1)
    stores.append(load(triple, triple_o))
    lse[...] = jnp.zeros_like(lse)
    pump.loop(8, functools.partial(attend_pair, triple=triple, mask=mask, attended=att, lse=lse), 1)
    stores += [load(att, att_o), load(lse, lse_o)]
    g_out.finish()
    half = pair.copy(w_nat.at[pl.ds(8 * (1 - c), 8)], w_out.at[:, mine], 7)
    half.start()
    keep = load(w_nat.at[pl.ds(8 * c, 8)], w_out.at[:, mine])
    keep.wait()
    half.wait_recv()
    stores.append(load(w_out, out_o))

    def send_part(i):
        rows = span(i, 256)
        return pair.copy(part.at[rows], part_in.at[rows], 8 + i)

    def mix(i):
        rows = span(i, 256)
        own_part = mm(att[rows, :], w_out[...].reshape(att.shape[1], depth))
        part[rows, :] = own_part.astype(BF)
        send_part(i).start()
        v = tok[i // 2, span(lax.rem(i, 2), 256), :].astype(F32)
        mid[rows, :] = v + own_part + vecs[OB : OB + 1, :]

    pump.loop(4, mix, 0)

    def second_norm(i):
        send_part(i).wait_recv()
        rows = span(i, 256)
        v = mid[rows, :] + part_in[rows, :].astype(F32)
        mid[rows, :] = v
        normed, inverse = stats(v)
        xhat[rows, :] = normed.astype(BF)
        inv[rows, :] = jnp.broadcast_to(inverse, (256, 128))
        norm2[rows, :] = (normed * vecs[G2 : G2 + 1, :] + vecs[B2 : B2 + 1, :]).astype(BF)

    pump.loop(4, second_norm, 0)
    stores += [load(xhat, xhat_o), load(inv, inv_o), load(norm2, norm2_o)]
    pump.take(max(len(pump.queue) - 7, 0))
    g_in.finish()
    stores.append(load(w_in, in_o))

    def expand(i):
        cols = span(i, 256)
        w = w_in[:, :, cols].reshape(depth, 256)
        pre = mm(norm2[...], w) + hshift[0:1, cols]
        bell = 0.5 * (1.0 + lax.erf(pre * ROOT_HALF))
        hidden[:, cols] = (pre * bell).astype(BF)
        slope[:, cols] = (bell + pre * jnp.exp(-0.5 * pre * pre) * INV_ROOT_TAU).astype(BF)

    loads[6].wait()
    swaps[6].wait_recv()
    stores.append(load(cot, cot_o))
    pump.loop(hidden.shape[1] // 256, expand, 1)
    stores.append(load(slope, slope_o))

    def down_grad(i):
        cols = span(i, 256)
        grad = mm(hidden[:, cols], cot[...].reshape(tokens, depth), TN).astype(BF)
        gdown[pl.ds(pl.multiple_of(2 * i, 2), 2)] = grad.reshape(2, 128, depth)

    pump.loop(hidden.shape[1] // 256, down_grad, 1)
    stores.append(load(gdown, gdown_o))
    pump.take(len(pump.queue))
    g_down.finish()
    stores.append(load(w_down, down_o))
    for i in range(4):
        send_part(i).wait_send()
    yours, ours = span(1 - c, length), span(c, length)
    units = hidden.shape[1]

    def theirs(i):
        cols = span(i, 256)
        w = w_down[:, :, cols].reshape(units, 256)
        part[yours, cols] = mm(hidden[yours, :], w).astype(BF)

    lax.fori_loop(0, depth // 256, lambda i, carry: (theirs(i), carry)[1], 0)
    last = pair.copy(part.at[yours], last_in, 12)
    last.start()

    def contract(i):
        cols = span(i, 256)
        w = w_down[:, :, cols].reshape(units, 256)
        mid[ours, cols] = mid[ours, cols] + mm(hidden[ours, :], w) + vecs[DB : DB + 1, cols]

    lax.fori_loop(0, depth // 256, lambda i, carry: (contract(i), carry)[1], 0)
    last.wait_recv()
    mid[ours, :] = mid[ours, :] + last_in[...].astype(F32)
    stores.append(load(mid.at[ours], layer_o))
    for g in (g_vec, g_qkv, g_out, g_in, g_down):
        g.drain()
    for copy in swaps:
        copy.wait_send()
    half.wait_send()
    last.wait_send()
    for store in stores:
        store.wait()


def forward_all(wqkv2, w_out, win2, w_down, tile, inputs, cotangent, col, row):
    dq, do, di = wqkv2.shape[2], w_out.shape[1], win2.shape[2]
    length, depth = inputs.shape
    tokens = 2 * length
    outs = [
        ((16, 64, dq), BF), ((8, 64, do), BF), ((16, 64, di), BF), ((16,) + w_down.shape, BF),
        ((8, depth), F32), ((tokens, depth), BF), ((tokens, dq), BF), ((tokens, dq // 3), BF), ((2, length, 128), F32),
        ((tokens, depth), BF), ((tokens, 128), F32), ((tokens, depth), BF), ((tokens, di), BF), ((2, length, depth), BF),
        ((2, length, length), F32), ((16,) + w_down.shape, BF), ((length, depth), F32),
    ]
    scratch = [
        ((16, 64, dq), BF), ((16, 32, do), BF), ((8, 64, do), BF), ((16, 64, di), BF), ((16,) + w_down.shape, BF),
        ((16, 16, 128), F32), ((16, 128), F32), ((16, 128), F32), ((2, length, depth), BF), ((2, length, depth), BF),
        ((2, length, 128), jnp.int32), ((2, 8, length), jnp.int32), ((2, length, length), F32),
        ((8, depth), F32), ((8, di), F32), ((8, dq), F32), ((tokens, depth), BF), ((tokens, dq), BF),
        ((tokens, dq // 3), BF), ((2, length, 128), F32), ((tokens, depth), F32), ((tokens, depth), BF),
        ((tokens, depth), BF), ((length, depth), BF), ((tokens, depth), BF), ((tokens, depth), BF), ((tokens, 128), F32),
        ((tokens, di), BF), ((tokens, di), BF), ((16,) + w_down.shape, BF),
    ]
    return pl.pallas_call(
        forward_kernel,
        out_shape=[jax.ShapeDtypeStruct(s, d) for s, d in outs],
        in_specs=[pl.BlockSpec(memory_space=pl.ANY)] * 9,
        out_specs=[pl.BlockSpec(memory_space=pl.ANY)] * len(outs),
        scratch_shapes=[pltpu.VMEM(s, d) for s, d in scratch]
        + [
            pltpu.SemaphoreType.DMA((5, 15)),
            pltpu.SemaphoreType.DMA((5, 15)),
            pltpu.SemaphoreType.DMA((13,)),
            pltpu.SemaphoreType.DMA((13,)),
            pltpu.SemaphoreType.DMA((32,)),
        ],
        compiler_params=pltpu.CompilerParams(
            collective_id=0, has_side_effects=True, vmem_limit_bytes=67043328
        ),
        name="forward_gather",
    )(wqkv2, w_out, win2, w_down, tile, inputs, cotangent, col, row)


def scatter_kernel(
    qkv_ref, out_ref, in_ref, down_ref, vec_ref,
    qkv_o, out_o, in_o, down_o, vec_o,
    b_qkv, b_out, b_in, b_down, b_vec,
    l_qkv, l_out, l_in, l_down, l_vec,
    f_qkv, f_out, f_in, f_down, f_vec, n_vec,
    sent, came, pair_sent, pair_came, local,
):
    p = Place()
    c = p.c
    mine = pl.ds(pl.multiple_of(ROWS * c, ROWS), ROWS)
    theirs = pl.ds(pl.multiple_of(ROWS * (1 - c), ROWS), ROWS)
    loads = [
        pltpu.make_async_copy(a, b, local.at[i])
        for i, (a, b) in enumerate(
            ((down_ref, b_down), (in_ref, b_in), (out_ref.at[:, mine], b_out.at[pl.ds(8 * c, 8)]), (qkv_ref, b_qkv), (vec_ref, b_vec))
        )
    ]
    for load in loads:
        load.start()
    p.greet()

    def to_partner(src, dst, slot):
        return pltpu.make_async_remote_copy(
            src_ref=src, dst_ref=dst, send_sem=pair_sent.at[slot], recv_sem=pair_came.at[slot],
            device_id=p.partner(), device_id_type=MESH_ID,
        )

    half = to_partner(out_ref.at[:, theirs], b_out.at[pl.ds(8 * c, 8)], 0)
    half.start()
    s_down, s_in, s_out, s_qkv, s_vec = (
        Scatter(p, blocks, landed, sent.at[i], came.at[i])
        for i, (blocks, landed) in enumerate(
            ((b_down, l_down), (b_in, l_in), (b_out, l_out), (b_qkv, l_qkv), (b_vec, l_vec))
        )
    )
    for i, s in enumerate((s_down, s_in, s_out, s_qkv, s_vec)):
        loads[i].wait()
        if i == 2:
            half.wait_recv()
        s.begin()

    def put(ref):
        def write(at, value):
            ref[at, :] = value

        return write

    finals = {0: f_down, 1: f_in, 2: f_out, 3: f_qkv, 4: f_vec}
    every = (s_down, s_in, s_out, s_qkv, s_vec)
    for s in every:
        for dz in (1, 2, 3, 0):
            s.across(dz)
        for dz in (1, 2, 3, 0):
            s.along(dz)
    for i, s in enumerate(every):
        s.total(put(finals[i]))
    pair = [
        to_partner(f_qkv.at[theirs], qkv_o.at[c], 1),
        to_partner(f_in.at[theirs], in_o.at[c], 2),
        to_partner(f_vec, n_vec, 3),
    ]
    for copy in pair:
        copy.start()
    stores = [
        pltpu.make_async_copy(f_down, down_o, local.at[5]),
        pltpu.make_async_copy(f_out, out_o, local.at[6]),
        pltpu.make_async_copy(f_qkv.at[mine], qkv_o.at[c], local.at[7]),
        pltpu.make_async_copy(f_in.at[mine], in_o.at[c], local.at[8]),
        pltpu.make_async_copy(f_vec, vec_o.at[0], local.at[9]),
    ]
    for store in stores:
        store.start()
    pair[2].wait_recv()
    other = pltpu.make_async_copy(n_vec, vec_o.at[1], local.at[10])
    other.start()
    for s in every:
        s.drain()
    half.wait_send()
    pair[0].wait()
    pair[1].wait()
    pair[2].wait_send()
    for store in stores:
        store.wait()
    other.wait()


def scatter_all(g_qkv, g_out, g_in, g_down, g_vec):
    bf, f32 = jnp.bfloat16, jnp.float32
    dq, do, di, dd = g_qkv.shape[2], g_out.shape[2], g_in.shape[2], g_down.shape[2]
    down = g_down.shape[1]
    outs = [((2, 32, dq), f32), ((32, do), f32), ((2, 32, di), f32), ((down, dd), f32), ((2, 16, 128), f32)]
    blocks = [((64, dq), bf), ((32, do), bf), ((64, di), bf), ((down, dd), bf), ((16, 128), f32)]
    return pl.pallas_call(
        scatter_kernel,
        out_shape=[jax.ShapeDtypeStruct(s, d) for s, d in outs],
        in_specs=[pl.BlockSpec(memory_space=pl.ANY)] * 5,
        out_specs=[pl.BlockSpec(memory_space=pl.ANY)] * 5,
        scratch_shapes=[pltpu.VMEM((16,) + s, d) for s, d in blocks]
        + [pltpu.VMEM((15,) + s, d) for s, d in blocks]
        + [pltpu.VMEM(s, f32) for s, d in blocks]
        + [pltpu.VMEM((16, 128), f32)]
        + [
            pltpu.SemaphoreType.DMA((5, 15)),
            pltpu.SemaphoreType.DMA((5, 15)),
            pltpu.SemaphoreType.DMA((4,)),
            pltpu.SemaphoreType.DMA((4,)),
            pltpu.SemaphoreType.DMA((11,)),
        ],
        compiler_params=pltpu.CompilerParams(
            collective_id=1, has_side_effects=True, vmem_limit_bytes=60 * 1024 * 1024
        ),
        name="gradients_scatter",
    )(g_qkv, g_out, g_in, g_down, g_vec)


def swap(value):
    return lax.ppermute(value, "c", [(0, 1), (1, 0)])


def local_split(
    inputs, segment_ids, cotangent, ln1_gain, ln1_shift, w_qkv, query_bias, value_bias, w_out, out_bias,
    ln2_gain, ln2_shift, w_in, in_bias, w_down, down_bias,
):
    f32, bf = jnp.float32, jnp.bfloat16
    c = lax.axis_index("c")
    narrow = lax.axis_index("x") * 2 + c
    wide = lax.axis_index("z") * 2 + lax.axis_index("y")
    length, d_model = inputs.shape
    rows = ln1_gain.shape[0]
    small = jnp.stack(
        [ln1_gain, ln1_shift, query_bias, value_bias, out_bias, ln2_gain, ln2_shift, down_bias]
    ).astype(f32)
    quarter = jnp.arange(4)[None, :, None] == narrow
    tile = jnp.where(quarter, small[:, None, :], 0.0).reshape(8, 128)
    tile = jnp.concatenate([tile, in_bias.astype(f32)[None], jnp.zeros((7, 128), f32)])
    wqkv2 = w_qkv.reshape(rows, 3, 2, d_model // 2).transpose(2, 0, 1, 3).reshape(2, rows, -1)
    win2 = w_in.reshape(rows, 16, 2, 128).transpose(2, 0, 1, 3).reshape(2, rows, -1)
    col = jnp.broadcast_to(segment_ids[:, None], (length, 128))
    row = jnp.broadcast_to(segment_ids[None, :], (8, length))
    half = d_model // 2
    (
        qkv_f, out_f, in_f, down_f, vecs, norm_one, triple, attended, lse, x2, r2, norm_two, slope, cot2, mask, grad_down,
        layer_out,
    ) = forward_all(wqkv2, w_out, win2, w_down, tile, inputs, cotangent, col, row)
    g1, g2 = vecs[0], vecs[5]
    qkv_m = qkv_f.reshape(d_model, -1)
    out_m = out_f.reshape(-1, d_model)
    in_m = in_f.reshape(d_model, -1)
    down_m = down_f.reshape(-1, d_model)
    cot = cot2.reshape(2 * length, d_model)
    pick = lambda a, i: lax.dynamic_index_in_dim(a, i, 0, False)
    x2 = x2.astype(f32)
    r2 = r2[:, :1]
    t5 = triple.reshape(2, length, 3, half // HD, HD)
    q, k, v = t5[:, :, 0], t5[:, :, 1], t5[:, :, 2]
    scores = jnp.einsum("sqhd,skhd->shqk", q, k, preferred_element_type=f32) * HD ** (-0.5) + mask[:, None]
    probs = jnp.exp(scores - lse[:, :, : half // HD].transpose(0, 2, 1)[..., None])
    probs_low = probs.astype(bf)
    grad_hidden = jnp.einsum("sd,fd->sf", cot, down_m, preferred_element_type=f32)
    grad_pre = (grad_hidden * slope.astype(f32)).astype(bf)
    grad_in = jnp.einsum("sd,sf->df", norm_two, grad_pre, preferred_element_type=f32).astype(bf)
    grad_in_bias = jnp.sum(grad_pre.astype(f32), 0)
    gn2 = jnp.einsum("sf,df->sd", grad_pre, in_m, preferred_element_type=f32)
    gn2 = gn2 + swap(gn2)
    gm = cot.astype(f32) + normalize_back(gn2, x2, r2, g2)
    grad_mixed = gm.astype(bf)
    grad_out = jnp.einsum("sd,se->de", attended, grad_mixed, preferred_element_type=f32).astype(bf)
    grad_att = jnp.einsum("se,de->sd", grad_mixed, out_m, preferred_element_type=f32).astype(bf)
    ga = grad_att.reshape(2, length, half // HD, HD)
    gp = jnp.einsum("sqhd,skhd->shqk", ga, v, preferred_element_type=f32)
    gs = (probs * (gp - jnp.sum(probs * gp, -1, keepdims=True))).astype(bf)
    gq = jnp.einsum("shqk,skhd->sqhd", gs, k, preferred_element_type=f32) * HD ** (-0.5)
    gk = jnp.einsum("shqk,sqhd->skhd", gs, q, preferred_element_type=f32) * HD ** (-0.5)
    gv = jnp.einsum("shqk,sqhd->skhd", probs_low, ga, preferred_element_type=f32)
    gt = jnp.stack([gq, gk, gv], 2).reshape(2 * length, 3 * half).astype(bf)
    grad_qkv = jnp.einsum("sd,st->dt", norm_one, gt, preferred_element_type=f32).astype(bf)
    gqb = jnp.sum(gt[:, :half].astype(f32), 0)
    gvb = jnp.sum(gt[:, 2 * half :].astype(f32), 0)
    gn1 = jnp.einsum("st,dt->sd", gt, qkv_m, preferred_element_type=f32).reshape(2, length, d_model)
    gn1 = pick(gn1, c) + swap(pick(gn1, 1 - c))
    own = lambda a: pick(a.reshape(2, length, d_model), c)
    _, x1, r1 = normalize(inputs.astype(f32), g1, g1)
    grad_input = own(gm) + normalize_back(gn1, x1, r1, g1)
    put = lambda v: lax.dynamic_update_slice(jnp.zeros((d_model,), f32), v, (c * half,))
    sums = jnp.stack(
        [
            jnp.sum(gn1 * x1, 0), jnp.sum(gn1, 0), put(gqb), put(gvb), jnp.sum(own(grad_mixed).astype(f32), 0),
            jnp.sum(own(gn2 * x2), 0), jnp.sum(own(gn2), 0), jnp.sum(own(cot).astype(f32), 0),
        ]
    )
    gvec = jnp.repeat(sums.reshape(8, 8, 128).transpose(1, 0, 2), 2, 0)
    gvec = jnp.concatenate([gvec, grad_in_bias.reshape(16, 1, 128), jnp.zeros((16, 7, 128), f32)], 1)
    d_qkv, d_out, d_in, d_down, d_vec = scatter_all(
        grad_qkv.reshape(16, 64, -1), grad_out.reshape(8, 64, -1), grad_in.reshape(16, 64, -1),
        grad_down.reshape(16, 128, -1), gvec,
    )
    d_qkv = d_qkv.reshape(2, rows, 3, half).transpose(1, 2, 0, 3).reshape(rows, -1)
    d_in = d_in.reshape(2, rows, 16, 128).transpose(1, 2, 0, 3).reshape(rows, -1)
    eight = (d_vec[0, :8] + d_vec[1, :8]).reshape(8, 4, 32)
    eight = lax.dynamic_index_in_dim(eight, narrow, 1, False)
    return (
        layer_out, grad_input, eight[0], eight[1], d_qkv, eight[2], eight[3], d_out, eight[4],
        eight[5], eight[6], d_in, d_vec[0, 8], d_down, eight[7],
    )


def solution(mesh):
    sizes = tuple(mesh.shape.values())
    step, names = local, (("wide", "narrow"),)
    if sizes == (8, 4):
        mesh = Mesh(mesh.devices.reshape(4, 2, 2, 2), ("z", "y", "x", "c"))
        step, names = local_split, (("z", "y", "x", "c"),)
    line, plane = P(names[0]), P(names[0], None)
    return jax.shard_map(
        step,
        mesh=mesh,
        in_specs=(plane, line, plane, line, line, plane, line, line, plane, line, line, line, plane, line, plane, line),
        out_specs=(plane, plane, line, line, plane, line, line, plane, line, line, line, plane, line, plane, line),
        check_vma=False,
    )
```

```python
import functools

import jax
import jax.numpy as jnp
from jax import lax
from jax.experimental import pallas as pl
from jax.experimental.pallas import tpu as pltpu
from jax.sharding import Mesh
from jax.sharding import PartitionSpec as P

HD = 64


EPS = 1e-05
ROOT_HALF = 0.7071067811865476
INV_ROOT_TAU = 0.3989422804014327
NEG_FILL = -1000000000.0


def normalize(values, gain, shift):
    average = jnp.mean(values, -1, keepdims=True)
    centred = values - average
    inverse = lax.rsqrt(jnp.mean(centred * centred, -1, keepdims=True) + EPS)
    normed = centred * inverse
    return (normed * gain + shift, normed, inverse)


def normalize_back(grad_norm, normed, inverse, gain):
    scaled = grad_norm * gain
    return inverse * (
        scaled
        - jnp.mean(scaled, -1, keepdims=True)
        - normed * jnp.mean(scaled * normed, -1, keepdims=True)
    )


def gelu_value(pre_act):
    return 0.5 * pre_act * (1.0 + lax.erf(pre_act * ROOT_HALF))


def gelu_slope(pre_act):
    return (
        0.5 * (1.0 + lax.erf(pre_act * ROOT_HALF))
        + pre_act * jnp.exp(-0.5 * pre_act * pre_act) * INV_ROOT_TAU
    )


def gather_forward(shards):
    return (
        lax.all_gather(shards[0], ("wide", "narrow"), axis=0, tiled=True),
        lax.all_gather(shards[1], ("wide", "narrow"), axis=0, tiled=True),
        lax.all_gather(shards[2], ("wide", "narrow"), axis=0, tiled=True),
        lax.all_gather(shards[3], ("wide", "narrow"), axis=0, tiled=True),
        lax.all_gather(shards[4], ("wide", "narrow"), axis=0, tiled=True),
        lax.all_gather(shards[5], ("wide", "narrow"), axis=0, tiled=True),
        lax.all_gather(shards[6], ("wide", "narrow"), axis=0, tiled=True),
        lax.all_gather(shards[7], ("wide", "narrow"), axis=0, tiled=True),
        lax.all_gather(shards[8], ("wide", "narrow"), axis=0, tiled=True),
        lax.all_gather(shards[9], ("wide", "narrow"), axis=0, tiled=True),
        lax.all_gather(shards[10], ("wide", "narrow"), axis=0, tiled=True),
        lax.all_gather(shards[11], ("wide", "narrow"), axis=0, tiled=True),
        lax.all_gather(shards[12], ("wide", "narrow"), axis=0, tiled=True),
    )


def gather_backward(shards):
    return (
        lax.all_gather(shards[0], ("wide", "narrow"), axis=0, tiled=True),
        lax.all_gather(shards[1], ("wide", "narrow"), axis=0, tiled=True),
        lax.all_gather(shards[2], ("wide", "narrow"), axis=0, tiled=True),
        lax.all_gather(shards[3], ("wide", "narrow"), axis=0, tiled=True),
        lax.all_gather(shards[4], ("wide", "narrow"), axis=0, tiled=True),
        lax.all_gather(shards[5], ("wide", "narrow"), axis=0, tiled=True),
        lax.all_gather(shards[6], ("wide", "narrow"), axis=0, tiled=True),
        lax.all_gather(shards[7], ("wide", "narrow"), axis=0, tiled=True),
        lax.all_gather(shards[8], ("wide", "narrow"), axis=0, tiled=True),
        lax.all_gather(shards[9], ("wide", "narrow"), axis=0, tiled=True),
        lax.all_gather(shards[10], ("wide", "narrow"), axis=0, tiled=True),
        lax.all_gather(shards[11], ("wide", "narrow"), axis=0, tiled=True),
        lax.all_gather(shards[12], ("wide", "narrow"), axis=0, tiled=True),
    )


def reduce_grads(grads):
    return (
        lax.psum_scatter(grads[0], ("wide", "narrow"), scatter_dimension=0, tiled=True),
        lax.psum_scatter(grads[1], ("wide", "narrow"), scatter_dimension=0, tiled=True),
        lax.psum_scatter(grads[2], ("wide", "narrow"), scatter_dimension=0, tiled=True),
        lax.psum_scatter(grads[3], ("wide", "narrow"), scatter_dimension=0, tiled=True),
        lax.psum_scatter(grads[4], ("wide", "narrow"), scatter_dimension=0, tiled=True),
        lax.psum_scatter(grads[5], ("wide", "narrow"), scatter_dimension=0, tiled=True),
        lax.psum_scatter(grads[6], ("wide", "narrow"), scatter_dimension=0, tiled=True),
        lax.psum_scatter(grads[7], ("wide", "narrow"), scatter_dimension=0, tiled=True),
        lax.psum_scatter(grads[8], ("wide", "narrow"), scatter_dimension=0, tiled=True),
        lax.psum_scatter(grads[9], ("wide", "narrow"), scatter_dimension=0, tiled=True),
        lax.psum_scatter(grads[10], ("wide", "narrow"), scatter_dimension=0, tiled=True),
        lax.psum_scatter(grads[11], ("wide", "narrow"), scatter_dimension=0, tiled=True),
        lax.psum_scatter(grads[12], ("wide", "narrow"), scatter_dimension=0, tiled=True),
    )


def head_block(triple_b, offset, group_width, d_model):
    length = triple_b.shape[0]
    queries = triple_b[:, offset : offset + group_width].reshape(length, group_width // HD, HD)
    key_rows = triple_b[:, d_model + offset : d_model + offset + group_width].reshape(
        length, group_width // HD, HD
    )
    values = triple_b[:, 2 * d_model + offset : 2 * d_model + offset + group_width].reshape(
        length, group_width // HD, HD
    )
    return (queries, key_rows, values)


def block_scores(queries, key_rows, allowed):
    scores = jnp.einsum(
        "qhd,khd->hqk", queries, key_rows, preferred_element_type=jnp.float32
    ) * HD ** (-0.5)
    return jnp.where(allowed[None], scores, NEG_FILL)


def attend(triple_b, allowed, d_model):
    length = triple_b.shape[0]
    group_width = 4 * HD
    pieces = []
    log_totals = []
    for offset in range(0, d_model, group_width):
        queries, key_rows, values = head_block(triple_b, offset, group_width, d_model)
        scores = block_scores(queries, key_rows, allowed)
        highest = jnp.max(scores, -1, keepdims=True)
        exponent = jnp.exp(scores - highest)
        row_total = jnp.sum(exponent, -1, keepdims=True)
        probs_low = (exponent / row_total).astype(jnp.bfloat16)
        mixed = jnp.einsum("hqk,khd->qhd", probs_low, values, preferred_element_type=jnp.float32)
        pieces.append(mixed.reshape(length, group_width))
        log_totals.append(highest + jnp.log(row_total))
    return (jnp.concatenate(pieces, 1), log_totals)


def attend_back(triple_b, grad_att_b, allowed, log_totals, d_model):
    length = triple_b.shape[0]
    group_width = 4 * HD
    query_parts = []
    key_parts = []
    value_parts = []
    for index, offset in enumerate(range(0, d_model, group_width)):
        queries, key_rows, values = head_block(triple_b, offset, group_width, d_model)
        scores = block_scores(queries, key_rows, allowed)
        attn_probs = jnp.exp(scores - log_totals[index])
        probs_low = attn_probs.astype(jnp.bfloat16)
        grad_heads = grad_att_b[:, offset : offset + group_width].reshape(
            length, group_width // HD, HD
        )
        grad_probs = jnp.einsum(
            "qhd,khd->hqk", grad_heads, values, preferred_element_type=jnp.float32
        )
        inner_sum = jnp.sum(attn_probs * grad_probs, -1, keepdims=True)
        grad_scores = (attn_probs * (grad_probs - inner_sum)).astype(jnp.bfloat16)
        grad_query = jnp.einsum(
            "hqk,khd->qhd", grad_scores, key_rows, preferred_element_type=jnp.float32
        ) * HD ** (-0.5)
        grad_key = jnp.einsum(
            "hqk,qhd->khd", grad_scores, queries, preferred_element_type=jnp.float32
        ) * HD ** (-0.5)
        grad_value = jnp.einsum(
            "hqk,qhd->khd", probs_low, grad_heads, preferred_element_type=jnp.float32
        )
        query_parts.append(grad_query.reshape(length, group_width))
        key_parts.append(grad_key.reshape(length, group_width))
        value_parts.append(grad_value.reshape(length, group_width))
    return jnp.concatenate(query_parts + key_parts + value_parts, 1).astype(jnp.bfloat16)


def local(
    inputs,
    segment_ids,
    cotangent,
    ln1_gain,
    ln1_shift,
    w_qkv,
    query_bias,
    value_bias,
    w_out,
    out_bias,
    ln2_gain,
    ln2_shift,
    w_in,
    in_bias,
    w_down,
    down_bias,
):
    shards = (
        ln1_gain,
        ln1_shift,
        w_qkv,
        query_bias,
        value_bias,
        w_out,
        out_bias,
        ln2_gain,
        ln2_shift,
        w_in,
        in_bias,
        w_down,
        down_bias,
    )
    fwd_weights = gather_forward(shards)
    (
        gain_one,
        shift_one,
        qkv_full,
        qbias_full,
        vbias_full,
        outw_full,
        outb_full,
        gain_two,
        shift_two,
        inw_full,
        inb_full,
        downw_full,
        downb_full,
    ) = fwd_weights
    d_model = inputs.shape[1]
    length = inputs.shape[0]
    tokens = inputs.astype(jnp.float32)
    position = jnp.arange(length, dtype=jnp.int32)
    allowed = (segment_ids[:, None] == segment_ids[None, :]) & (segment_ids[:, None] >= 0) | (
        position[:, None] == position[None, :]
    )
    normed_out, normed_one, inverse_one = normalize(
        tokens, gain_one.astype(jnp.float32), shift_one.astype(jnp.float32)
    )
    norm_one = normed_out.astype(jnp.bfloat16)
    shifts = jnp.concatenate(
        [
            qbias_full.astype(jnp.float32),
            jnp.zeros((d_model,), jnp.float32),
            vbias_full.astype(jnp.float32),
        ]
    )
    triple_b = (jnp.dot(norm_one, qkv_full, preferred_element_type=jnp.float32) + shifts).astype(
        jnp.bfloat16
    )
    attended_f, log_totals = attend(triple_b, allowed, d_model)
    attended = attended_f.astype(jnp.bfloat16)
    middle = (
        tokens
        + jnp.dot(attended, outw_full, preferred_element_type=jnp.float32)
        + outb_full.astype(jnp.float32)
    )
    normed_out_two, normed_two, inverse_two = normalize(
        middle, gain_two.astype(jnp.float32), shift_two.astype(jnp.float32)
    )
    norm_two = normed_out_two.astype(jnp.bfloat16)
    pre_act = jnp.dot(norm_two, inw_full, preferred_element_type=jnp.float32) + inb_full.astype(
        jnp.float32
    )
    hidden = gelu_value(pre_act).astype(jnp.bfloat16)
    layer_out = (
        middle
        + jnp.dot(hidden, downw_full, preferred_element_type=jnp.float32)
        + downb_full.astype(jnp.float32)
    )
    back_weights = gather_backward(shards)
    (
        gain_one_b,
        shift_one_b,
        qkv_back,
        qbias_back,
        vbias_back,
        outw_back,
        outb_back,
        gain_two_b,
        shift_two_b,
        inw_back,
        inb_back,
        downw_back,
        downb_back,
    ) = back_weights
    grad_top = cotangent.astype(jnp.float32)
    grad_w_down = jnp.einsum("sf,sd->fd", hidden, cotangent, preferred_element_type=jnp.float32)
    grad_down_bias = jnp.sum(grad_top, 0)
    grad_hidden = jnp.einsum("sd,fd->sf", cotangent, downw_back, preferred_element_type=jnp.float32)
    grad_pre = (grad_hidden * gelu_slope(pre_act)).astype(jnp.bfloat16)
    grad_w_in = jnp.einsum("sd,sf->df", norm_two, grad_pre, preferred_element_type=jnp.float32)
    grad_in_bias = jnp.sum(grad_pre.astype(jnp.float32), 0)
    grad_norm_two = jnp.einsum("sf,df->sd", grad_pre, inw_back, preferred_element_type=jnp.float32)
    grad_ln2_gain = jnp.sum(grad_norm_two * normed_two, 0)
    grad_ln2_shift = jnp.sum(grad_norm_two, 0)
    grad_middle = grad_top + normalize_back(
        grad_norm_two, normed_two, inverse_two, gain_two_b.astype(jnp.float32)
    )
    grad_mixed = grad_middle.astype(jnp.bfloat16)
    grad_w_out = jnp.einsum("sd,se->de", attended, grad_mixed, preferred_element_type=jnp.float32)
    grad_out_bias = jnp.sum(grad_mixed.astype(jnp.float32), 0)
    grad_attended = jnp.einsum(
        "se,de->sd", grad_mixed, outw_back, preferred_element_type=jnp.float32
    ).astype(jnp.bfloat16)
    grad_triple = attend_back(triple_b, grad_attended, allowed, log_totals, d_model)
    grad_w_qkv = jnp.einsum("sd,st->dt", norm_one, grad_triple, preferred_element_type=jnp.float32)
    grad_query_bias = jnp.sum(grad_triple[:, :d_model].astype(jnp.float32), 0)
    grad_value_bias = jnp.sum(grad_triple[:, 2 * d_model :].astype(jnp.float32), 0)
    grad_norm_one = jnp.einsum(
        "st,dt->sd", grad_triple, qkv_back, preferred_element_type=jnp.float32
    )
    grad_ln1_gain = jnp.sum(grad_norm_one * normed_one, 0)
    grad_ln1_shift = jnp.sum(grad_norm_one, 0)
    grad_input = grad_middle + normalize_back(
        grad_norm_one, normed_one, inverse_one, gain_one_b.astype(jnp.float32)
    )
    owned = reduce_grads(
        (
            grad_ln1_gain,
            grad_ln1_shift,
            grad_w_qkv,
            grad_query_bias,
            grad_value_bias,
            grad_w_out,
            grad_out_bias,
            grad_ln2_gain,
            grad_ln2_shift,
            grad_w_in,
            grad_in_bias,
            grad_w_down,
            grad_down_bias,
        )
    )
    return (
        layer_out,
        grad_input,
        owned[0],
        owned[1],
        owned[2],
        owned[3],
        owned[4],
        owned[5],
        owned[6],
        owned[7],
        owned[8],
        owned[9],
        owned[10],
        owned[11],
        owned[12],
    )


MESH_ID = pl.DeviceIdType.MESH
ROWS = 32
BF, F32 = jnp.bfloat16, jnp.float32


class Place:
    def __init__(self):
        self.z = lax.axis_index("z")
        self.y = lax.axis_index("y")
        self.x = lax.axis_index("x")
        self.c = lax.axis_index("c")

    def chip(self, dz=0, dy=0, dx=0):
        z = self.z
        if dz == 2:
            z = lax.rem(z + 2, 4)
        elif dz == 1:
            z = z + 1 - 2 * lax.rem(z, 2)
        elif dz == 3:
            z = 3 - z
        y = 1 - self.y if dy else self.y
        x = 1 - self.x if dx else self.x
        return z, y, x

    def index(self, dz=0, dy=0, dx=0):
        z, y, x = self.chip(dz, dy, dx)
        return (z * 2 + y) * 2 + x

    def device(self, dz=0, dy=0, dx=0):
        z, y, x = self.chip(dz, dy, dx)
        return {"z": z, "y": y, "x": x, "c": self.c}

    def partner(self):
        return {"z": self.z, "y": self.y, "x": self.x, "c": 1 - self.c}

    def greet(self):
        barrier = pltpu.get_barrier_semaphore()
        peers = [self.device(dz=1), self.device(dz=2), self.device(dz=3)]
        peers += [self.device(dy=1), self.device(dx=1), self.partner()]
        for peer in peers:
            pl.semaphore_signal(barrier, inc=1, device_id=peer, device_id_type=MESH_ID)
        pl.semaphore_wait(barrier, len(peers))


class Pair:
    def __init__(self, place, sent, came):
        self.p, self.sent, self.came = place, sent, came

    def copy(self, src, dst, slot):
        return pltpu.make_async_remote_copy(
            src_ref=src,
            dst_ref=dst,
            send_sem=self.sent.at[slot],
            recv_sem=self.came.at[slot],
            device_id=self.p.partner(),
            device_id_type=MESH_ID,
        )


Z_AT, X_AT, Y_AT, D_AT = -1, 3, 7, 11


class Gather:
    def __init__(self, place, blocks, sent, came):
        self.p, self.blocks, self.sent, self.came = place, blocks, sent, came
        self.left = []

    def copy(self, block, slot, to):
        at = self.p.index(**block)
        return pltpu.make_async_remote_copy(
            src_ref=self.blocks.at[at],
            dst_ref=self.blocks.at[at],
            send_sem=self.sent.at[slot],
            recv_sem=self.came.at[slot],
            device_id=self.p.device(**to),
            device_id_type=MESH_ID,
        )

    def send(self, block, slot, to):
        self.copy(block, slot, to).start()
        self.left.append((block, slot, to))

    def wait(self, block, slot):
        self.copy(block, slot, dict(dx=1)).wait_recv()

    def begin(self):
        for dz in (3, 2, 1):
            self.send({}, Z_AT + dz, dict(dz=dz))
        self.send({}, X_AT, dict(dx=1))
        self.send({}, Y_AT, dict(dy=1))

    def along(self, dz):
        self.wait(dict(dz=dz), Z_AT + dz)
        self.send(dict(dz=dz), X_AT + dz, dict(dx=1))
        self.send(dict(dz=dz), Y_AT + dz, dict(dy=1))

    def across(self, dz):
        if dz < 2:
            self.wait(dict(dz=dz, dx=1), X_AT + dz)
            self.send(dict(dz=dz, dx=1), D_AT + dz, dict(dy=1))
        else:
            self.wait(dict(dz=dz, dy=1), Y_AT + dz)
            self.send(dict(dz=dz, dy=1), D_AT + dz, dict(dx=1))

    def finish(self):
        for dz in range(4):
            if dz < 2:
                self.wait(dict(dz=dz, dy=1), Y_AT + dz)
            else:
                self.wait(dict(dz=dz, dx=1), X_AT + dz)
        for dz in range(4):
            self.wait(dict(dz=dz, dy=1, dx=1), D_AT + dz)

    def steps(self):
        for dz in (1, 2, 3):
            yield functools.partial(self.along, dz)
        for dz in (0, 1, 2, 3):
            yield functools.partial(self.across, dz)

    def drain(self):
        for block, slot, to in self.left:
            self.copy(block, slot, to).wait_send()


class Scatter:
    def __init__(self, place, blocks, landed, sent, came):
        self.p, self.blocks, self.landed = place, blocks, landed
        self.sent, self.came = sent, came
        self.left = []

    def copy(self, block, slot, to):
        return pltpu.make_async_remote_copy(
            src_ref=self.blocks.at[self.p.index(**block)],
            dst_ref=self.landed.at[slot],
            send_sem=self.sent.at[slot],
            recv_sem=self.came.at[slot],
            device_id=self.p.device(**to),
            device_id_type=MESH_ID,
        )

    def send(self, block, slot, to):
        self.copy(block, slot, to).start()
        self.left.append((block, slot, to))

    def wait(self, slot):
        self.copy({}, slot, dict(dx=1)).wait_recv()

    def add(self, at, slots, write):
        rows = self.blocks.shape[1]
        step = 16

        def body(i, carry):
            some = pl.ds(pl.multiple_of(i * step, step), step)
            total = self.blocks[at, some, :].astype(F32)
            for slot in slots:
                total = total + self.landed[slot, some, :].astype(F32)
            write(some, total)
            return carry

        lax.fori_loop(0, rows // step, body, 0)

    def merge(self, block, slots):
        at = self.p.index(**block)

        def write(some, total):
            self.blocks[at, some, :] = total.astype(self.blocks.dtype)

        self.add(at, slots, write)

    def begin(self):
        for dz in (1, 2, 3, 0):
            if dz < 2:
                self.send(dict(dz=dz, dy=1, dx=1), D_AT + dz, dict(dy=1))
                self.send(dict(dz=dz, dy=1), Y_AT + dz, dict(dy=1))
            else:
                self.send(dict(dz=dz, dy=1, dx=1), D_AT + dz, dict(dx=1))
                self.send(dict(dz=dz, dx=1), X_AT + dz, dict(dx=1))

    def across(self, dz):
        self.wait(D_AT + dz)
        if dz < 2:
            self.merge(dict(dz=dz, dx=1), (D_AT + dz,))
            self.send(dict(dz=dz, dx=1), X_AT + dz, dict(dx=1))
        else:
            self.merge(dict(dz=dz, dy=1), (D_AT + dz,))
            self.send(dict(dz=dz, dy=1), Y_AT + dz, dict(dy=1))

    def along(self, dz):
        self.wait(X_AT + dz)
        self.wait(Y_AT + dz)
        if dz:
            self.merge(dict(dz=dz), (X_AT + dz, Y_AT + dz))
            self.send(dict(dz=dz), Z_AT + dz, dict(dz=dz))

    def total(self, write):
        for dz in (1, 2, 3):
            self.wait(Z_AT + dz)
        self.add(self.p.index(), (X_AT, Y_AT, Z_AT + 1, Z_AT + 2, Z_AT + 3), write)

    def steps(self):
        for dz in (1, 2, 3, 0):
            yield functools.partial(self.across, dz)
        for dz in (1, 2, 3, 0):
            yield functools.partial(self.along, dz)

    def drain(self):
        for block, slot, to in self.left:
            self.copy(block, slot, to).wait_send()


class Pump:
    def __init__(self):
        self.queue = []

    def add(self, steps):
        self.queue.extend(steps)

    def take(self, count):
        now, self.queue = self.queue[:count], self.queue[count:]
        for step in now:
            step()

    def loop(self, trips, body, per_trip=0):
        groups = []
        for i in range(trips):
            groups.append(self.queue[:per_trip])
            self.queue = self.queue[per_trip:]

        def trip(i, carry):
            body(i)
            for k, group in enumerate(groups):
                if group:

                    @pl.when(i == k)
                    def _(group=group):
                        for step in group:
                            step()

            return carry

        lax.fori_loop(0, trips, trip, 0)


NN = (((1,), (0,)), ((), ()))
NT = (((1,), (1,)), ((), ()))
TN = (((0,), (0,)), ((), ()))


def mm(a, b, dims=NN):
    return lax.dot_general(a, b, dims, preferred_element_type=F32)


def span(i, size):
    if isinstance(i, int):
        return pl.ds(i * size, size)
    return pl.ds(pl.multiple_of(i * size, size), size)


def stats(v):
    average = jnp.mean(v, -1, keepdims=True)
    centred = v - average
    inverse = lax.rsqrt(jnp.mean(centred * centred, -1, keepdims=True) + EPS)
    return centred * inverse, inverse


def build_mask(mask, seg_col, seg_row):
    size = mask.shape[1]
    for s in range(2):

        def body(i, carry, s=s):
            rows = span(i, 128)
            col = seg_col[s, rows, :][:, :1]
            row = seg_row[s, :1, :]
            here = lax.broadcasted_iota(jnp.int32, (128, size), 0) + i * 128
            there = lax.broadcasted_iota(jnp.int32, (128, size), 1)
            fine = ((col == row) & (col >= 0)) | (here == there)
            mask[s, rows, :] = jnp.where(fine, 0.0, NEG_FILL).astype(BF)
            return carry

        lax.fori_loop(0, size // 128, body, 0)


def build_vectors(vecs, hidden_shift, triple_shift, tiles, c):
    for w in range(8):
        vecs[0:8, 128 * w : 128 * (w + 1)] = tiles[2 * w, 0:8, :] + tiles[2 * w + 1, 0:8, :]
    for j in range(16):
        hidden_shift[0:1, 128 * j : 128 * (j + 1)] = tiles[j, 8:9, :]
    half = vecs.shape[1] // 2
    first = c == 0
    triple_shift[0:1, 0:half] = jnp.where(first, vecs[2:3, 0:half], vecs[2:3, half:])
    triple_shift[0:1, half : 2 * half] = jnp.zeros((1, half), F32)
    triple_shift[0:1, 2 * half :] = jnp.where(first, vecs[3:4, 0:half], vecs[3:4, half:])


G1, B1, QB, VB, OB, G2, B2, DB = range(8)
INV_AT = 64


def attend_pair(i, triple, mask, attended, lse):
    length = mask.shape[1]
    half = attended.shape[1]
    pairs = half // 128
    s, pair = i // pairs, lax.rem(i, pairs)
    rows = span(s, length)
    q = triple[rows, pl.ds(pl.multiple_of(pair * 128, 128), 128)]
    k = triple[rows, pl.ds(pl.multiple_of(half + pair * 128, 128), 128)]
    v = triple[rows, pl.ds(pl.multiple_of(2 * half + pair * 128, 128), 128)]
    lane = lax.broadcasted_iota(jnp.int32, (length, 128), 1)
    low = lane < HD
    outs = []
    kept = lse[s]
    for h in range(2):
        mine = low if h == 0 else ~low
        scores = mm(jnp.where(mine, q, jnp.zeros_like(q)), k, NT) * HD ** (-0.5) + mask[s].astype(F32)
        highest = jnp.max(scores, -1, keepdims=True)
        exponent = jnp.exp(scores - highest)
        total = jnp.sum(exponent, -1, keepdims=True)
        probs = (exponent * (1.0 / total)).astype(BF)
        outs.append(mm(probs, v))
        kept = jnp.where(lane == pair * 2 + h, highest + jnp.log(total), kept)
    lse[s] = kept
    attended[rows, pl.ds(pl.multiple_of(pair * 128, 128), 128)] = jnp.where(low, outs[0], outs[1]).astype(BF)


def forward_kernel(
    wqkv_ref, wout_ref, win_ref, wdown_ref, tile_ref, tok_ref, cot_ref, col_ref, row_ref,
    qkv_o, out_o, in_o, down_o, vecs_o, norm1_o, triple_o, att_o, lse_o, xhat_o, norm2_o, slope_o, cot_o,
    mask_o, gdown_o, layer_o,
    w_qkv, w_nat, w_out, w_in, w_down, tiles, tile, tile_in, tok, cot, col, row, mask,
    vecs, hshift, tshift, norm1, triple, att, lse, mid, part, part_in, last_in, norm2, xhat, hidden, slope, gdown,
    sent, came, pair_sent, pair_came, local,
):
    p = Place()
    own, c = p.index(), p.c
    length = tok.shape[1]
    mine = pl.ds(pl.multiple_of(ROWS * c, ROWS), ROWS)
    slots = iter(range(local.shape[0]))

    def load(src, dst):
        copy = pltpu.make_async_copy(src, dst, local.at[next(slots)])
        copy.start()
        return copy

    loads = [
        load(wqkv_ref.at[c], w_qkv.at[own, mine]),
        load(wout_ref, w_nat.at[own]),
        load(win_ref.at[c], w_in.at[own, mine]),
        load(wdown_ref, w_down.at[own]),
        load(tile_ref, tile),
        load(tok_ref, tok.at[c]),
        load(cot_ref, cot.at[c]),
        load(col_ref, col.at[c]),
        load(row_ref, row.at[c]),
    ]
    p.greet()
    pair = Pair(p, pair_sent, pair_came)
    swaps = [
        pair.copy(tile_ref, tile_in, 0),
        pair.copy(wqkv_ref.at[1 - c], w_qkv.at[own, mine], 1),
        pair.copy(win_ref.at[1 - c], w_in.at[own, mine], 2),
        pair.copy(row_ref, row.at[c], 3),
        pair.copy(col_ref, col.at[c], 4),
        pair.copy(tok_ref, tok.at[c], 5),
        pair.copy(cot_ref, cot.at[c], 6),
    ]
    for copy in swaps:
        copy.start()
    g_qkv, g_out, g_in, g_down, g_vec = (
        Gather(p, blocks, sent.at[i], came.at[i])
        for i, blocks in enumerate((w_qkv, w_nat, w_in, w_down, tiles))
    )
    loads[0].wait()
    swaps[1].wait_recv()
    g_qkv.begin()
    loads[4].wait()
    swaps[0].wait_recv()
    tiles[own, 0:8, :] = tile[0:8, :] + tile_in[0:8, :]
    tiles[own, 8:16, :] = tile[8:16, :]
    g_vec.begin()
    loads[1].wait()
    g_out.begin()
    loads[2].wait()
    swaps[2].wait_recv()
    g_in.begin()
    loads[3].wait()
    g_down.begin()
    pump = Pump()
    for g in (g_vec, g_qkv, g_out, g_in, g_down):
        pump.add(g.steps())
    for i in (7, 8, 5):
        loads[i].wait()
    for i in (3, 4, 5):
        swaps[i].wait_recv()
    build_mask(mask, col, row)
    pump.take(7)
    g_vec.finish()
    build_vectors(vecs, hshift, tshift, tiles, c)
    tokens = tok.shape[0] * length

    def first_norm(i):
        rows = span(i, 128)
        v = tok[i // 4, span(lax.rem(i, 4), 128), :].astype(F32)
        normed, _ = stats(v)
        norm1[rows, :] = (normed * vecs[G1 : G1 + 1, :] + vecs[B1 : B1 + 1, :]).astype(BF)

    pump.loop(tokens // 128, first_norm, 0)
    pump.take(7)
    g_qkv.finish()
    stores = [load(w_qkv, qkv_o), load(norm1, norm1_o), load(vecs, vecs_o), load(mask, mask_o)]
    depth = norm1.shape[1]

    def project(i):
        cols = span(i, 256)
        w = w_qkv[:, :, cols].reshape(depth, 256)
        triple[:, cols] = (mm(norm1[...], w) + tshift[0:1, cols]).astype(BF)

    pump.loop(triple.shape[1] // 256, project, 1)
    stores.append(load(triple, triple_o))
    lse[...] = jnp.zeros_like(lse)
    pump.loop(8, functools.partial(attend_pair, triple=triple, mask=mask, attended=att, lse=lse), 1)
    stores.append(load(att, att_o))
    g_out.finish()
    half = pair.copy(w_nat.at[pl.ds(8 * (1 - c), 8)], w_out.at[:, mine], 7)
    half.start()
    keep = load(w_nat.at[pl.ds(8 * c, 8)], w_out.at[:, mine])
    keep.wait()
    half.wait_recv()
    stores.append(load(w_out, out_o))

    def send_part(i):
        rows = span(i, 256)
        return pair.copy(part.at[rows], part_in.at[rows], 8 + i)

    def mix(i):
        rows = span(i, 256)
        own_part = mm(att[rows, :], w_out[...].reshape(att.shape[1], depth))
        part[rows, :] = own_part.astype(BF)
        send_part(i).start()
        v = tok[i // 2, span(lax.rem(i, 2), 256), :].astype(F32)
        mid[rows, :] = v + own_part + vecs[OB : OB + 1, :]

    pump.loop(4, mix, 0)

    def second_norm(i):
        send_part(i).wait_recv()
        rows = span(i, 256)
        v = mid[rows, :] + part_in[rows, :].astype(F32)
        mid[rows, :] = v
        normed, inverse = stats(v)
        xhat[rows, :] = normed.astype(BF)
        lane = lax.broadcasted_iota(jnp.int32, (256, 128), 1)
        inside = span(lax.rem(i, 2), 256)
        lse[i // 2, inside, :] = jnp.where(lane < INV_AT, lse[i // 2, inside, :], inverse)
        norm2[rows, :] = (normed * vecs[G2 : G2 + 1, :] + vecs[B2 : B2 + 1, :]).astype(BF)

    pump.loop(4, second_norm, 0)
    stores += [load(xhat, xhat_o), load(lse, lse_o), load(norm2, norm2_o)]
    pump.take(max(len(pump.queue) - 7, 0))
    g_in.finish()
    stores.append(load(w_in, in_o))

    def expand(i):
        cols = span(i, 256)
        w = w_in[:, :, cols].reshape(depth, 256)
        pre = mm(norm2[...], w) + hshift[0:1, cols]
        bell = 0.5 * (1.0 + lax.erf(pre * ROOT_HALF))
        hidden[:, cols] = (pre * bell).astype(BF)
        slope[:, cols] = (bell + pre * jnp.exp(-0.5 * pre * pre) * INV_ROOT_TAU).astype(BF)

    loads[6].wait()
    swaps[6].wait_recv()
    stores.append(load(cot, cot_o))
    pump.loop(hidden.shape[1] // 256, expand, 1)
    stores.append(load(slope, slope_o))

    def down_grad(i):
        cols = span(i, 256)
        grad = mm(hidden[:, cols], cot[...].reshape(tokens, depth), TN).astype(BF)
        gdown[pl.ds(pl.multiple_of(2 * i, 2), 2)] = grad.reshape(2, 128, depth)

    pump.loop(hidden.shape[1] // 256, down_grad, 1)
    stores.append(load(gdown, gdown_o))
    pump.take(len(pump.queue))
    g_down.finish()
    stores.append(load(w_down, down_o))
    for i in range(4):
        send_part(i).wait_send()
    yours, ours = span(1 - c, length), span(c, length)
    units = hidden.shape[1]

    def theirs(i):
        cols = span(i, 256)
        w = w_down[:, :, cols].reshape(units, 256)
        part[yours, cols] = mm(hidden[yours, :], w).astype(BF)

    lax.fori_loop(0, depth // 256, lambda i, carry: (theirs(i), carry)[1], 0)
    last = pair.copy(part.at[yours], last_in, 12)
    last.start()

    def contract(i):
        cols = span(i, 256)
        w = w_down[:, :, cols].reshape(units, 256)
        mid[ours, cols] = mid[ours, cols] + mm(hidden[ours, :], w) + vecs[DB : DB + 1, cols]

    lax.fori_loop(0, depth // 256, lambda i, carry: (contract(i), carry)[1], 0)
    last.wait_recv()
    mid[ours, :] = mid[ours, :] + last_in[...].astype(F32)
    stores.append(load(mid.at[ours], layer_o))
    for g in (g_vec, g_qkv, g_out, g_in, g_down):
        g.drain()
    for copy in swaps:
        copy.wait_send()
    half.wait_send()
    last.wait_send()
    for store in stores:
        store.wait()


def forward_all(wqkv2, w_out, win2, w_down, tile, inputs, cotangent, col, row):
    dq, do, di = wqkv2.shape[2], w_out.shape[1], win2.shape[2]
    length, depth = inputs.shape
    tokens = 2 * length
    outs = [
        ((16, 64, dq), BF), ((8, 64, do), BF), ((16, 64, di), BF), ((16,) + w_down.shape, BF),
        ((8, depth), F32), ((tokens, depth), BF), ((tokens, dq), BF), ((tokens, dq // 3), BF), ((2, length, 128), F32),
        ((tokens, depth), BF), ((tokens, depth), BF), ((tokens, di), BF), ((2, length, depth), BF),
        ((2, length, length), BF), ((16,) + w_down.shape, BF), ((length, depth), F32),
    ]
    scratch = [
        ((16, 64, dq), BF), ((16, 32, do), BF), ((8, 64, do), BF), ((16, 64, di), BF), ((16,) + w_down.shape, BF),
        ((16, 16, 128), F32), ((16, 128), F32), ((16, 128), F32), ((2, length, depth), BF), ((2, length, depth), BF),
        ((2, length, 128), jnp.int32), ((2, 8, length), jnp.int32), ((2, length, length), BF),
        ((8, depth), F32), ((8, di), F32), ((8, dq), F32), ((tokens, depth), BF), ((tokens, dq), BF),
        ((tokens, dq // 3), BF), ((2, length, 128), F32), ((tokens, depth), F32), ((tokens, depth), BF),
        ((tokens, depth), BF), ((length, depth), BF), ((tokens, depth), BF), ((tokens, depth), BF),
        ((tokens, di), BF), ((tokens, di), BF), ((16,) + w_down.shape, BF),
    ]
    return pl.pallas_call(
        forward_kernel,
        out_shape=[jax.ShapeDtypeStruct(s, d) for s, d in outs],
        in_specs=[pl.BlockSpec(memory_space=pl.ANY)] * 9,
        out_specs=[pl.BlockSpec(memory_space=pl.ANY)] * len(outs),
        scratch_shapes=[pltpu.VMEM(s, d) for s, d in scratch]
        + [
            pltpu.SemaphoreType.DMA((5, 15)),
            pltpu.SemaphoreType.DMA((5, 15)),
            pltpu.SemaphoreType.DMA((13,)),
            pltpu.SemaphoreType.DMA((13,)),
            pltpu.SemaphoreType.DMA((32,)),
        ],
        compiler_params=pltpu.CompilerParams(
            collective_id=0, has_side_effects=True, vmem_limit_bytes=67043328
        ),
        name="forward_gather",
    )(wqkv2, w_out, win2, w_down, tile, inputs, cotangent, col, row)


def attend_pair_back(i, triple, mask, lse, gatt, gtriple, sums, c):
    length = mask.shape[1]
    half = gatt.shape[1]
    pairs = half // 128
    s, pair = i // pairs, lax.rem(i, pairs)
    rows, blocks = span(s, length), span(s, length // 64)

    def at(third):
        return pl.ds(pl.multiple_of(third * half + pair * 128, 128), 128)

    q, k, v = (triple[blocks, :, at(t)].reshape(length, 128) for t in range(3))
    g = gatt[rows, at(0)]
    lane = lax.broadcasted_iota(jnp.int32, (length, 128), 1)
    low = lane < HD
    zero = jnp.zeros_like(q)
    scale = HD ** (-0.5)
    parts = []
    for h in range(2):
        mine = low if h == 0 else ~low
        scores = mm(jnp.where(mine, q, zero), k, NT) * scale + mask[s].astype(F32)
        level = jnp.sum(jnp.where(lane == pair * 2 + h, lse[s], 0.0), -1, keepdims=True)
        probs = jnp.exp(scores - level)
        grad_probs = mm(jnp.where(mine, g, zero), v, NT)
        inner = jnp.sum(probs * grad_probs, -1, keepdims=True)
        grad_scores = (probs * (grad_probs - inner)).astype(BF)
        parts.append(
            (
                mm(grad_scores, k) * scale,
                mm(grad_scores, q, TN) * scale,
                mm(probs.astype(BF), g, TN),
            )
        )
    for t in range(3):
        joined = jnp.where(low, parts[0][t], parts[1][t]).astype(BF)
        gtriple[rows, at(t)] = joined
        if t != 1:
            row = QB if t == 0 else VB
            where = pl.ds(pl.multiple_of(half * c + pair * 128, 128), 128)
            sums[row : row + 1, where] += jnp.sum(joined.astype(F32), 0, keepdims=True)


class Later:
    def __init__(self, wait):
        self.wait = wait


def backward_kernel(
    qkv_ref, out_ref, in_ref, down_ref, vecs_ref, norm1_ref, triple_ref, att_ref, lse_ref, xhat_ref, norm2_ref,
    slope_ref, cot_ref, mask_ref, gdown_ref, tok_ref,
    qkv_o, out_o, in_o, down_o, vec_o, input_o,
    b_qkv, b_out, b_in, b_down, b_vec,
    l_qkv, l_out, l_in, l_down, l_vec,
    f_qkv, f_out, f_in, f_down, f_vec, n_vec,
    w_qkv, w_out, area, area2, wide, vecs, att, lse, xhat, norm2, cot, mask, part, part_in, gmid, gmixed,
    gatt, gout, sums,
    sent, came, pair_sent, pair_came, local,
):
    p = Place()
    c = p.c
    length, depth = gmid.shape
    tokens, units = wide.shape
    half = depth // 2
    mine = pl.ds(pl.multiple_of(ROWS * c, ROWS), ROWS)
    theirs = pl.ds(pl.multiple_of(ROWS * (1 - c), ROWS), ROWS)
    slots = iter(range(local.shape[0]))

    def load(src, dst):
        slot = next(slots)
        pltpu.make_async_copy(src, dst, local.at[slot]).start()
        return Later(lambda: pltpu.make_async_copy(src, dst, local.at[slot]).wait())

    in_down = load(gdown_ref, b_down)
    first = [load(down_ref, area), load(cot_ref, cot), load(slope_ref, wide)]
    second = [load(norm2_ref, norm2), load(in_ref, area2)]
    third = [load(xhat_ref, xhat), load(lse_ref, lse), load(vecs_ref, vecs), load(att_ref, att), load(out_ref, w_out)]
    fourth = [load(mask_ref, mask), load(qkv_ref, w_qkv)]
    p.greet()
    pair = Pair(p, pair_sent, pair_came)
    s_down, s_in, s_out, s_qkv, s_vec = (
        Scatter(p, blocks, landed, sent.at[i], came.at[i])
        for i, (blocks, landed) in enumerate(
            ((b_down, l_down), (b_in, l_in), (b_out, l_out), (b_qkv, l_qkv), (b_vec, l_vec))
        )
    )
    in_down.wait()
    s_down.begin()
    stores = []

    def put(ref):
        def write(at, value):
            ref[at, :] = value

        return write

    def end_down():
        s_down.total(put(f_down))
        stores.append(load(f_down, down_o))

    def end_in():
        s_in.total(put(f_in))
        pair.copy(f_in.at[theirs], in_o.at[c], 1).start()
        stores.append(load(f_in.at[mine], in_o.at[c]))

    def end_out():
        s_out.total(put(f_out))
        stores.append(load(f_out, out_o))

    def end_qkv():
        s_qkv.total(put(f_qkv))
        pair.copy(f_qkv.at[theirs], qkv_o.at[c], 2).start()
        stores.append(load(f_qkv.at[mine], qkv_o.at[c]))

    def end_vec():
        s_vec.total(put(f_vec))
        pair.copy(f_vec, n_vec, 3).start()
        stores.append(load(f_vec, vec_o.at[0]))

    pump = Pump()
    pump.add(s_down.steps())
    sums[...] = jnp.zeros_like(sums)
    b_vec[...] = jnp.zeros_like(b_vec)
    for copy in first:
        copy.wait()

    def hidden_grad(i):
        cols = span(i, 256)
        w = area[span(i, 2)].reshape(256, depth)
        grad = mm(cot[...].reshape(tokens, depth), w, NT) * wide[:, cols].astype(F32)
        low = grad.astype(BF)
        wide[:, cols] = low
        total = jnp.sum(low.astype(F32), 0, keepdims=True)
        b_vec[2 * i, 8:9, :] = total[:, 0:128]
        b_vec[2 * i + 1, 8:9, :] = total[:, 128:256]

    pump.loop(units // 256, hidden_grad, 1)
    for copy in second:
        copy.wait()

    def in_grad(i):
        cols = span(i, 256)
        b_in[span(i, 4)] = mm(norm2[:, cols], wide[...], TN).astype(BF).reshape(4, 64, units)

    pump.loop(depth // 256, in_grad, 0)
    pump.take(len(pump.queue))
    s_in.begin()
    pump.add([end_down])
    pump.add(s_in.steps())

    def send_part(i):
        rows = span(i, 256)
        return pair.copy(part.at[rows], part_in.at[rows], 4 + i)

    def norm_grad(i):
        rows = span(i, 256)
        part[rows, :] = mm(wide[rows, :], area2[...].reshape(depth, units), NT).astype(BF)
        send_part(i).start()

    pump.loop(4, norm_grad, 1)
    norm1_in = load(norm1_ref, area.at[0:8])
    tok_in = load(tok_ref, area.at[8:12])
    triple_in = load(triple_ref, area2.at[:, :, 0 : 3 * half])
    for copy in third:
        copy.wait()

    def middle_rows(i, ours):
        s = c if ours else 1 - c
        inside = span(i, 128)
        rows = pl.ds(pl.multiple_of(s * length + i * 128, 128), 128)
        grad = part[rows, :].astype(F32) + part_in[rows, :].astype(F32)
        normed = xhat[rows, :].astype(F32)
        scaled = grad * vecs[G2 : G2 + 1, :]
        top = cot[s, inside, :].astype(F32)
        middle = top + lse[s, inside, INV_AT : INV_AT + 1] * (
            scaled
            - jnp.mean(scaled, -1, keepdims=True)
            - normed * jnp.mean(scaled * normed, -1, keepdims=True)
        )
        low = middle.astype(BF)
        gmixed[rows, :] = low
        if ours:
            gmid[inside, :] = middle
            sums[G2 : G2 + 1, :] += jnp.sum(grad * normed, 0, keepdims=True)
            sums[B2 : B2 + 1, :] += jnp.sum(grad, 0, keepdims=True)
            sums[OB : OB + 1, :] += jnp.sum(low.astype(F32), 0, keepdims=True)
            sums[DB : DB + 1, :] += jnp.sum(top, 0, keepdims=True)

    for i in range(4):
        send_part(i).wait_recv()
    pump.loop(length // 128, functools.partial(middle_rows, ours=True), 0)
    pump.loop(length // 128, functools.partial(middle_rows, ours=False), 0)

    def out_grad(i):
        cols = span(i, 256)
        gout[span(i, 4)] = mm(att[:, cols], gmixed[...], TN).astype(BF).reshape(4, 64, depth)

    pump.loop(half // 256, out_grad, 1)
    keep = load(gout.at[:, mine], b_out.at[pl.ds(8 * c, 8)])
    mate = pair.copy(gout.at[:, theirs], b_out.at[pl.ds(8 * c, 8)], 0)
    mate.start()

    def att_grad(i):
        rows = span(i, 512)
        gatt[rows, :] = mm(gmixed[rows, :], w_out[...].reshape(half, depth), NT).astype(BF)

    pump.loop(2, att_grad, 1)
    keep.wait()
    mate.wait_recv()
    s_out.begin()
    pump.add([end_in])
    pump.add(s_out.steps())
    triple_in.wait()
    for copy in fourth:
        copy.wait()
    pump.loop(
        8,
        functools.partial(
            attend_pair_back, triple=area2, mask=mask, lse=lse, gatt=gatt, gtriple=wide, sums=sums, c=c
        ),
        2,
    )
    norm1_in.wait()

    def qkv_grad(i):
        cols = span(i, 256)
        normed = area[0:8, :, cols].reshape(tokens, 256)
        b_qkv[span(i, 4)] = mm(normed, wide[:, 0 : 3 * half], TN).astype(BF).reshape(4, 64, 3 * half)

    pump.loop(depth // 256, qkv_grad, 0)
    s_qkv.begin()
    pump.add([end_out])
    pump.add(s_qkv.steps())
    for i in range(4):
        send_part(i).wait_send()

    def input_grad(i, s):
        rows = pl.ds(pl.multiple_of(s * length + i * 128, 128), 128)
        return mm(wide[rows, 0 : 3 * half], w_qkv[...].reshape(depth, 3 * half), NT)

    def first_theirs(i):
        part[span(i, 128), :] = input_grad(i, 1 - c).astype(BF)

    pump.loop(length // 128, first_theirs, 1)
    last = pair.copy(part.at[0:length], part_in.at[0:length], 8)
    last.start()
    tok_in.wait()

    def first_ours(i):
        inside = span(i, 128)
        grad = input_grad(i, c) + part_in[inside, :].astype(F32)
        normed, inverse = stats(area[8 + i, :, :].astype(F32))
        scaled = grad * vecs[G1 : G1 + 1, :]
        gmid[inside, :] = gmid[inside, :] + inverse * (
            scaled
            - jnp.mean(scaled, -1, keepdims=True)
            - normed * jnp.mean(scaled * normed, -1, keepdims=True)
        )
        sums[G1 : G1 + 1, :] += jnp.sum(grad * normed, 0, keepdims=True)
        sums[B1 : B1 + 1, :] += jnp.sum(grad, 0, keepdims=True)

    last.wait_recv()
    pump.loop(length // 128, first_ours, 1)
    stores.append(load(gmid, input_o))
    for w in range(8):
        for k in range(2):
            b_vec[2 * w + k, 0:8, :] = sums[:, 128 * w : 128 * (w + 1)]
    s_vec.begin()
    rest, pump.queue = pump.queue, []
    pump.add(rest)
    pump.add(s_vec.steps())
    pump.add([end_qkv, end_vec])
    pump.take(len(pump.queue))
    pair.copy(f_vec, n_vec, 3).wait_recv()
    stores.append(load(n_vec, vec_o.at[1]))
    for s in (s_down, s_in, s_out, s_qkv, s_vec):
        s.drain()
    mate.wait_send()
    last.wait_send()
    pair.copy(f_vec, n_vec, 3).wait_send()
    pair.copy(f_in.at[theirs], in_o.at[c], 1).wait()
    pair.copy(f_qkv.at[theirs], qkv_o.at[c], 2).wait()
    for store in stores:
        store.wait()


def backward_all(saved, inputs):
    (
        qkv, w_out, w_in, w_down, vecs, norm1, triple, att, lse, xhat, norm2, slope, cot, mask, gdown,
    ) = saved
    length, depth = inputs.shape
    tokens = 2 * length
    dq, do, di = qkv.shape[2], w_out.shape[2], w_in.shape[2]
    down, dd = w_down.shape[1:]
    outs = [
        ((2, 32, dq), F32), ((32, do), F32), ((2, 32, di), F32), ((down, dd), F32), ((2, 16, 128), F32),
        ((length, depth), F32),
    ]
    blocks = [((64, dq), BF), ((32, do), BF), ((64, di), BF), ((down, dd), BF), ((16, 128), F32)]
    scratch = [((16,) + s, d) for s, d in blocks] + [((15,) + s, d) for s, d in blocks] + [(s, F32) for s, d in blocks]
    scratch += [
        ((16, 128), F32), (qkv.shape, BF), (w_out.shape, BF), (w_down.shape, BF), (w_in.shape, BF), (slope.shape, BF),
        (vecs.shape, F32), (att.shape, BF), (lse.shape, F32), (xhat.shape, BF), (norm2.shape, BF),
        (cot.shape, BF), (mask.shape, mask.dtype), ((tokens, depth), BF), ((tokens, depth), BF),
        ((length, depth), F32), ((tokens, depth), BF), ((tokens, depth // 2), BF), (w_out.shape, BF), ((8, depth), F32),
    ]
    args = (
        qkv, w_out, w_in, w_down, vecs, norm1.reshape(8, 128, depth), triple.reshape(16, 64, dq), att, lse, xhat,
        norm2, slope, cot, mask, gdown, inputs.reshape(4, 128, depth),
    )
    return pl.pallas_call(
        backward_kernel,
        out_shape=[jax.ShapeDtypeStruct(s, d) for s, d in outs],
        in_specs=[pl.BlockSpec(memory_space=pl.ANY)] * len(args),
        out_specs=[pl.BlockSpec(memory_space=pl.ANY)] * len(outs),
        scratch_shapes=[pltpu.VMEM(s, d) for s, d in scratch]
        + [
            pltpu.SemaphoreType.DMA((5, 15)),
            pltpu.SemaphoreType.DMA((5, 15)),
            pltpu.SemaphoreType.DMA((9,)),
            pltpu.SemaphoreType.DMA((9,)),
            pltpu.SemaphoreType.DMA((28,)),
        ],
        compiler_params=pltpu.CompilerParams(
            collective_id=1, has_side_effects=True, vmem_limit_bytes=67043328
        ),
        name="backward_scatter",
    )(*args)

def local_split(
    inputs, segment_ids, cotangent, ln1_gain, ln1_shift, w_qkv, query_bias, value_bias, w_out, out_bias,
    ln2_gain, ln2_shift, w_in, in_bias, w_down, down_bias,
):
    c = lax.axis_index("c")
    narrow = lax.axis_index("x") * 2 + c
    length, d_model = inputs.shape
    rows = ln1_gain.shape[0]
    half = d_model // 2
    small = jnp.stack(
        [ln1_gain, ln1_shift, query_bias, value_bias, out_bias, ln2_gain, ln2_shift, down_bias]
    ).astype(F32)
    quarter = jnp.arange(4)[None, :, None] == narrow
    tile = jnp.where(quarter, small[:, None, :], 0.0).reshape(8, 128)
    tile = jnp.concatenate([tile, in_bias.astype(F32)[None], jnp.zeros((7, 128), F32)])
    wqkv2 = w_qkv.reshape(rows, 3, 2, half).transpose(2, 0, 1, 3).reshape(2, rows, -1)
    win2 = w_in.reshape(rows, 16, 2, 128).transpose(2, 0, 1, 3).reshape(2, rows, -1)
    col = jnp.broadcast_to(segment_ids[:, None], (length, 128))
    row = jnp.broadcast_to(segment_ids[None, :], (8, length))
    *saved, layer_out = forward_all(wqkv2, w_out, win2, w_down, tile, inputs, cotangent, col, row)
    d_qkv, d_out, d_in, d_down, d_vec, grad_input = backward_all(saved, inputs)
    d_qkv = d_qkv.reshape(2, rows, 3, half).transpose(1, 2, 0, 3).reshape(rows, -1)
    d_in = d_in.reshape(2, rows, 16, 128).transpose(1, 2, 0, 3).reshape(rows, -1)
    eight = (d_vec[0, :8] + d_vec[1, :8]).reshape(8, 4, 32)
    eight = lax.dynamic_index_in_dim(eight, narrow, 1, False)
    return (
        layer_out, grad_input, eight[0], eight[1], d_qkv, eight[2], eight[3], d_out, eight[4],
        eight[5], eight[6], d_in, d_vec[0, 8], d_down, eight[7],
    )


def solution(mesh):
    sizes = tuple(mesh.shape.values())
    step, names = local, (("wide", "narrow"),)
    if sizes == (8, 4):
        mesh = Mesh(mesh.devices.reshape(4, 2, 2, 2), ("z", "y", "x", "c"))
        step, names = local_split, (("z", "y", "x", "c"),)
    line, plane = P(names[0]), P(names[0], None)
    return jax.shard_map(
        step,
        mesh=mesh,
        in_specs=(plane, line, plane, line, line, plane, line, line, plane, line, line, line, plane, line, plane, line),
        out_specs=(plane, plane, line, line, plane, line, line, plane, line, line, line, plane, line, plane, line),
        check_vma=False,
    )
```

```python
import functools

import jax
import jax.numpy as jnp
from jax import lax
from jax.experimental import pallas as pl
from jax.experimental.pallas import tpu as pltpu
from jax.sharding import Mesh
from jax.sharding import PartitionSpec as P

HD = 64


EPS = 1e-05
ROOT_HALF = 0.7071067811865476
INV_ROOT_TAU = 0.3989422804014327
NEG_FILL = -1000000000.0


def normalize(values, gain, shift):
    average = jnp.mean(values, -1, keepdims=True)
    centred = values - average
    inverse = lax.rsqrt(jnp.mean(centred * centred, -1, keepdims=True) + EPS)
    normed = centred * inverse
    return (normed * gain + shift, normed, inverse)


def normalize_back(grad_norm, normed, inverse, gain):
    scaled = grad_norm * gain
    return inverse * (
        scaled
        - jnp.mean(scaled, -1, keepdims=True)
        - normed * jnp.mean(scaled * normed, -1, keepdims=True)
    )


def gelu_value(pre_act):
    return 0.5 * pre_act * (1.0 + lax.erf(pre_act * ROOT_HALF))


def gelu_slope(pre_act):
    return (
        0.5 * (1.0 + lax.erf(pre_act * ROOT_HALF))
        + pre_act * jnp.exp(-0.5 * pre_act * pre_act) * INV_ROOT_TAU
    )


def gather_forward(shards):
    return (
        lax.all_gather(shards[0], ("wide", "narrow"), axis=0, tiled=True),
        lax.all_gather(shards[1], ("wide", "narrow"), axis=0, tiled=True),
        lax.all_gather(shards[2], ("wide", "narrow"), axis=0, tiled=True),
        lax.all_gather(shards[3], ("wide", "narrow"), axis=0, tiled=True),
        lax.all_gather(shards[4], ("wide", "narrow"), axis=0, tiled=True),
        lax.all_gather(shards[5], ("wide", "narrow"), axis=0, tiled=True),
        lax.all_gather(shards[6], ("wide", "narrow"), axis=0, tiled=True),
        lax.all_gather(shards[7], ("wide", "narrow"), axis=0, tiled=True),
        lax.all_gather(shards[8], ("wide", "narrow"), axis=0, tiled=True),
        lax.all_gather(shards[9], ("wide", "narrow"), axis=0, tiled=True),
        lax.all_gather(shards[10], ("wide", "narrow"), axis=0, tiled=True),
        lax.all_gather(shards[11], ("wide", "narrow"), axis=0, tiled=True),
        lax.all_gather(shards[12], ("wide", "narrow"), axis=0, tiled=True),
    )


def gather_backward(shards):
    return (
        lax.all_gather(shards[0], ("wide", "narrow"), axis=0, tiled=True),
        lax.all_gather(shards[1], ("wide", "narrow"), axis=0, tiled=True),
        lax.all_gather(shards[2], ("wide", "narrow"), axis=0, tiled=True),
        lax.all_gather(shards[3], ("wide", "narrow"), axis=0, tiled=True),
        lax.all_gather(shards[4], ("wide", "narrow"), axis=0, tiled=True),
        lax.all_gather(shards[5], ("wide", "narrow"), axis=0, tiled=True),
        lax.all_gather(shards[6], ("wide", "narrow"), axis=0, tiled=True),
        lax.all_gather(shards[7], ("wide", "narrow"), axis=0, tiled=True),
        lax.all_gather(shards[8], ("wide", "narrow"), axis=0, tiled=True),
        lax.all_gather(shards[9], ("wide", "narrow"), axis=0, tiled=True),
        lax.all_gather(shards[10], ("wide", "narrow"), axis=0, tiled=True),
        lax.all_gather(shards[11], ("wide", "narrow"), axis=0, tiled=True),
        lax.all_gather(shards[12], ("wide", "narrow"), axis=0, tiled=True),
    )


def reduce_grads(grads):
    return (
        lax.psum_scatter(grads[0], ("wide", "narrow"), scatter_dimension=0, tiled=True),
        lax.psum_scatter(grads[1], ("wide", "narrow"), scatter_dimension=0, tiled=True),
        lax.psum_scatter(grads[2], ("wide", "narrow"), scatter_dimension=0, tiled=True),
        lax.psum_scatter(grads[3], ("wide", "narrow"), scatter_dimension=0, tiled=True),
        lax.psum_scatter(grads[4], ("wide", "narrow"), scatter_dimension=0, tiled=True),
        lax.psum_scatter(grads[5], ("wide", "narrow"), scatter_dimension=0, tiled=True),
        lax.psum_scatter(grads[6], ("wide", "narrow"), scatter_dimension=0, tiled=True),
        lax.psum_scatter(grads[7], ("wide", "narrow"), scatter_dimension=0, tiled=True),
        lax.psum_scatter(grads[8], ("wide", "narrow"), scatter_dimension=0, tiled=True),
        lax.psum_scatter(grads[9], ("wide", "narrow"), scatter_dimension=0, tiled=True),
        lax.psum_scatter(grads[10], ("wide", "narrow"), scatter_dimension=0, tiled=True),
        lax.psum_scatter(grads[11], ("wide", "narrow"), scatter_dimension=0, tiled=True),
        lax.psum_scatter(grads[12], ("wide", "narrow"), scatter_dimension=0, tiled=True),
    )


def head_block(triple_b, offset, group_width, d_model):
    length = triple_b.shape[0]
    queries = triple_b[:, offset : offset + group_width].reshape(length, group_width // HD, HD)
    key_rows = triple_b[:, d_model + offset : d_model + offset + group_width].reshape(
        length, group_width // HD, HD
    )
    values = triple_b[:, 2 * d_model + offset : 2 * d_model + offset + group_width].reshape(
        length, group_width // HD, HD
    )
    return (queries, key_rows, values)


def block_scores(queries, key_rows, allowed):
    scores = jnp.einsum(
        "qhd,khd->hqk", queries, key_rows, preferred_element_type=jnp.float32
    ) * HD ** (-0.5)
    return jnp.where(allowed[None], scores, NEG_FILL)


def attend(triple_b, allowed, d_model):
    length = triple_b.shape[0]
    group_width = 4 * HD
    pieces = []
    log_totals = []
    for offset in range(0, d_model, group_width):
        queries, key_rows, values = head_block(triple_b, offset, group_width, d_model)
        scores = block_scores(queries, key_rows, allowed)
        highest = jnp.max(scores, -1, keepdims=True)
        exponent = jnp.exp(scores - highest)
        row_total = jnp.sum(exponent, -1, keepdims=True)
        probs_low = (exponent / row_total).astype(jnp.bfloat16)
        mixed = jnp.einsum("hqk,khd->qhd", probs_low, values, preferred_element_type=jnp.float32)
        pieces.append(mixed.reshape(length, group_width))
        log_totals.append(highest + jnp.log(row_total))
    return (jnp.concatenate(pieces, 1), log_totals)


def attend_back(triple_b, grad_att_b, allowed, log_totals, d_model):
    length = triple_b.shape[0]
    group_width = 4 * HD
    query_parts = []
    key_parts = []
    value_parts = []
    for index, offset in enumerate(range(0, d_model, group_width)):
        queries, key_rows, values = head_block(triple_b, offset, group_width, d_model)
        scores = block_scores(queries, key_rows, allowed)
        attn_probs = jnp.exp(scores - log_totals[index])
        probs_low = attn_probs.astype(jnp.bfloat16)
        grad_heads = grad_att_b[:, offset : offset + group_width].reshape(
            length, group_width // HD, HD
        )
        grad_probs = jnp.einsum(
            "qhd,khd->hqk", grad_heads, values, preferred_element_type=jnp.float32
        )
        inner_sum = jnp.sum(attn_probs * grad_probs, -1, keepdims=True)
        grad_scores = (attn_probs * (grad_probs - inner_sum)).astype(jnp.bfloat16)
        grad_query = jnp.einsum(
            "hqk,khd->qhd", grad_scores, key_rows, preferred_element_type=jnp.float32
        ) * HD ** (-0.5)
        grad_key = jnp.einsum(
            "hqk,qhd->khd", grad_scores, queries, preferred_element_type=jnp.float32
        ) * HD ** (-0.5)
        grad_value = jnp.einsum(
            "hqk,qhd->khd", probs_low, grad_heads, preferred_element_type=jnp.float32
        )
        query_parts.append(grad_query.reshape(length, group_width))
        key_parts.append(grad_key.reshape(length, group_width))
        value_parts.append(grad_value.reshape(length, group_width))
    return jnp.concatenate(query_parts + key_parts + value_parts, 1).astype(jnp.bfloat16)


def local(
    inputs,
    segment_ids,
    cotangent,
    ln1_gain,
    ln1_shift,
    w_qkv,
    query_bias,
    value_bias,
    w_out,
    out_bias,
    ln2_gain,
    ln2_shift,
    w_in,
    in_bias,
    w_down,
    down_bias,
):
    shards = (
        ln1_gain,
        ln1_shift,
        w_qkv,
        query_bias,
        value_bias,
        w_out,
        out_bias,
        ln2_gain,
        ln2_shift,
        w_in,
        in_bias,
        w_down,
        down_bias,
    )
    fwd_weights = gather_forward(shards)
    (
        gain_one,
        shift_one,
        qkv_full,
        qbias_full,
        vbias_full,
        outw_full,
        outb_full,
        gain_two,
        shift_two,
        inw_full,
        inb_full,
        downw_full,
        downb_full,
    ) = fwd_weights
    d_model = inputs.shape[1]
    length = inputs.shape[0]
    tokens = inputs.astype(jnp.float32)
    position = jnp.arange(length, dtype=jnp.int32)
    allowed = (segment_ids[:, None] == segment_ids[None, :]) & (segment_ids[:, None] >= 0) | (
        position[:, None] == position[None, :]
    )
    normed_out, normed_one, inverse_one = normalize(
        tokens, gain_one.astype(jnp.float32), shift_one.astype(jnp.float32)
    )
    norm_one = normed_out.astype(jnp.bfloat16)
    shifts = jnp.concatenate(
        [
            qbias_full.astype(jnp.float32),
            jnp.zeros((d_model,), jnp.float32),
            vbias_full.astype(jnp.float32),
        ]
    )
    triple_b = (jnp.dot(norm_one, qkv_full, preferred_element_type=jnp.float32) + shifts).astype(
        jnp.bfloat16
    )
    attended_f, log_totals = attend(triple_b, allowed, d_model)
    attended = attended_f.astype(jnp.bfloat16)
    middle = (
        tokens
        + jnp.dot(attended, outw_full, preferred_element_type=jnp.float32)
        + outb_full.astype(jnp.float32)
    )
    normed_out_two, normed_two, inverse_two = normalize(
        middle, gain_two.astype(jnp.float32), shift_two.astype(jnp.float32)
    )
    norm_two = normed_out_two.astype(jnp.bfloat16)
    pre_act = jnp.dot(norm_two, inw_full, preferred_element_type=jnp.float32) + inb_full.astype(
        jnp.float32
    )
    hidden = gelu_value(pre_act).astype(jnp.bfloat16)
    layer_out = (
        middle
        + jnp.dot(hidden, downw_full, preferred_element_type=jnp.float32)
        + downb_full.astype(jnp.float32)
    )
    back_weights = gather_backward(shards)
    (
        gain_one_b,
        shift_one_b,
        qkv_back,
        qbias_back,
        vbias_back,
        outw_back,
        outb_back,
        gain_two_b,
        shift_two_b,
        inw_back,
        inb_back,
        downw_back,
        downb_back,
    ) = back_weights
    grad_top = cotangent.astype(jnp.float32)
    grad_w_down = jnp.einsum("sf,sd->fd", hidden, cotangent, preferred_element_type=jnp.float32)
    grad_down_bias = jnp.sum(grad_top, 0)
    grad_hidden = jnp.einsum("sd,fd->sf", cotangent, downw_back, preferred_element_type=jnp.float32)
    grad_pre = (grad_hidden * gelu_slope(pre_act)).astype(jnp.bfloat16)
    grad_w_in = jnp.einsum("sd,sf->df", norm_two, grad_pre, preferred_element_type=jnp.float32)
    grad_in_bias = jnp.sum(grad_pre.astype(jnp.float32), 0)
    grad_norm_two = jnp.einsum("sf,df->sd", grad_pre, inw_back, preferred_element_type=jnp.float32)
    grad_ln2_gain = jnp.sum(grad_norm_two * normed_two, 0)
    grad_ln2_shift = jnp.sum(grad_norm_two, 0)
    grad_middle = grad_top + normalize_back(
        grad_norm_two, normed_two, inverse_two, gain_two_b.astype(jnp.float32)
    )
    grad_mixed = grad_middle.astype(jnp.bfloat16)
    grad_w_out = jnp.einsum("sd,se->de", attended, grad_mixed, preferred_element_type=jnp.float32)
    grad_out_bias = jnp.sum(grad_mixed.astype(jnp.float32), 0)
    grad_attended = jnp.einsum(
        "se,de->sd", grad_mixed, outw_back, preferred_element_type=jnp.float32
    ).astype(jnp.bfloat16)
    grad_triple = attend_back(triple_b, grad_attended, allowed, log_totals, d_model)
    grad_w_qkv = jnp.einsum("sd,st->dt", norm_one, grad_triple, preferred_element_type=jnp.float32)
    grad_query_bias = jnp.sum(grad_triple[:, :d_model].astype(jnp.float32), 0)
    grad_value_bias = jnp.sum(grad_triple[:, 2 * d_model :].astype(jnp.float32), 0)
    grad_norm_one = jnp.einsum(
        "st,dt->sd", grad_triple, qkv_back, preferred_element_type=jnp.float32
    )
    grad_ln1_gain = jnp.sum(grad_norm_one * normed_one, 0)
    grad_ln1_shift = jnp.sum(grad_norm_one, 0)
    grad_input = grad_middle + normalize_back(
        grad_norm_one, normed_one, inverse_one, gain_one_b.astype(jnp.float32)
    )
    owned = reduce_grads(
        (
            grad_ln1_gain,
            grad_ln1_shift,
            grad_w_qkv,
            grad_query_bias,
            grad_value_bias,
            grad_w_out,
            grad_out_bias,
            grad_ln2_gain,
            grad_ln2_shift,
            grad_w_in,
            grad_in_bias,
            grad_w_down,
            grad_down_bias,
        )
    )
    return (
        layer_out,
        grad_input,
        owned[0],
        owned[1],
        owned[2],
        owned[3],
        owned[4],
        owned[5],
        owned[6],
        owned[7],
        owned[8],
        owned[9],
        owned[10],
        owned[11],
        owned[12],
    )


MESH_ID = pl.DeviceIdType.MESH
ROWS = 32
BF, F32 = jnp.bfloat16, jnp.float32


class Place:
    def __init__(self):
        self.z = lax.axis_index("z")
        self.y = lax.axis_index("y")
        self.x = lax.axis_index("x")
        self.c = lax.axis_index("c")

    def chip(self, dz=0, dy=0, dx=0):
        z = self.z
        if dz == 2:
            z = lax.rem(z + 2, 4)
        elif dz == 1:
            z = z + 1 - 2 * lax.rem(z, 2)
        elif dz == 3:
            z = 3 - z
        y = 1 - self.y if dy else self.y
        x = 1 - self.x if dx else self.x
        return z, y, x

    def index(self, dz=0, dy=0, dx=0):
        z, y, x = self.chip(dz, dy, dx)
        return (z * 2 + y) * 2 + x

    def device(self, dz=0, dy=0, dx=0):
        z, y, x = self.chip(dz, dy, dx)
        return {"z": z, "y": y, "x": x, "c": self.c}

    def partner(self):
        return {"z": self.z, "y": self.y, "x": self.x, "c": 1 - self.c}

    def greet(self):
        barrier = pltpu.get_barrier_semaphore()
        peers = [self.device(dz=1), self.device(dz=2), self.device(dz=3)]
        peers += [self.device(dy=1), self.device(dx=1), self.partner()]
        for peer in peers:
            pl.semaphore_signal(barrier, inc=1, device_id=peer, device_id_type=MESH_ID)
        pl.semaphore_wait(barrier, len(peers))


class Pair:
    def __init__(self, place, sent, came):
        self.p, self.sent, self.came = place, sent, came

    def copy(self, src, dst, slot):
        return pltpu.make_async_remote_copy(
            src_ref=src,
            dst_ref=dst,
            send_sem=self.sent.at[slot],
            recv_sem=self.came.at[slot],
            device_id=self.p.partner(),
            device_id_type=MESH_ID,
        )


Z_AT, X_AT, Y_AT, D_AT = -1, 3, 7, 11
FAR_FIRST, BY_Y = (3, 2, 1, 0), (3, 1)


class Gather:
    def __init__(self, place, blocks, sent, came):
        self.p, self.blocks, self.sent, self.came = place, blocks, sent, came
        self.left = []

    def copy(self, block, slot, to):
        at = self.p.index(**block)
        return pltpu.make_async_remote_copy(
            src_ref=self.blocks.at[at],
            dst_ref=self.blocks.at[at],
            send_sem=self.sent.at[slot],
            recv_sem=self.came.at[slot],
            device_id=self.p.device(**to),
            device_id_type=MESH_ID,
        )

    def send(self, block, slot, to):
        self.copy(block, slot, to).start()
        self.left.append((block, slot, to))

    def wait(self, block, slot):
        self.copy(block, slot, dict(dx=1)).wait_recv()

    def begin(self):
        for dz in (1, 2, 3):
            self.send({}, Z_AT + dz, dict(dz=dz))
        self.send({}, X_AT, dict(dx=1))
        self.send({}, Y_AT, dict(dy=1))

    def along(self, dz):
        self.wait(dict(dz=dz), Z_AT + dz)
        self.send(dict(dz=dz), X_AT + dz, dict(dx=1))
        self.send(dict(dz=dz), Y_AT + dz, dict(dy=1))

    def across(self, dz):
        if dz < 2:
            self.wait(dict(dz=dz, dx=1), X_AT + dz)
            self.send(dict(dz=dz, dx=1), D_AT + dz, dict(dy=1))
        else:
            self.wait(dict(dz=dz, dy=1), Y_AT + dz)
            self.send(dict(dz=dz, dy=1), D_AT + dz, dict(dx=1))

    def finish(self):
        for dz in range(4):
            if dz < 2:
                self.wait(dict(dz=dz, dy=1), Y_AT + dz)
            else:
                self.wait(dict(dz=dz, dx=1), X_AT + dz)
        for dz in range(4):
            self.wait(dict(dz=dz, dy=1, dx=1), D_AT + dz)

    def steps(self):
        for dz in (1, 2, 3):
            yield functools.partial(self.along, dz)
        for dz in (0, 1, 2, 3):
            yield functools.partial(self.across, dz)

    def drain(self):
        for block, slot, to in self.left:
            self.copy(block, slot, to).wait_send()


class Scatter:
    def __init__(self, place, blocks, landed, sent, came):
        self.p, self.blocks, self.landed = place, blocks, landed
        self.sent, self.came = sent, came
        self.left = []

    def copy(self, block, slot, to):
        return pltpu.make_async_remote_copy(
            src_ref=self.blocks.at[self.p.index(**block)],
            dst_ref=self.landed.at[slot],
            send_sem=self.sent.at[slot],
            recv_sem=self.came.at[slot],
            device_id=self.p.device(**to),
            device_id_type=MESH_ID,
        )

    def send(self, block, slot, to):
        self.copy(block, slot, to).start()
        self.left.append((block, slot, to))

    def wait(self, slot):
        self.copy({}, slot, dict(dx=1)).wait_recv()

    def add(self, at, slots, write):
        rows = self.blocks.shape[1]
        step = 16

        def body(i, carry):
            some = pl.ds(pl.multiple_of(i * step, step), step)
            total = self.blocks[at, some, :].astype(F32)
            for slot in slots:
                total = total + self.landed[slot, some, :].astype(F32)
            write(some, total)
            return carry

        lax.fori_loop(0, rows // step, body, 0)

    def merge(self, block, slots):
        at = self.p.index(**block)

        def write(some, total):
            self.blocks[at, some, :] = total.astype(self.blocks.dtype)

        self.add(at, slots, write)

    def begin(self):
        for dz in FAR_FIRST:
            to = dict(dy=1) if dz in BY_Y else dict(dx=1)
            self.send(dict(dz=dz, dy=1, dx=1), D_AT + dz, to)
            self.send(dict(dz=dz, **to), (Y_AT if dz in BY_Y else X_AT) + dz, to)

    def across(self, dz):
        to = dict(dx=1) if dz in BY_Y else dict(dy=1)
        self.wait(D_AT + dz)
        self.merge(dict(dz=dz, **to), (D_AT + dz,))
        self.send(dict(dz=dz, **to), (X_AT if dz in BY_Y else Y_AT) + dz, to)

    def along(self, dz):
        self.wait(X_AT + dz)
        self.wait(Y_AT + dz)
        if dz:
            self.merge(dict(dz=dz), (X_AT + dz, Y_AT + dz))
            self.send(dict(dz=dz), Z_AT + dz, dict(dz=dz))

    def total(self, write):
        for dz in (1, 2, 3):
            self.wait(Z_AT + dz)
        self.add(self.p.index(), (X_AT, Y_AT, Z_AT + 1, Z_AT + 2, Z_AT + 3), write)

    def acrosses(self):
        return [functools.partial(self.across, dz) for dz in FAR_FIRST]

    def alongs(self):
        return [functools.partial(self.along, dz) for dz in FAR_FIRST]

    def drain(self):
        for block, slot, to in self.left:
            self.copy(block, slot, to).wait_send()


class Pump:
    def __init__(self):
        self.queue = []

    def add(self, steps):
        self.queue.extend(steps)

    def take(self, count):
        now, self.queue = self.queue[:count], self.queue[count:]
        for step in now:
            step()

    def loop(self, trips, body, per_trip=0):
        groups = []
        for i in range(trips):
            groups.append(self.queue[:per_trip])
            self.queue = self.queue[per_trip:]

        def trip(i, carry):
            body(i)
            for k, group in enumerate(groups):
                if group:

                    @pl.when(i == k)
                    def _(group=group):
                        for step in group:
                            step()

            return carry

        lax.fori_loop(0, trips, trip, 0)


NN = (((1,), (0,)), ((), ()))
NT = (((1,), (1,)), ((), ()))
TN = (((0,), (0,)), ((), ()))


def mm(a, b, dims=NN):
    return lax.dot_general(a, b, dims, preferred_element_type=F32)


def span(i, size):
    if isinstance(i, int):
        return pl.ds(i * size, size)
    return pl.ds(pl.multiple_of(i * size, size), size)


def stats(v):
    average = jnp.mean(v, -1, keepdims=True)
    centred = v - average
    inverse = lax.rsqrt(jnp.mean(centred * centred, -1, keepdims=True) + EPS)
    return centred * inverse, inverse


def build_mask(mask, seg_col, seg_row):
    size = mask.shape[1]
    for s in range(2):

        def body(i, carry, s=s):
            rows = span(i, 128)
            col = seg_col[s, rows, :][:, :1]
            row = seg_row[s, :1, :]
            here = lax.broadcasted_iota(jnp.int32, (128, size), 0) + i * 128
            there = lax.broadcasted_iota(jnp.int32, (128, size), 1)
            fine = ((col == row) & (col >= 0)) | (here == there)
            mask[s, rows, :] = jnp.where(fine, 0.0, NEG_FILL).astype(BF)
            return carry

        lax.fori_loop(0, size // 128, body, 0)


def build_vectors(vecs, hidden_shift, triple_shift, tiles, c):
    for w in range(8):
        vecs[0:8, 128 * w : 128 * (w + 1)] = tiles[2 * w, 0:8, :] + tiles[2 * w + 1, 0:8, :]
    for j in range(16):
        hidden_shift[0:1, 128 * j : 128 * (j + 1)] = tiles[j, 8:9, :]
    half = vecs.shape[1] // 2
    first = c == 0
    triple_shift[0:1, 0:half] = jnp.where(first, vecs[2:3, 0:half], vecs[2:3, half:])
    triple_shift[0:1, half : 2 * half] = jnp.zeros((1, half), F32)
    triple_shift[0:1, 2 * half :] = jnp.where(first, vecs[3:4, 0:half], vecs[3:4, half:])


G1, B1, QB, VB, OB, G2, B2, DB = range(8)
INV_AT = 64


def attend_pair(i, triple, mask, attended, lse):
    length = mask.shape[1]
    half = attended.shape[1]
    pairs = half // 128
    s, pair = i // pairs, lax.rem(i, pairs)
    rows = span(s, length)
    q = triple[rows, pl.ds(pl.multiple_of(pair * 128, 128), 128)]
    k = triple[rows, pl.ds(pl.multiple_of(half + pair * 128, 128), 128)]
    v = triple[rows, pl.ds(pl.multiple_of(2 * half + pair * 128, 128), 128)]
    lane = lax.broadcasted_iota(jnp.int32, (length, 128), 1)
    low = lane < HD
    outs = []
    kept = lse[s]
    for h in range(2):
        mine = low if h == 0 else ~low
        scores = mm(jnp.where(mine, q, jnp.zeros_like(q)), k, NT) * HD ** (-0.5) + mask[s].astype(F32)
        highest = jnp.max(scores, -1, keepdims=True)
        exponent = jnp.exp(scores - highest)
        total = jnp.sum(exponent, -1, keepdims=True)
        probs = (exponent * (1.0 / total)).astype(BF)
        outs.append(mm(probs, v))
        kept = jnp.where(lane == pair * 2 + h, highest + jnp.log(total), kept)
    lse[s] = kept
    attended[rows, pl.ds(pl.multiple_of(pair * 128, 128), 128)] = jnp.where(low, outs[0], outs[1]).astype(BF)


def forward_kernel(
    wqkv_ref, wout_ref, win_ref, wdown_ref, tile_ref, tok_ref, cot_ref, col_ref, row_ref,
    qkv_o, out_o, in_o, down_o, vecs_o, norm1_o, triple_o, att_o, lse_o, xhat_o, norm2_o, slope_o, cot_o,
    mask_o, gdown_o, hidden_o, mid_o,
    w_qkv, w_nat, w_out, w_in, w_down, tiles, tile, tile_in, tok, cot, col, row, mask,
    vecs, hshift, tshift, norm1, triple, att, lse, mid, part, part_in, norm2, xhat, hidden, slope, gdown,
    sent, came, pair_sent, pair_came, local,
):
    p = Place()
    own, c = p.index(), p.c
    length = tok.shape[1]
    mine = pl.ds(pl.multiple_of(ROWS * c, ROWS), ROWS)
    slots = iter(range(local.shape[0]))

    def load(src, dst):
        copy = pltpu.make_async_copy(src, dst, local.at[next(slots)])
        copy.start()
        return copy

    loads = [
        load(wqkv_ref.at[c], w_qkv.at[own, mine]),
        load(wout_ref, w_nat.at[own]),
        load(win_ref.at[c], w_in.at[own, mine]),
        load(wdown_ref, w_down.at[own]),
        load(tile_ref, tile),
        load(tok_ref, tok.at[c]),
        load(cot_ref, cot.at[c]),
        load(col_ref, col.at[c]),
        load(row_ref, row.at[c]),
    ]
    p.greet()
    pair = Pair(p, pair_sent, pair_came)
    swaps = [
        pair.copy(tile_ref, tile_in, 0),
        pair.copy(wqkv_ref.at[1 - c], w_qkv.at[own, mine], 1),
        pair.copy(win_ref.at[1 - c], w_in.at[own, mine], 2),
        pair.copy(row_ref, row.at[c], 3),
        pair.copy(col_ref, col.at[c], 4),
        pair.copy(tok_ref, tok.at[c], 5),
        pair.copy(cot_ref, cot.at[c], 6),
    ]
    for copy in swaps:
        copy.start()
    g_qkv, g_out, g_in, g_down, g_vec = (
        Gather(p, blocks, sent.at[i], came.at[i])
        for i, blocks in enumerate((w_qkv, w_nat, w_in, w_down, tiles))
    )
    loads[0].wait()
    swaps[1].wait_recv()
    g_qkv.begin()
    loads[4].wait()
    swaps[0].wait_recv()
    tiles[own, 0:8, :] = tile[0:8, :] + tile_in[0:8, :]
    tiles[own, 8:16, :] = tile[8:16, :]
    g_vec.begin()
    loads[1].wait()
    g_out.begin()
    loads[2].wait()
    swaps[2].wait_recv()
    g_in.begin()
    loads[3].wait()
    g_down.begin()
    pump = Pump()
    for g in (g_vec, g_qkv, g_out, g_in, g_down):
        pump.add(g.steps())
    for i in (7, 8, 5):
        loads[i].wait()
    for i in (3, 4, 5):
        swaps[i].wait_recv()
    build_mask(mask, col, row)
    pump.take(7)
    g_vec.finish()
    build_vectors(vecs, hshift, tshift, tiles, c)
    tokens = tok.shape[0] * length

    def first_norm(i):
        rows = span(i, 128)
        v = tok[i // 4, span(lax.rem(i, 4), 128), :].astype(F32)
        normed, _ = stats(v)
        norm1[rows, :] = (normed * vecs[G1 : G1 + 1, :] + vecs[B1 : B1 + 1, :]).astype(BF)

    pump.loop(tokens // 128, first_norm, 0)
    pump.take(7)
    g_qkv.finish()
    stores = [load(w_qkv, qkv_o), load(norm1, norm1_o), load(vecs, vecs_o), load(mask, mask_o)]
    depth = norm1.shape[1]

    def project(i):
        cols = span(i, 256)
        w = w_qkv[:, :, cols].reshape(depth, 256)
        triple[:, cols] = (mm(norm1[...], w) + tshift[0:1, cols]).astype(BF)

    pump.loop(triple.shape[1] // 256, project, 1)
    stores.append(load(triple, triple_o))
    lse[...] = jnp.zeros_like(lse)
    pump.loop(8, functools.partial(attend_pair, triple=triple, mask=mask, attended=att, lse=lse), 1)
    stores.append(load(att, att_o))
    g_out.finish()
    half = pair.copy(w_nat.at[pl.ds(8 * (1 - c), 8)], w_out.at[:, mine], 7)
    half.start()
    keep = load(w_nat.at[pl.ds(8 * c, 8)], w_out.at[:, mine])
    keep.wait()
    half.wait_recv()
    stores.append(load(w_out, out_o))

    def send_part(i):
        rows = span(i, 256)
        return pair.copy(part.at[rows], part_in.at[rows], 8 + i)

    def mix(i):
        rows = span(i, 256)
        own_part = mm(att[rows, :], w_out[...].reshape(att.shape[1], depth))
        part[rows, :] = own_part.astype(BF)
        send_part(i).start()
        v = tok[i // 2, span(lax.rem(i, 2), 256), :].astype(F32)
        mid[rows, :] = v + own_part + vecs[OB : OB + 1, :]

    pump.loop(4, mix, 0)

    def second_norm(i):
        send_part(i).wait_recv()
        rows = span(i, 256)
        v = mid[rows, :] + part_in[rows, :].astype(F32)
        mid[rows, :] = v
        normed, inverse = stats(v)
        xhat[rows, :] = normed.astype(BF)
        lane = lax.broadcasted_iota(jnp.int32, (256, 128), 1)
        inside = span(lax.rem(i, 2), 256)
        lse[i // 2, inside, :] = jnp.where(lane < INV_AT, lse[i // 2, inside, :], inverse)
        norm2[rows, :] = (normed * vecs[G2 : G2 + 1, :] + vecs[B2 : B2 + 1, :]).astype(BF)

    pump.loop(4, second_norm, 0)
    stores += [load(xhat, xhat_o), load(lse, lse_o), load(norm2, norm2_o), load(mid.at[span(c, length)], mid_o)]
    pump.take(max(len(pump.queue) - 4, 0))
    g_in.finish()
    stores.append(load(w_in, in_o))

    def expand(i):
        cols = span(i, 256)
        w = w_in[:, :, cols].reshape(depth, 256)
        pre = mm(norm2[...], w) + hshift[0:1, cols]
        bell = 0.5 * (1.0 + lax.erf(pre * ROOT_HALF))
        hidden[:, cols] = (pre * bell).astype(BF)
        slope[:, cols] = (bell + pre * jnp.exp(-0.5 * pre * pre) * INV_ROOT_TAU).astype(BF)

    loads[6].wait()
    swaps[6].wait_recv()
    stores.append(load(cot, cot_o))
    pump.loop(hidden.shape[1] // 256, expand, 0)
    stores += [load(slope, slope_o), load(hidden, hidden_o)]

    def down_grad(i):
        cols = span(i, 256)
        grad = mm(hidden[:, cols], cot[...].reshape(tokens, depth), TN).astype(BF)
        gdown[pl.ds(pl.multiple_of(2 * i, 2), 2)] = grad.reshape(2, 128, depth)

    pump.loop(hidden.shape[1] // 256, down_grad, 1)
    stores.append(load(gdown, gdown_o))
    pump.take(len(pump.queue))
    g_down.finish()
    stores.append(load(w_down, down_o))
    for i in range(4):
        send_part(i).wait_send()
    for g in (g_vec, g_qkv, g_out, g_in, g_down):
        g.drain()
    for copy in swaps:
        copy.wait_send()
    half.wait_send()
    for store in stores:
        store.wait()


def forward_all(wqkv2, w_out, win2, w_down, tile, inputs, cotangent, col, row):
    dq, do, di = wqkv2.shape[2], w_out.shape[1], win2.shape[2]
    length, depth = inputs.shape
    tokens = 2 * length
    outs = [
        ((16, 64, dq), BF), ((8, 64, do), BF), ((16, 64, di), BF), ((16,) + w_down.shape, BF),
        ((8, depth), F32), ((tokens, depth), BF), ((tokens, dq), BF), ((tokens, dq // 3), BF), ((2, length, 128), F32),
        ((tokens, depth), BF), ((tokens, depth), BF), ((tokens, di), BF), ((2, length, depth), BF),
        ((2, length, length), BF), ((16,) + w_down.shape, BF), ((tokens, di), BF),
        ((length, depth), F32),
    ]
    scratch = [
        ((16, 64, dq), BF), ((16, 32, do), BF), ((8, 64, do), BF), ((16, 64, di), BF), ((16,) + w_down.shape, BF),
        ((16, 16, 128), F32), ((16, 128), F32), ((16, 128), F32), ((2, length, depth), BF), ((2, length, depth), BF),
        ((2, length, 128), jnp.int32), ((2, 8, length), jnp.int32), ((2, length, length), BF),
        ((8, depth), F32), ((8, di), F32), ((8, dq), F32), ((tokens, depth), BF), ((tokens, dq), BF),
        ((tokens, dq // 3), BF), ((2, length, 128), F32), ((tokens, depth), F32), ((tokens, depth), BF),
        ((tokens, depth), BF), ((tokens, depth), BF), ((tokens, depth), BF),
        ((tokens, di), BF), ((tokens, di), BF), ((16,) + w_down.shape, BF),
    ]
    return pl.pallas_call(
        forward_kernel,
        out_shape=[jax.ShapeDtypeStruct(s, d) for s, d in outs],
        in_specs=[pl.BlockSpec(memory_space=pl.ANY)] * 9,
        out_specs=[pl.BlockSpec(memory_space=pl.ANY)] * len(outs),
        scratch_shapes=[pltpu.VMEM(s, d) for s, d in scratch]
        + [
            pltpu.SemaphoreType.DMA((5, 15)),
            pltpu.SemaphoreType.DMA((5, 15)),
            pltpu.SemaphoreType.DMA((12,)),
            pltpu.SemaphoreType.DMA((12,)),
            pltpu.SemaphoreType.DMA((32,)),
        ],
        compiler_params=pltpu.CompilerParams(
            collective_id=0, has_side_effects=True, vmem_limit_bytes=67043328
        ),
        name="forward_gather",
    )(wqkv2, w_out, win2, w_down, tile, inputs, cotangent, col, row)


def attend_pair_back(i, triple, mask, lse, gatt, gtriple, sums, c):
    length = mask.shape[1]
    half = gatt.shape[1]
    pairs = half // 128
    s, pair = i // pairs, lax.rem(i, pairs)
    rows, blocks = span(s, length), span(s, length // 64)

    def at(third):
        return pl.ds(pl.multiple_of(third * half + pair * 128, 128), 128)

    q, k, v = (triple[blocks, :, at(t)].reshape(length, 128) for t in range(3))
    g = gatt[rows, at(0)]
    lane = lax.broadcasted_iota(jnp.int32, (length, 128), 1)
    low = lane < HD
    zero = jnp.zeros_like(q)
    scale = HD ** (-0.5)
    parts = []
    for h in range(2):
        mine = low if h == 0 else ~low
        scores = mm(jnp.where(mine, q, zero), k, NT) * scale + mask[s].astype(F32)
        level = jnp.sum(jnp.where(lane == pair * 2 + h, lse[s], 0.0), -1, keepdims=True)
        probs = jnp.exp(scores - level)
        grad_probs = mm(jnp.where(mine, g, zero), v, NT)
        inner = jnp.sum(probs * grad_probs, -1, keepdims=True)
        grad_scores = (probs * (grad_probs - inner)).astype(BF)
        parts.append(
            (
                mm(grad_scores, k) * scale,
                mm(grad_scores, q, TN) * scale,
                mm(probs.astype(BF), g, TN),
            )
        )
    for t in range(3):
        joined = jnp.where(low, parts[0][t], parts[1][t]).astype(BF)
        gtriple[rows, at(t)] = joined
        if t != 1:
            row = QB if t == 0 else VB
            where = pl.ds(pl.multiple_of(half * c + pair * 128, 128), 128)
            sums[row : row + 1, where] += jnp.sum(joined.astype(F32), 0, keepdims=True)


class Later:
    def __init__(self, wait):
        self.wait = wait


def backward_kernel(
    qkv_ref, out_ref, in_ref, down_ref, vecs_ref, norm1_ref, triple_ref, att_ref, lse_ref, xhat_ref, norm2_ref,
    slope_ref, cot_ref, mask_ref, gdown_ref, hidden_ref, mid_ref, tok_ref,
    qkv_o, out_o, in_o, down_o, vec_o, input_o, layer_o,
    b_qkv, b_out, b_in, b_down, b_vec,
    l_qkv, l_out, l_in, l_down, l_vec,
    f_qkv, f_out, f_in, f_down, f_vec, n_vec,
    w_qkv, w_out, area, area2, wide, vecs, att, lse, xhat, norm2, cot, mask, part, part_in, gmid, gmixed,
    gatt, gout, sums,
    sent, came, pair_sent, pair_came, local,
):
    p = Place()
    c = p.c
    length, depth = gmid.shape
    tokens, units = wide.shape
    half = depth // 2
    mine = pl.ds(pl.multiple_of(ROWS * c, ROWS), ROWS)
    theirs = pl.ds(pl.multiple_of(ROWS * (1 - c), ROWS), ROWS)
    slots = iter(range(local.shape[0]))

    def load(src, dst):
        slot = next(slots)
        pltpu.make_async_copy(src, dst, local.at[slot]).start()
        return Later(lambda: pltpu.make_async_copy(src, dst, local.at[slot]).wait())

    in_down = load(gdown_ref, b_down)
    first = [
        load(down_ref, area),
        load(hidden_ref.at[:, 0:depth], part),
        load(hidden_ref.at[:, depth:], gmixed),
        load(mid_ref, gmid),
        load(vecs_ref, vecs),
    ]
    second = [load(cot_ref, cot), load(slope_ref, wide), load(norm2_ref, norm2), load(in_ref, area2)]
    third = [load(lse_ref, lse), load(att_ref, att), load(out_ref, w_out)]
    fourth = [load(mask_ref, mask), load(qkv_ref, w_qkv)]
    p.greet()
    pair = Pair(p, pair_sent, pair_came)
    s_down, s_in, s_out, s_qkv, s_vec = (
        Scatter(p, blocks, landed, sent.at[i], came.at[i])
        for i, (blocks, landed) in enumerate(
            ((b_down, l_down), (b_in, l_in), (b_out, l_out), (b_qkv, l_qkv), (b_vec, l_vec))
        )
    )
    in_down.wait()
    s_down.begin()
    stores = []

    def put(ref):
        def write(at, value):
            ref[at, :] = value

        return write

    def end_down():
        s_down.total(put(f_down))
        stores.append(load(f_down, down_o))

    def end_in():
        s_in.total(put(f_in))
        pair.copy(f_in.at[theirs], in_o.at[c], 1).start()
        stores.append(load(f_in.at[mine], in_o.at[c]))

    def end_out():
        s_out.total(put(f_out))
        stores.append(load(f_out, out_o))

    def end_qkv():
        s_qkv.total(put(f_qkv))
        pair.copy(f_qkv.at[theirs], qkv_o.at[c], 2).start()
        stores.append(load(f_qkv.at[mine], qkv_o.at[c]))

    def end_vec():
        s_vec.total(put(f_vec))
        pair.copy(f_vec, n_vec, 9).start()
        stores.append(load(f_vec, vec_o.at[0]))

    pump = Pump()
    sums[...] = jnp.zeros_like(sums)
    b_vec[...] = jnp.zeros_like(b_vec)
    for copy in first:
        copy.wait()
    ours, yours = span(c, length), span(1 - c, length)

    def contract(rows, cols):
        w = area[:, :, cols].reshape(2, depth, 256)
        return mm(part[rows, :], w[0]) + mm(gmixed[rows, :], w[1])

    def out_theirs(i):
        cols = span(i, 256)
        xhat[length:tokens, cols] = contract(yours, cols).astype(BF)

    pump.loop(depth // 256, out_theirs, 0)
    rest = pair.copy(xhat.at[length:tokens], xhat.at[0:length], 3)
    rest.start()

    def out_ours(i):
        cols = span(i, 256)
        gmid[:, cols] = gmid[:, cols] + contract(ours, cols) + vecs[DB : DB + 1, cols]

    pump.loop(depth // 256, out_ours, 0)
    for copy in second:
        copy.wait()

    def hidden_grad(i):
        cols = span(i, 256)
        w = area[span(i, 2)].reshape(256, depth)
        grad = mm(cot[...].reshape(tokens, depth), w, NT) * wide[:, cols].astype(F32)
        low = grad.astype(BF)
        wide[:, cols] = low
        total = jnp.sum(low.astype(F32), 0, keepdims=True)
        b_vec[2 * i, 8:9, :] = total[:, 0:128]
        b_vec[2 * i + 1, 8:9, :] = total[:, 128:256]

    pump.loop(units // 256, hidden_grad, 0)

    def in_grad(i):
        cols = span(i, 256)
        b_in[span(i, 4)] = mm(norm2[:, cols], wide[...], TN).astype(BF).reshape(4, 64, units)

    pump.loop(depth // 256, in_grad, 0)
    pump.add(s_down.acrosses())
    pump.take(4)
    s_in.begin()
    rest.wait_recv()
    gmid[...] = gmid[...] + xhat[0:length, :].astype(F32)
    layer = load(gmid, layer_o)
    rest.wait_send()
    third.append(load(xhat_ref, xhat))

    def send_part(i):
        rows = span(i, 256)
        return pair.copy(part.at[rows], part_in.at[rows], 4 + i)

    def norm_grad(i):
        rows = span(i, 256)
        part[rows, :] = mm(wide[rows, :], area2[...].reshape(depth, units), NT).astype(BF)
        send_part(i).start()

    pump.loop(4, norm_grad, 0)
    norm1_in = load(norm1_ref, area.at[0:8])
    tok_in = load(tok_ref, area.at[8:12])
    triple_in = load(triple_ref, area2.at[:, :, 0 : 3 * half])
    for copy in third:
        copy.wait()

    def middle_rows(i, ours):
        s = c if ours else 1 - c
        inside = span(i, 128)
        rows = pl.ds(pl.multiple_of(s * length + i * 128, 128), 128)
        grad = part[rows, :].astype(F32) + part_in[rows, :].astype(F32)
        normed = xhat[rows, :].astype(F32)
        scaled = grad * vecs[G2 : G2 + 1, :]
        top = cot[s, inside, :].astype(F32)
        middle = top + lse[s, inside, INV_AT : INV_AT + 1] * (
            scaled
            - jnp.mean(scaled, -1, keepdims=True)
            - normed * jnp.mean(scaled * normed, -1, keepdims=True)
        )
        low = middle.astype(BF)
        gmixed[rows, :] = low
        if ours:
            gmid[inside, :] = middle
            sums[G2 : G2 + 1, :] += jnp.sum(grad * normed, 0, keepdims=True)
            sums[B2 : B2 + 1, :] += jnp.sum(grad, 0, keepdims=True)
            sums[OB : OB + 1, :] += jnp.sum(low.astype(F32), 0, keepdims=True)
            sums[DB : DB + 1, :] += jnp.sum(top, 0, keepdims=True)

    for i in range(4):
        send_part(i).wait_recv()
    layer.wait()
    pump.loop(length // 128, functools.partial(middle_rows, ours=True), 0)
    pump.loop(length // 128, functools.partial(middle_rows, ours=False), 0)

    def out_grad(i):
        cols = span(i, 256)
        gout[span(i, 4)] = mm(att[:, cols], gmixed[...], TN).astype(BF).reshape(4, 64, depth)

    pump.loop(half // 256, out_grad, 0)
    keep = load(gout.at[:, mine], b_out.at[pl.ds(8 * c, 8)])
    mate = pair.copy(gout.at[:, theirs], b_out.at[pl.ds(8 * c, 8)], 0)
    mate.start()

    def att_grad(i):
        rows = span(i, 512)
        gatt[rows, :] = mm(gmixed[rows, :], w_out[...].reshape(half, depth), NT).astype(BF)

    pump.loop(2, att_grad, 0)
    keep.wait()
    mate.wait_recv()
    pump.add(s_down.alongs())
    pump.take(4)
    s_out.begin()
    pump.add(s_in.acrosses())
    triple_in.wait()
    for copy in fourth:
        copy.wait()
    pump.loop(
        8,
        functools.partial(
            attend_pair_back, triple=area2, mask=mask, lse=lse, gatt=gatt, gtriple=wide, sums=sums, c=c
        ),
        1,
    )
    norm1_in.wait()

    def qkv_grad(i):
        cols = span(i, 256)
        normed = area[0:8, :, cols].reshape(tokens, 256)
        b_qkv[span(i, 4)] = mm(normed, wide[:, 0 : 3 * half], TN).astype(BF).reshape(4, 64, 3 * half)

    pump.loop(depth // 256, qkv_grad, 0)
    s_qkv.begin()
    pump.add([end_down])
    pump.add(s_out.acrosses())
    for i in range(4):
        send_part(i).wait_send()

    def input_grad(i, s):
        rows = pl.ds(pl.multiple_of(s * length + i * 128, 128), 128)
        return mm(wide[rows, 0 : 3 * half], w_qkv[...].reshape(depth, 3 * half), NT)

    def first_theirs(i):
        part[span(i, 128), :] = input_grad(i, 1 - c).astype(BF)

    pump.loop(length // 128, first_theirs, 0)
    last = pair.copy(part.at[0:length], part_in.at[0:length], 8)
    last.start()
    tok_in.wait()

    def first_ours(i):
        inside = span(i, 128)
        grad = input_grad(i, c) + part_in[inside, :].astype(F32)
        normed, inverse = stats(area[8 + i, :, :].astype(F32))
        scaled = grad * vecs[G1 : G1 + 1, :]
        gmid[inside, :] = gmid[inside, :] + inverse * (
            scaled
            - jnp.mean(scaled, -1, keepdims=True)
            - normed * jnp.mean(scaled * normed, -1, keepdims=True)
        )
        sums[G1 : G1 + 1, :] += jnp.sum(grad * normed, 0, keepdims=True)
        sums[B1 : B1 + 1, :] += jnp.sum(grad, 0, keepdims=True)

    last.wait_recv()
    pump.loop(length // 128, first_ours, 0)
    stores.append(load(gmid, input_o))
    for w in range(8):
        for k in range(2):
            b_vec[2 * w + k, 0:8, :] = sums[:, 128 * w : 128 * (w + 1)]
    s_vec.begin()
    for steps in (
        s_in.alongs(), s_qkv.acrosses(), s_vec.acrosses(), s_out.alongs(), [end_in, end_out], s_vec.alongs(),
        s_qkv.alongs(), [end_vec, end_qkv],
    ):
        pump.add(steps)
    pump.take(len(pump.queue))
    pair.copy(f_vec, n_vec, 9).wait_recv()
    stores.append(load(n_vec, vec_o.at[1]))
    for s in (s_down, s_in, s_out, s_qkv, s_vec):
        s.drain()
    mate.wait_send()
    last.wait_send()
    pair.copy(f_vec, n_vec, 9).wait_send()
    pair.copy(f_in.at[theirs], in_o.at[c], 1).wait()
    pair.copy(f_qkv.at[theirs], qkv_o.at[c], 2).wait()
    for store in stores:
        store.wait()


def backward_all(saved, inputs):
    (
        qkv, w_out, w_in, w_down, vecs, norm1, triple, att, lse, xhat, norm2, slope, cot, mask, gdown, hidden, mid,
    ) = saved
    length, depth = inputs.shape
    tokens = 2 * length
    dq, do, di = qkv.shape[2], w_out.shape[2], w_in.shape[2]
    down, dd = w_down.shape[1:]
    outs = [
        ((2, 32, dq), F32), ((32, do), F32), ((2, 32, di), F32), ((down, dd), F32), ((2, 16, 128), F32),
        ((length, depth), F32), ((length, depth), F32),
    ]
    blocks = [((64, dq), BF), ((32, do), BF), ((64, di), BF), ((down, dd), BF), ((16, 128), F32)]
    scratch = [((16,) + s, d) for s, d in blocks] + [((15,) + s, d) for s, d in blocks] + [(s, F32) for s, d in blocks]
    scratch += [
        ((16, 128), F32), (qkv.shape, BF), (w_out.shape, BF), (w_down.shape, BF), (w_in.shape, BF), (slope.shape, BF),
        (vecs.shape, F32), (att.shape, BF), (lse.shape, F32), (xhat.shape, BF), (norm2.shape, BF),
        (cot.shape, BF), (mask.shape, mask.dtype), ((tokens, depth), BF), ((tokens, depth), BF),
        ((length, depth), F32), ((tokens, depth), BF), ((tokens, depth // 2), BF), (w_out.shape, BF), ((8, depth), F32),
    ]
    args = (
        qkv, w_out, w_in, w_down, vecs, norm1.reshape(8, 128, depth), triple.reshape(16, 64, dq), att, lse, xhat,
        norm2, slope, cot, mask, gdown, hidden, mid, inputs.reshape(4, 128, depth),
    )
    return pl.pallas_call(
        backward_kernel,
        out_shape=[jax.ShapeDtypeStruct(s, d) for s, d in outs],
        in_specs=[pl.BlockSpec(memory_space=pl.ANY)] * len(args),
        out_specs=[pl.BlockSpec(memory_space=pl.ANY)] * len(outs),
        scratch_shapes=[pltpu.VMEM(s, d) for s, d in scratch]
        + [
            pltpu.SemaphoreType.DMA((5, 15)),
            pltpu.SemaphoreType.DMA((5, 15)),
            pltpu.SemaphoreType.DMA((10,)),
            pltpu.SemaphoreType.DMA((10,)),
            pltpu.SemaphoreType.DMA((32,)),
        ],
        compiler_params=pltpu.CompilerParams(
            collective_id=1, has_side_effects=True, vmem_limit_bytes=67043328
        ),
        name="backward_scatter",
    )(*args)

def local_split(
    inputs, segment_ids, cotangent, ln1_gain, ln1_shift, w_qkv, query_bias, value_bias, w_out, out_bias,
    ln2_gain, ln2_shift, w_in, in_bias, w_down, down_bias,
):
    c = lax.axis_index("c")
    narrow = lax.axis_index("x") * 2 + c
    length, d_model = inputs.shape
    rows = ln1_gain.shape[0]
    half = d_model // 2
    small = jnp.stack(
        [ln1_gain, ln1_shift, query_bias, value_bias, out_bias, ln2_gain, ln2_shift, down_bias]
    ).astype(F32)
    quarter = jnp.arange(4)[None, :, None] == narrow
    tile = jnp.where(quarter, small[:, None, :], 0.0).reshape(8, 128)
    tile = jnp.concatenate([tile, in_bias.astype(F32)[None], jnp.zeros((7, 128), F32)])
    wqkv2 = w_qkv.reshape(rows, 3, 2, half).transpose(2, 0, 1, 3).reshape(2, rows, -1)
    win2 = w_in.reshape(rows, 16, 2, 128).transpose(2, 0, 1, 3).reshape(2, rows, -1)
    col = jnp.broadcast_to(segment_ids[:, None], (length, 128))
    row = jnp.broadcast_to(segment_ids[None, :], (8, length))
    saved = forward_all(wqkv2, w_out, win2, w_down, tile, inputs, cotangent, col, row)
    d_qkv, d_out, d_in, d_down, d_vec, grad_input, layer_out = backward_all(saved, inputs)
    d_qkv = d_qkv.reshape(2, rows, 3, half).transpose(1, 2, 0, 3).reshape(rows, -1)
    d_in = d_in.reshape(2, rows, 16, 128).transpose(1, 2, 0, 3).reshape(rows, -1)
    eight = (d_vec[0, :8] + d_vec[1, :8]).reshape(8, 4, 32)
    eight = lax.dynamic_index_in_dim(eight, narrow, 1, False)
    return (
        layer_out, grad_input, eight[0], eight[1], d_qkv, eight[2], eight[3], d_out, eight[4],
        eight[5], eight[6], d_in, d_vec[0, 8], d_down, eight[7],
    )


def solution(mesh):
    sizes = tuple(mesh.shape.values())
    step, names = local, (("wide", "narrow"),)
    if sizes == (8, 4):
        mesh = Mesh(mesh.devices.reshape(4, 2, 2, 2), ("z", "y", "x", "c"))
        step, names = local_split, (("z", "y", "x", "c"),)
    line, plane = P(names[0]), P(names[0], None)
    return jax.shard_map(
        step,
        mesh=mesh,
        in_specs=(plane, line, plane, line, line, plane, line, line, plane, line, line, line, plane, line, plane, line),
        out_specs=(plane, plane, line, line, plane, line, line, plane, line, line, line, plane, line, plane, line),
        check_vma=False,
    )
```

```python
import functools

import jax
import jax.numpy as jnp
from jax import lax
from jax.experimental import pallas as pl
from jax.experimental.pallas import tpu as pltpu
from jax.sharding import Mesh
from jax.sharding import PartitionSpec as P

HD = 64


EPS = 1e-05
ROOT_HALF = 0.7071067811865476
INV_ROOT_TAU = 0.3989422804014327
NEG_FILL = -1000000000.0


def normalize(values, gain, shift):
    average = jnp.mean(values, -1, keepdims=True)
    centred = values - average
    inverse = lax.rsqrt(jnp.mean(centred * centred, -1, keepdims=True) + EPS)
    normed = centred * inverse
    return (normed * gain + shift, normed, inverse)


def normalize_back(grad_norm, normed, inverse, gain):
    scaled = grad_norm * gain
    return inverse * (
        scaled
        - jnp.mean(scaled, -1, keepdims=True)
        - normed * jnp.mean(scaled * normed, -1, keepdims=True)
    )


def gelu_value(pre_act):
    return 0.5 * pre_act * (1.0 + lax.erf(pre_act * ROOT_HALF))


def gelu_slope(pre_act):
    return (
        0.5 * (1.0 + lax.erf(pre_act * ROOT_HALF))
        + pre_act * jnp.exp(-0.5 * pre_act * pre_act) * INV_ROOT_TAU
    )


def gather_forward(shards):
    return (
        lax.all_gather(shards[0], ("wide", "narrow"), axis=0, tiled=True),
        lax.all_gather(shards[1], ("wide", "narrow"), axis=0, tiled=True),
        lax.all_gather(shards[2], ("wide", "narrow"), axis=0, tiled=True),
        lax.all_gather(shards[3], ("wide", "narrow"), axis=0, tiled=True),
        lax.all_gather(shards[4], ("wide", "narrow"), axis=0, tiled=True),
        lax.all_gather(shards[5], ("wide", "narrow"), axis=0, tiled=True),
        lax.all_gather(shards[6], ("wide", "narrow"), axis=0, tiled=True),
        lax.all_gather(shards[7], ("wide", "narrow"), axis=0, tiled=True),
        lax.all_gather(shards[8], ("wide", "narrow"), axis=0, tiled=True),
        lax.all_gather(shards[9], ("wide", "narrow"), axis=0, tiled=True),
        lax.all_gather(shards[10], ("wide", "narrow"), axis=0, tiled=True),
        lax.all_gather(shards[11], ("wide", "narrow"), axis=0, tiled=True),
        lax.all_gather(shards[12], ("wide", "narrow"), axis=0, tiled=True),
    )


def gather_backward(shards):
    return (
        lax.all_gather(shards[0], ("wide", "narrow"), axis=0, tiled=True),
        lax.all_gather(shards[1], ("wide", "narrow"), axis=0, tiled=True),
        lax.all_gather(shards[2], ("wide", "narrow"), axis=0, tiled=True),
        lax.all_gather(shards[3], ("wide", "narrow"), axis=0, tiled=True),
        lax.all_gather(shards[4], ("wide", "narrow"), axis=0, tiled=True),
        lax.all_gather(shards[5], ("wide", "narrow"), axis=0, tiled=True),
        lax.all_gather(shards[6], ("wide", "narrow"), axis=0, tiled=True),
        lax.all_gather(shards[7], ("wide", "narrow"), axis=0, tiled=True),
        lax.all_gather(shards[8], ("wide", "narrow"), axis=0, tiled=True),
        lax.all_gather(shards[9], ("wide", "narrow"), axis=0, tiled=True),
        lax.all_gather(shards[10], ("wide", "narrow"), axis=0, tiled=True),
        lax.all_gather(shards[11], ("wide", "narrow"), axis=0, tiled=True),
        lax.all_gather(shards[12], ("wide", "narrow"), axis=0, tiled=True),
    )


def reduce_grads(grads):
    return (
        lax.psum_scatter(grads[0], ("wide", "narrow"), scatter_dimension=0, tiled=True),
        lax.psum_scatter(grads[1], ("wide", "narrow"), scatter_dimension=0, tiled=True),
        lax.psum_scatter(grads[2], ("wide", "narrow"), scatter_dimension=0, tiled=True),
        lax.psum_scatter(grads[3], ("wide", "narrow"), scatter_dimension=0, tiled=True),
        lax.psum_scatter(grads[4], ("wide", "narrow"), scatter_dimension=0, tiled=True),
        lax.psum_scatter(grads[5], ("wide", "narrow"), scatter_dimension=0, tiled=True),
        lax.psum_scatter(grads[6], ("wide", "narrow"), scatter_dimension=0, tiled=True),
        lax.psum_scatter(grads[7], ("wide", "narrow"), scatter_dimension=0, tiled=True),
        lax.psum_scatter(grads[8], ("wide", "narrow"), scatter_dimension=0, tiled=True),
        lax.psum_scatter(grads[9], ("wide", "narrow"), scatter_dimension=0, tiled=True),
        lax.psum_scatter(grads[10], ("wide", "narrow"), scatter_dimension=0, tiled=True),
        lax.psum_scatter(grads[11], ("wide", "narrow"), scatter_dimension=0, tiled=True),
        lax.psum_scatter(grads[12], ("wide", "narrow"), scatter_dimension=0, tiled=True),
    )


def head_block(triple_b, offset, group_width, d_model):
    length = triple_b.shape[0]
    queries = triple_b[:, offset : offset + group_width].reshape(length, group_width // HD, HD)
    key_rows = triple_b[:, d_model + offset : d_model + offset + group_width].reshape(
        length, group_width // HD, HD
    )
    values = triple_b[:, 2 * d_model + offset : 2 * d_model + offset + group_width].reshape(
        length, group_width // HD, HD
    )
    return (queries, key_rows, values)


def block_scores(queries, key_rows, allowed):
    scores = jnp.einsum(
        "qhd,khd->hqk", queries, key_rows, preferred_element_type=jnp.float32
    ) * HD ** (-0.5)
    return jnp.where(allowed[None], scores, NEG_FILL)


def attend(triple_b, allowed, d_model):
    length = triple_b.shape[0]
    group_width = 4 * HD
    pieces = []
    log_totals = []
    for offset in range(0, d_model, group_width):
        queries, key_rows, values = head_block(triple_b, offset, group_width, d_model)
        scores = block_scores(queries, key_rows, allowed)
        highest = jnp.max(scores, -1, keepdims=True)
        exponent = jnp.exp(scores - highest)
        row_total = jnp.sum(exponent, -1, keepdims=True)
        probs_low = (exponent / row_total).astype(jnp.bfloat16)
        mixed = jnp.einsum("hqk,khd->qhd", probs_low, values, preferred_element_type=jnp.float32)
        pieces.append(mixed.reshape(length, group_width))
        log_totals.append(highest + jnp.log(row_total))
    return (jnp.concatenate(pieces, 1), log_totals)


def attend_back(triple_b, grad_att_b, allowed, log_totals, d_model):
    length = triple_b.shape[0]
    group_width = 4 * HD
    query_parts = []
    key_parts = []
    value_parts = []
    for index, offset in enumerate(range(0, d_model, group_width)):
        queries, key_rows, values = head_block(triple_b, offset, group_width, d_model)
        scores = block_scores(queries, key_rows, allowed)
        attn_probs = jnp.exp(scores - log_totals[index])
        probs_low = attn_probs.astype(jnp.bfloat16)
        grad_heads = grad_att_b[:, offset : offset + group_width].reshape(
            length, group_width // HD, HD
        )
        grad_probs = jnp.einsum(
            "qhd,khd->hqk", grad_heads, values, preferred_element_type=jnp.float32
        )
        inner_sum = jnp.sum(attn_probs * grad_probs, -1, keepdims=True)
        grad_scores = (attn_probs * (grad_probs - inner_sum)).astype(jnp.bfloat16)
        grad_query = jnp.einsum(
            "hqk,khd->qhd", grad_scores, key_rows, preferred_element_type=jnp.float32
        ) * HD ** (-0.5)
        grad_key = jnp.einsum(
            "hqk,qhd->khd", grad_scores, queries, preferred_element_type=jnp.float32
        ) * HD ** (-0.5)
        grad_value = jnp.einsum(
            "hqk,qhd->khd", probs_low, grad_heads, preferred_element_type=jnp.float32
        )
        query_parts.append(grad_query.reshape(length, group_width))
        key_parts.append(grad_key.reshape(length, group_width))
        value_parts.append(grad_value.reshape(length, group_width))
    return jnp.concatenate(query_parts + key_parts + value_parts, 1).astype(jnp.bfloat16)


def local(
    inputs,
    segment_ids,
    cotangent,
    ln1_gain,
    ln1_shift,
    w_qkv,
    query_bias,
    value_bias,
    w_out,
    out_bias,
    ln2_gain,
    ln2_shift,
    w_in,
    in_bias,
    w_down,
    down_bias,
):
    shards = (
        ln1_gain,
        ln1_shift,
        w_qkv,
        query_bias,
        value_bias,
        w_out,
        out_bias,
        ln2_gain,
        ln2_shift,
        w_in,
        in_bias,
        w_down,
        down_bias,
    )
    fwd_weights = gather_forward(shards)
    (
        gain_one,
        shift_one,
        qkv_full,
        qbias_full,
        vbias_full,
        outw_full,
        outb_full,
        gain_two,
        shift_two,
        inw_full,
        inb_full,
        downw_full,
        downb_full,
    ) = fwd_weights
    d_model = inputs.shape[1]
    length = inputs.shape[0]
    tokens = inputs.astype(jnp.float32)
    position = jnp.arange(length, dtype=jnp.int32)
    allowed = (segment_ids[:, None] == segment_ids[None, :]) & (segment_ids[:, None] >= 0) | (
        position[:, None] == position[None, :]
    )
    normed_out, normed_one, inverse_one = normalize(
        tokens, gain_one.astype(jnp.float32), shift_one.astype(jnp.float32)
    )
    norm_one = normed_out.astype(jnp.bfloat16)
    shifts = jnp.concatenate(
        [
            qbias_full.astype(jnp.float32),
            jnp.zeros((d_model,), jnp.float32),
            vbias_full.astype(jnp.float32),
        ]
    )
    triple_b = (jnp.dot(norm_one, qkv_full, preferred_element_type=jnp.float32) + shifts).astype(
        jnp.bfloat16
    )
    attended_f, log_totals = attend(triple_b, allowed, d_model)
    attended = attended_f.astype(jnp.bfloat16)
    middle = (
        tokens
        + jnp.dot(attended, outw_full, preferred_element_type=jnp.float32)
        + outb_full.astype(jnp.float32)
    )
    normed_out_two, normed_two, inverse_two = normalize(
        middle, gain_two.astype(jnp.float32), shift_two.astype(jnp.float32)
    )
    norm_two = normed_out_two.astype(jnp.bfloat16)
    pre_act = jnp.dot(norm_two, inw_full, preferred_element_type=jnp.float32) + inb_full.astype(
        jnp.float32
    )
    hidden = gelu_value(pre_act).astype(jnp.bfloat16)
    layer_out = (
        middle
        + jnp.dot(hidden, downw_full, preferred_element_type=jnp.float32)
        + downb_full.astype(jnp.float32)
    )
    back_weights = gather_backward(shards)
    (
        gain_one_b,
        shift_one_b,
        qkv_back,
        qbias_back,
        vbias_back,
        outw_back,
        outb_back,
        gain_two_b,
        shift_two_b,
        inw_back,
        inb_back,
        downw_back,
        downb_back,
    ) = back_weights
    grad_top = cotangent.astype(jnp.float32)
    grad_w_down = jnp.einsum("sf,sd->fd", hidden, cotangent, preferred_element_type=jnp.float32)
    grad_down_bias = jnp.sum(grad_top, 0)
    grad_hidden = jnp.einsum("sd,fd->sf", cotangent, downw_back, preferred_element_type=jnp.float32)
    grad_pre = (grad_hidden * gelu_slope(pre_act)).astype(jnp.bfloat16)
    grad_w_in = jnp.einsum("sd,sf->df", norm_two, grad_pre, preferred_element_type=jnp.float32)
    grad_in_bias = jnp.sum(grad_pre.astype(jnp.float32), 0)
    grad_norm_two = jnp.einsum("sf,df->sd", grad_pre, inw_back, preferred_element_type=jnp.float32)
    grad_ln2_gain = jnp.sum(grad_norm_two * normed_two, 0)
    grad_ln2_shift = jnp.sum(grad_norm_two, 0)
    grad_middle = grad_top + normalize_back(
        grad_norm_two, normed_two, inverse_two, gain_two_b.astype(jnp.float32)
    )
    grad_mixed = grad_middle.astype(jnp.bfloat16)
    grad_w_out = jnp.einsum("sd,se->de", attended, grad_mixed, preferred_element_type=jnp.float32)
    grad_out_bias = jnp.sum(grad_mixed.astype(jnp.float32), 0)
    grad_attended = jnp.einsum(
        "se,de->sd", grad_mixed, outw_back, preferred_element_type=jnp.float32
    ).astype(jnp.bfloat16)
    grad_triple = attend_back(triple_b, grad_attended, allowed, log_totals, d_model)
    grad_w_qkv = jnp.einsum("sd,st->dt", norm_one, grad_triple, preferred_element_type=jnp.float32)
    grad_query_bias = jnp.sum(grad_triple[:, :d_model].astype(jnp.float32), 0)
    grad_value_bias = jnp.sum(grad_triple[:, 2 * d_model :].astype(jnp.float32), 0)
    grad_norm_one = jnp.einsum(
        "st,dt->sd", grad_triple, qkv_back, preferred_element_type=jnp.float32
    )
    grad_ln1_gain = jnp.sum(grad_norm_one * normed_one, 0)
    grad_ln1_shift = jnp.sum(grad_norm_one, 0)
    grad_input = grad_middle + normalize_back(
        grad_norm_one, normed_one, inverse_one, gain_one_b.astype(jnp.float32)
    )
    owned = reduce_grads(
        (
            grad_ln1_gain,
            grad_ln1_shift,
            grad_w_qkv,
            grad_query_bias,
            grad_value_bias,
            grad_w_out,
            grad_out_bias,
            grad_ln2_gain,
            grad_ln2_shift,
            grad_w_in,
            grad_in_bias,
            grad_w_down,
            grad_down_bias,
        )
    )
    return (
        layer_out,
        grad_input,
        owned[0],
        owned[1],
        owned[2],
        owned[3],
        owned[4],
        owned[5],
        owned[6],
        owned[7],
        owned[8],
        owned[9],
        owned[10],
        owned[11],
        owned[12],
    )


MESH_ID = pl.DeviceIdType.MESH
ROWS = 32
BF, F32 = jnp.bfloat16, jnp.float32


class Place:
    def __init__(self):
        self.z = lax.axis_index("z")
        self.y = lax.axis_index("y")
        self.x = lax.axis_index("x")
        self.c = lax.axis_index("c")

    def chip(self, dz=0, dy=0, dx=0):
        z = self.z
        if dz == 2:
            z = lax.rem(z + 2, 4)
        elif dz == 1:
            z = z + 1 - 2 * lax.rem(z, 2)
        elif dz == 3:
            z = 3 - z
        y = 1 - self.y if dy else self.y
        x = 1 - self.x if dx else self.x
        return z, y, x

    def index(self, dz=0, dy=0, dx=0):
        z, y, x = self.chip(dz, dy, dx)
        return (z * 2 + y) * 2 + x

    def device(self, dz=0, dy=0, dx=0):
        z, y, x = self.chip(dz, dy, dx)
        return {"z": z, "y": y, "x": x, "c": self.c}

    def partner(self):
        return {"z": self.z, "y": self.y, "x": self.x, "c": 1 - self.c}

    def greet(self):
        barrier = pltpu.get_barrier_semaphore()
        peers = [self.device(dz=1), self.device(dz=2), self.device(dz=3)]
        peers += [self.device(dy=1), self.device(dx=1), self.partner()]
        for peer in peers:
            pl.semaphore_signal(barrier, inc=1, device_id=peer, device_id_type=MESH_ID)
        pl.semaphore_wait(barrier, len(peers))


class Pair:
    def __init__(self, place, sent, came):
        self.p, self.sent, self.came = place, sent, came

    def copy(self, src, dst, slot):
        return pltpu.make_async_remote_copy(
            src_ref=src,
            dst_ref=dst,
            send_sem=self.sent.at[slot],
            recv_sem=self.came.at[slot],
            device_id=self.p.partner(),
            device_id_type=MESH_ID,
        )


Z_AT, X_AT, Y_AT, D_AT = -1, 3, 7, 11
FAR_FIRST, BY_Y = (3, 2, 1, 0), (3, 1)


class Gather:
    def __init__(self, place, blocks, sent, came):
        self.p, self.blocks, self.sent, self.came = place, blocks, sent, came
        self.left = []

    def copy(self, block, slot, to):
        at = self.p.index(**block)
        return pltpu.make_async_remote_copy(
            src_ref=self.blocks.at[at],
            dst_ref=self.blocks.at[at],
            send_sem=self.sent.at[slot],
            recv_sem=self.came.at[slot],
            device_id=self.p.device(**to),
            device_id_type=MESH_ID,
        )

    def send(self, block, slot, to):
        self.copy(block, slot, to).start()
        self.left.append((block, slot, to))

    def wait(self, block, slot):
        self.copy(block, slot, dict(dx=1)).wait_recv()

    def begin(self):
        for dz in (1, 2, 3):
            self.send({}, Z_AT + dz, dict(dz=dz))
        self.send({}, X_AT, dict(dx=1))
        self.send({}, Y_AT, dict(dy=1))

    def alongs(self, *dzs):
        return [functools.partial(self.along, dz) for dz in dzs]

    def acrosses(self, *dzs):
        return [functools.partial(self.across, dz) for dz in dzs]

    def along(self, dz):
        self.wait(dict(dz=dz), Z_AT + dz)
        self.send(dict(dz=dz), X_AT + dz, dict(dx=1))
        self.send(dict(dz=dz), Y_AT + dz, dict(dy=1))

    def across(self, dz):
        if dz < 2:
            self.wait(dict(dz=dz, dx=1), X_AT + dz)
            self.send(dict(dz=dz, dx=1), D_AT + dz, dict(dy=1))
        else:
            self.wait(dict(dz=dz, dy=1), Y_AT + dz)
            self.send(dict(dz=dz, dy=1), D_AT + dz, dict(dx=1))

    def finish(self):
        for dz in range(4):
            if dz < 2:
                self.wait(dict(dz=dz, dy=1), Y_AT + dz)
            else:
                self.wait(dict(dz=dz, dx=1), X_AT + dz)
        for dz in range(4):
            self.wait(dict(dz=dz, dy=1, dx=1), D_AT + dz)

    def drain(self):
        for block, slot, to in self.left:
            self.copy(block, slot, to).wait_send()


PLANE = ({}, dict(dx=1), dict(dy=1), dict(dx=1, dy=1))


def line_slot(dz, k):
    return 4 * dz - 1 + k


class PlaneFirstGather(Gather):
    def line(self, k):
        for dz in (1, 2, 3):
            self.send(PLANE[k], line_slot(dz, k), dict(dz=dz))

    def begin(self):
        self.send({}, 0, dict(dx=1))
        self.send({}, 1, dict(dy=1))
        self.line(0)

    def steps(self):
        def step(k):
            self.wait(PLANE[k], k - 1)
            if k == 1:
                self.send(PLANE[1], 2, dict(dy=1))
            self.line(k)

        return [functools.partial(step, k) for k in (1, 2, 3)]

    def finish(self):
        for dz in (1, 2, 3):
            for k in range(4):
                self.wait(dict(dz=dz, **PLANE[k]), line_slot(dz, k))


class Scatter:
    def __init__(self, place, blocks, landed, sent, came):
        self.p, self.blocks, self.landed = place, blocks, landed
        self.sent, self.came = sent, came
        self.left = []

    def copy(self, block, slot, to):
        return pltpu.make_async_remote_copy(
            src_ref=self.blocks.at[self.p.index(**block)],
            dst_ref=self.landed.at[slot],
            send_sem=self.sent.at[slot],
            recv_sem=self.came.at[slot],
            device_id=self.p.device(**to),
            device_id_type=MESH_ID,
        )

    def send(self, block, slot, to):
        self.copy(block, slot, to).start()
        self.left.append((block, slot, to))

    def wait(self, slot):
        self.copy({}, slot, dict(dx=1)).wait_recv()

    def add(self, at, slots, write):
        rows = self.blocks.shape[1]
        step = 16

        def body(i, carry):
            some = pl.ds(pl.multiple_of(i * step, step), step)
            total = self.blocks[at, some, :].astype(F32)
            for slot in slots:
                total = total + self.landed[slot, some, :].astype(F32)
            write(some, total)
            return carry

        lax.fori_loop(0, rows // step, body, 0)

    def merge(self, block, slots):
        at = self.p.index(**block)

        def write(some, total):
            self.blocks[at, some, :] = total.astype(self.blocks.dtype)

        self.add(at, slots, write)

    def begin(self):
        for dz in FAR_FIRST:
            to = dict(dy=1) if dz in BY_Y else dict(dx=1)
            self.send(dict(dz=dz, dy=1, dx=1), D_AT + dz, to)
            self.send(dict(dz=dz, **to), (Y_AT if dz in BY_Y else X_AT) + dz, to)

    def across(self, dz):
        to = dict(dx=1) if dz in BY_Y else dict(dy=1)
        self.wait(D_AT + dz)
        self.merge(dict(dz=dz, **to), (D_AT + dz,))
        self.send(dict(dz=dz, **to), (X_AT if dz in BY_Y else Y_AT) + dz, to)

    def along(self, dz):
        self.wait(X_AT + dz)
        self.wait(Y_AT + dz)
        if dz:
            self.merge(dict(dz=dz), (X_AT + dz, Y_AT + dz))
            self.send(dict(dz=dz), Z_AT + dz, dict(dz=dz))

    def total(self, write):
        for dz in (1, 2, 3):
            self.wait(Z_AT + dz)
        self.add(self.p.index(), (X_AT, Y_AT, Z_AT + 1, Z_AT + 2, Z_AT + 3), write)

    def acrosses(self, *dzs):
        return [functools.partial(self.across, dz) for dz in dzs or FAR_FIRST]

    def alongs(self, *dzs):
        return [functools.partial(self.along, dz) for dz in dzs or FAR_FIRST]

    def drain(self):
        for block, slot, to in self.left:
            self.copy(block, slot, to).wait_send()


class LineFirstScatter(Scatter):
    def begin(self):
        for k in (3, 2, 1, 0):
            for dz in (3, 2, 1):
                self.send(dict(dz=dz, **PLANE[k]), line_slot(dz, k), dict(dz=dz))

    def lines(self, k):
        slots = [line_slot(dz, k) for dz in (1, 2, 3)]
        for slot in slots:
            self.wait(slot)
        if k == 1:
            self.wait(2)
            slots.append(2)
        if k:
            self.merge(PLANE[k], slots)
            self.send(PLANE[k], k - 1, dict(dx=1) if k == 1 else dict(dy=1))

    def steps(self):
        return [functools.partial(self.lines, k) for k in (3, 2, 1)]

    def total(self, write):
        self.lines(0)
        self.wait(0)
        self.wait(1)
        self.add(self.p.index(), (0, 1, line_slot(1, 0), line_slot(2, 0), line_slot(3, 0)), write)


def run(*steps):
    for step in steps:
        if isinstance(step, (list, tuple)):
            run(*step)
        else:
            step()


def loop(trips, body, after=()):
    def trip(i, carry):
        body(i)
        for k, steps in dict(after).items():

            @pl.when(i == k)
            def _(steps=steps):
                run(steps)

        return carry

    lax.fori_loop(0, trips, trip, 0)


NN = (((1,), (0,)), ((), ()))
NT = (((1,), (1,)), ((), ()))
TN = (((0,), (0,)), ((), ()))


def mm(a, b, dims=NN):
    return lax.dot_general(a, b, dims, preferred_element_type=F32)


def span(i, size):
    if isinstance(i, int):
        return pl.ds(i * size, size)
    return pl.ds(pl.multiple_of(i * size, size), size)


def stats(v):
    average = jnp.mean(v, -1, keepdims=True)
    centred = v - average
    inverse = lax.rsqrt(jnp.mean(centred * centred, -1, keepdims=True) + EPS)
    return centred * inverse, inverse


def third_at(pair, third):
    return pair * 384 + third * 128


def third_of(pair, third, core, depth):
    return third * depth + core * (depth // 2) + pair * 128


def build_mask(mask, seg_col, seg_row):
    size = mask.shape[1]
    for s in range(2):

        def body(i, carry, s=s):
            rows = span(i, 128)
            col = seg_col[s, rows, :][:, :1]
            row = seg_row[s, :1, :]
            here = lax.broadcasted_iota(jnp.int32, (128, size), 0) + i * 128
            there = lax.broadcasted_iota(jnp.int32, (128, size), 1)
            fine = ((col == row) & (col >= 0)) | (here == there)
            mask[s, rows, :] = jnp.where(fine, 0.0, NEG_FILL).astype(BF)
            return carry

        lax.fori_loop(0, size // 128, body, 0)


def build_vectors(vecs, hidden_shift, triple_shift, tiles, c):
    for w in range(8):
        vecs[0:8, 128 * w : 128 * (w + 1)] = tiles[2 * w, 0:8, :] + tiles[2 * w + 1, 0:8, :]
    for j in range(16):
        hidden_shift[0:1, 128 * j : 128 * (j + 1)] = tiles[j, 8:9, :]
    half = vecs.shape[1] // 2
    first = c == 0
    for pair in range(half // 128):
        low, high = 128 * pair, half + 128 * pair
        for third, row in enumerate((QB, None, VB)):
            at = third_at(pair, third)
            if row is None:
                triple_shift[0:1, at : at + 128] = jnp.zeros((1, 128), F32)
            else:
                triple_shift[0:1, at : at + 128] = jnp.where(
                    first, vecs[row : row + 1, low : low + 128], vecs[row : row + 1, high : high + 128]
                )


G1, B1, QB, VB, OB, G2, B2, DB = range(8)
INV_AT = 64
LINE_FROM = 640


def attend_pair(i, triple, mask, attended, lse):
    length = mask.shape[1]
    half = attended.shape[1]
    pairs = half // 128
    s, pair = i // pairs, lax.rem(i, pairs)
    rows = span(s, length)
    q, k, v = (triple[rows, pl.ds(pl.multiple_of(third_at(pair, t), 128), 128)] for t in range(3))
    lane = lax.broadcasted_iota(jnp.int32, (length, 128), 1)
    low = lane < HD
    outs = []
    kept = lse[s]
    for h in range(2):
        mine = low if h == 0 else ~low
        scores = mm(jnp.where(mine, q, jnp.zeros_like(q)), k, NT) * HD ** (-0.5) + mask[s].astype(F32)
        highest = jnp.max(scores, -1, keepdims=True)
        exponent = jnp.exp(scores - highest)
        total = jnp.sum(exponent, -1, keepdims=True)
        probs = (exponent * (1.0 / total)).astype(BF)
        outs.append(mm(probs, v))
        kept = jnp.where(lane == pair * 2 + h, highest + jnp.log(total), kept)
    lse[s] = kept
    attended[rows, pl.ds(pl.multiple_of(pair * 128, 128), 128)] = jnp.where(low, outs[0], outs[1]).astype(BF)


def forward_kernel(
    wqkv_ref, wout_ref, win_ref, wdown_ref, tile_ref, tok_ref, cot_ref, col_ref, row_ref,
    qkv_o, out_o, in_o, down_o, vecs_o, norm1_o, triple_o, att_o, lse_o, xhat_o, norm2_o, slope_o, cot_o,
    mask_o, gdown_o, hidden_o, mid_o,
    w_qkv, w_nat, w_out, w_in, w_down, tiles, tile, tile_in, tok, cot, col, row, mask,
    vecs, hshift, tshift, norm1, triple, att, lse, mid, part, part_in, norm2, xhat, hidden, slope, gdown,
    sent, came, pair_sent, pair_came, local,
):
    p = Place()
    own, c = p.index(), p.c
    length = tok.shape[1]
    mine = pl.ds(pl.multiple_of(ROWS * c, ROWS), ROWS)
    slots = iter(range(local.shape[0]))
    depth, units = norm1.shape[1], hidden.shape[1]
    pairs = att.shape[1] // 128

    def load(src, dst):
        copy = pltpu.make_async_copy(src, dst, local.at[next(slots)])
        copy.start()
        return copy

    def load_parts(parts, whole):
        slot = local.at[next(slots)]
        for src, dst in parts:
            pltpu.make_async_copy(src, dst, slot).start()
        return pltpu.make_async_copy(whole, whole, slot)

    def qkv_parts(core):
        return [
            (
                wqkv_ref.at[:, pl.ds(pl.multiple_of(third_of(i, t, core, depth), 128), 128)],
                w_qkv.at[own, mine, pl.ds(third_at(i, t), 128)],
            )
            for i in range(pairs)
            for t in range(3)
        ]

    def in_parts(core):
        return [
            (
                win_ref.at[:, pl.ds(pl.multiple_of((2 * j + core) * 128, 128), 128)],
                w_in.at[own, mine, pl.ds(128 * j, 128)],
            )
            for j in range(units // 128)
        ]

    whole_qkv, whole_in = w_qkv.at[own, mine], w_in.at[own, mine]
    loads = [
        load(tile_ref, tile),
        load_parts(qkv_parts(c), whole_qkv),
        load(wout_ref, w_nat.at[own]),
        load_parts(in_parts(c), whole_in),
        load(wdown_ref, w_down.at[own]),
        load(tok_ref, tok.at[c]),
        load(cot_ref, cot.at[c]),
        load(col_ref, col.at[c]),
        load(row_ref, row.at[c]),
    ]
    p.greet()
    pair = Pair(p, pair_sent, pair_came)
    swaps = [pair.copy(tile_ref, tile_in, 0)]
    swaps[0].start()
    for slot, parts, whole in ((1, qkv_parts(1 - c), whole_qkv), (2, in_parts(1 - c), whole_in)):
        for src, dst in parts:
            pair.copy(src, dst, slot).start()
        swaps.append(pair.copy(whole, whole, slot))
    for slot, src, dst in (
        (3, row_ref, row.at[c]), (4, col_ref, col.at[c]), (5, tok_ref, tok.at[c]), (6, cot_ref, cot.at[c])
    ):
        swaps.append(pair.copy(src, dst, slot))
        swaps[-1].start()
    g_vec, g_qkv, g_out, g_in, g_down = (
        Gather(p, blocks, sent.at[i], came.at[i])
        for i, blocks in enumerate((tiles, w_qkv, w_nat, w_in, w_down.at[:, :, 0:LINE_FROM]))
    )
    g_last = PlaneFirstGather(p, w_down.at[:, :, LINE_FROM:], sent.at[5], came.at[5])
    loads[0].wait()
    swaps[0].wait_recv()
    tiles[own, 0:8, :] = tile[0:8, :] + tile_in[0:8, :]
    tiles[own, 8:16, :] = tile[8:16, :]
    g_vec.begin()
    for g, load_of, swap_of in ((g_qkv, 1, 1), (g_out, 2, None), (g_in, 3, 2)):
        loads[load_of].wait()
        if swap_of is not None:
            swaps[swap_of].wait_recv()
        g.begin()
    run(g_vec.alongs(1, 2, 3), g_qkv.acrosses(0), g_qkv.alongs(1, 2, 3))
    loads[4].wait()
    g_down.begin()
    g_last.begin()
    run(g_vec.acrosses(0, 1, 2, 3), g_vec.finish)
    for i in (7, 8, 5):
        loads[i].wait()
    for i in (3, 4, 5):
        swaps[i].wait_recv()
    build_mask(mask, col, row)
    build_vectors(vecs, hshift, tshift, tiles, c)
    tokens = tok.shape[0] * length

    def first_norm(i):
        rows = span(i, 128)
        v = tok[i // 4, span(lax.rem(i, 4), 128), :].astype(F32)
        normed, _ = stats(v)
        norm1[rows, :] = (normed * vecs[G1 : G1 + 1, :] + vecs[B1 : B1 + 1, :]).astype(BF)

    loop(tokens // 128, first_norm)
    run(g_qkv.acrosses(1, 2, 3), g_out.acrosses(0), g_out.alongs(1, 2, 3), g_in.acrosses(0), g_qkv.finish)
    stores = [load(w_qkv, qkv_o), load(norm1, norm1_o), load(vecs, vecs_o), load(mask, mask_o)]

    def project(i):
        cols = span(i, 256)
        w = w_qkv[:, :, cols].reshape(depth, 256)
        triple[:, cols] = (mm(norm1[...], w) + tshift[0:1, cols]).astype(BF)

    last = g_last.steps()
    loop(triple.shape[1] // 256, project, {1: g_in.alongs(1), 3: last[0], 4: last[1], 5: last[2]})
    stores.append(load(triple, triple_o))
    lse[...] = jnp.zeros_like(lse)
    loop(
        8,
        functools.partial(attend_pair, triple=triple, mask=mask, attended=att, lse=lse),
        {
            0: g_out.acrosses(1), 1: g_out.acrosses(2), 2: g_out.acrosses(3), 3: g_in.alongs(2), 5: g_in.alongs(3),
            7: g_in.acrosses(1),
        },
    )
    stores.append(load(att, att_o))
    g_out.finish()
    half = pair.copy(w_nat.at[pl.ds(8 * (1 - c), 8)], w_out.at[:, mine], 7)
    half.start()
    keep = load(w_nat.at[pl.ds(8 * c, 8)], w_out.at[:, mine])
    keep.wait()
    half.wait_recv()
    stores.append(load(w_out, out_o))

    def send_part(i):
        rows = span(i, 256)
        return pair.copy(part.at[rows], part_in.at[rows], 8 + i)

    def mix(i):
        rows = span(i, 256)
        own_part = mm(att[rows, :], w_out[...].reshape(att.shape[1], depth))
        part[rows, :] = own_part.astype(BF)
        send_part(i).start()
        v = tok[i // 2, span(lax.rem(i, 2), 256), :].astype(F32)
        mid[rows, :] = v + own_part + vecs[OB : OB + 1, :]

    loop(4, mix)

    def second_norm(i):
        send_part(i).wait_recv()
        rows = span(i, 256)
        v = mid[rows, :] + part_in[rows, :].astype(F32)
        mid[rows, :] = v
        normed, inverse = stats(v)
        xhat[rows, :] = normed.astype(BF)
        lane = lax.broadcasted_iota(jnp.int32, (256, 128), 1)
        inside = span(lax.rem(i, 2), 256)
        lse[i // 2, inside, :] = jnp.where(lane < INV_AT, lse[i // 2, inside, :], inverse)
        norm2[rows, :] = (normed * vecs[G2 : G2 + 1, :] + vecs[B2 : B2 + 1, :]).astype(BF)

    loop(4, second_norm)
    stores += [load(xhat, xhat_o), load(lse, lse_o), load(norm2, norm2_o), load(mid.at[span(c, length)], mid_o)]
    run(g_in.acrosses(2, 3), g_down.acrosses(0), g_down.alongs(1), g_in.finish)
    stores.append(load(w_in, in_o))

    def expand(i):
        cols = span(i, 256)
        w = w_in[:, :, cols].reshape(depth, 256)
        pre = mm(norm2[...], w) + hshift[0:1, cols]
        bell = 0.5 * (1.0 + lax.erf(pre * ROOT_HALF))
        hidden[:, cols] = (pre * bell).astype(BF)
        slope[:, cols] = (bell + pre * jnp.exp(-0.5 * pre * pre) * INV_ROOT_TAU).astype(BF)

    loads[6].wait()
    swaps[6].wait_recv()
    stores.append(load(cot, cot_o))
    loop(units // 256, expand, {2: g_down.alongs(2), 4: g_down.alongs(3)})
    stores += [load(slope, slope_o), load(hidden, hidden_o)]

    def down_grad(i):
        cols = span(i, 256)
        grad = mm(hidden[:, cols], cot[...].reshape(tokens, depth), TN).astype(BF)
        gdown[pl.ds(pl.multiple_of(2 * i, 2), 2)] = grad.reshape(2, 128, depth)

    loop(units // 256, down_grad, {1: g_down.acrosses(1), 4: g_down.acrosses(2), 7: g_down.acrosses(3)})
    stores.append(load(gdown, gdown_o))
    run(g_down.finish, g_last.finish)
    stores.append(load(w_down, down_o))
    for i in range(4):
        send_part(i).wait_send()
    for g in (g_vec, g_qkv, g_out, g_in, g_down, g_last):
        g.drain()
    for copy in swaps:
        copy.wait_send()
    half.wait_send()
    for store in stores:
        store.wait()


def forward_all(w_qkv, w_out, w_in, w_down, tile, inputs, cotangent, col, row):
    dq, do, di = w_qkv.shape[1] // 2, w_out.shape[1], w_in.shape[1] // 2
    length, depth = inputs.shape
    tokens = 2 * length
    outs = [
        ((16, 64, dq), BF), ((8, 64, do), BF), ((16, 64, di), BF), ((16,) + w_down.shape, BF),
        ((8, depth), F32), ((tokens, depth), BF), ((tokens, dq), BF), ((tokens, dq // 3), BF), ((2, length, 128), F32),
        ((tokens, depth), BF), ((tokens, depth), BF), ((tokens, di), BF), ((2, length, depth), BF),
        ((2, length, length), BF), ((16,) + w_down.shape, BF), ((tokens, di), BF),
        ((length, depth), F32),
    ]
    scratch = [
        ((16, 64, dq), BF), ((16, 32, do), BF), ((8, 64, do), BF), ((16, 64, di), BF), ((16,) + w_down.shape, BF),
        ((16, 16, 128), F32), ((16, 128), F32), ((16, 128), F32), ((2, length, depth), BF), ((2, length, depth), BF),
        ((2, length, 128), jnp.int32), ((2, 8, length), jnp.int32), ((2, length, length), BF),
        ((8, depth), F32), ((8, di), F32), ((8, dq), F32), ((tokens, depth), BF), ((tokens, dq), BF),
        ((tokens, dq // 3), BF), ((2, length, 128), F32), ((tokens, depth), F32), ((tokens, depth), BF),
        ((tokens, depth), BF), ((tokens, depth), BF), ((tokens, depth), BF),
        ((tokens, di), BF), ((tokens, di), BF), ((16,) + w_down.shape, BF),
    ]
    return pl.pallas_call(
        forward_kernel,
        out_shape=[jax.ShapeDtypeStruct(s, d) for s, d in outs],
        in_specs=[pl.BlockSpec(memory_space=pl.ANY)] * 9,
        out_specs=[pl.BlockSpec(memory_space=pl.ANY)] * len(outs),
        scratch_shapes=[pltpu.VMEM(s, d) for s, d in scratch]
        + [
            pltpu.SemaphoreType.DMA((6, 15)),
            pltpu.SemaphoreType.DMA((6, 15)),
            pltpu.SemaphoreType.DMA((12,)),
            pltpu.SemaphoreType.DMA((12,)),
            pltpu.SemaphoreType.DMA((32,)),
        ],
        compiler_params=pltpu.CompilerParams(
            collective_id=0, has_side_effects=True, vmem_limit_bytes=67043328
        ),
        name="forward_gather",
    )(w_qkv, w_out, w_in, w_down, tile, inputs, cotangent, col, row)


def attend_pair_back(i, triple, mask, lse, gatt, gtriple, sums, c):
    length = mask.shape[1]
    half = gatt.shape[1]
    pair, s = i // 2, lax.rem(i, 2)
    rows, blocks = span(s, length), span(s, length // 64)

    def at(third):
        return pl.ds(pl.multiple_of(third_at(pair, third), 128), 128)

    q, k, v = (triple[blocks, :, at(t)].reshape(length, 128) for t in range(3))
    g = gatt[rows, span(pair, 128)]
    lane = lax.broadcasted_iota(jnp.int32, (length, 128), 1)
    low = lane < HD
    zero = jnp.zeros_like(q)
    scale = HD ** (-0.5)
    parts = []
    for h in range(2):
        mine = low if h == 0 else ~low
        scores = mm(jnp.where(mine, q, zero), k, NT) * scale + mask[s].astype(F32)
        level = jnp.sum(jnp.where(lane == pair * 2 + h, lse[s], 0.0), -1, keepdims=True)
        probs = jnp.exp(scores - level)
        grad_probs = mm(jnp.where(mine, g, zero), v, NT)
        inner = jnp.sum(probs * grad_probs, -1, keepdims=True)
        grad_scores = (probs * (grad_probs - inner)).astype(BF)
        parts.append(
            (
                mm(grad_scores, k) * scale,
                mm(grad_scores, q, TN) * scale,
                mm(probs.astype(BF), g, TN),
            )
        )
    for t in range(3):
        joined = jnp.where(low, parts[0][t], parts[1][t]).astype(BF)
        gtriple[rows, at(t)] = joined
        if t != 1:
            row = QB if t == 0 else VB
            where = pl.ds(pl.multiple_of(half * c + pair * 128, 128), 128)
            sums[row : row + 1, where] += jnp.sum(joined.astype(F32), 0, keepdims=True)


class Later:
    def __init__(self, wait):
        self.wait = wait


def backward_kernel(
    qkv_ref, out_ref, in_ref, down_ref, vecs_ref, norm1_ref, triple_ref, att_ref, lse_ref, xhat_ref, norm2_ref,
    slope_ref, cot_ref, mask_ref, gdown_ref, hidden_ref, mid_ref, tok_ref,
    qkv_o, out_o, in_o, down_o, vec_o, input_o, layer_o,
    b_qkv, b_out, b_in, b_down, b_vec,
    l_qkv, l_out, l_in, l_down, l_vec,
    f_qkv, f_out, f_in, f_down, f_vec, n_vec,
    w_qkv, w_out, area, area2, wide, vecs, att, lse, xhat, norm2, cot, mask, part, part_in, gmid, gmixed,
    gatt, gout, sums,
    sent, came, pair_sent, pair_came, local,
):
    p = Place()
    c = p.c
    length, depth = gmid.shape
    tokens, units = wide.shape
    half = depth // 2
    mine = pl.ds(pl.multiple_of(ROWS * c, ROWS), ROWS)
    theirs = pl.ds(pl.multiple_of(ROWS * (1 - c), ROWS), ROWS)
    slots = iter(range(local.shape[0]))

    def load(src, dst):
        slot = next(slots)
        pltpu.make_async_copy(src, dst, local.at[slot]).start()
        return Later(lambda: pltpu.make_async_copy(src, dst, local.at[slot]).wait())

    in_down = load(gdown_ref, b_down)
    first = [
        load(down_ref, area),
        load(hidden_ref.at[:, 0:depth], part),
        load(hidden_ref.at[:, depth:], gmixed),
        load(mid_ref, gmid),
        load(vecs_ref, vecs),
    ]
    second = [load(cot_ref, cot), load(slope_ref, wide), load(norm2_ref, norm2), load(in_ref, area2)]
    third = [load(lse_ref, lse), load(att_ref, att), load(out_ref, w_out)]
    fourth = [load(mask_ref, mask), load(qkv_ref, w_qkv)]
    p.greet()
    pair = Pair(p, pair_sent, pair_came)
    trees = [
        (b_down.at[:, :, 0:LINE_FROM], l_down.at[:, :, 0:LINE_FROM]),
        (b_in, l_in),
        (b_out, l_out),
        (b_vec, l_vec),
    ]
    cuts = [(0, 768), (768, 1152), (1152, 1536)]
    trees += [(b_qkv.at[:, :, low:high], l_qkv.at[:, :, low:high]) for low, high in cuts]
    every = [Scatter(p, blocks, landed, sent.at[i], came.at[i]) for i, (blocks, landed) in enumerate(trees)]
    s_down, s_in, s_out, s_vec, *s_qkv = every
    s_line = LineFirstScatter(p, b_down.at[:, :, LINE_FROM:], l_down.at[:, :, LINE_FROM:], sent.at[7], came.at[7])
    every.append(s_line)
    in_down.wait()
    s_line.begin()
    s_down.begin()
    stores = []

    def put(ref):
        def write(at, value):
            ref[at, :] = value

        return write

    def end_down():
        s_down.total(put(f_down.at[:, 0:LINE_FROM]))
        s_line.total(put(f_down.at[:, LINE_FROM:]))
        stores.append(load(f_down, down_o))

    def parts_out(ref, out, places, slot):
        here = next(slots)
        for at, place in places:
            to = out.at[:, pl.ds(pl.multiple_of(place, 128), 128)]
            pltpu.make_async_copy(ref.at[mine, pl.ds(at, 128)], to, local.at[here]).start()
            pair.copy(ref.at[theirs, pl.ds(at, 128)], to, slot).start()
        size = 128 * len(places)

        def wait():
            low = places[0][0]
            some = ref.at[mine, pl.ds(low, size)]
            pltpu.make_async_copy(some, some, local.at[here]).wait()
            pair.copy(some, some, slot).wait()

        stores.append(Later(wait))

    def end_in():
        s_in.total(put(f_in))
        parts_out(f_in, in_o, [(128 * j, (2 * j + c) * 128) for j in range(units // 128)], 1)

    def end_out():
        s_out.total(put(f_out))
        stores.append(load(f_out, out_o))

    def end_qkv(n):
        low, high = cuts[n]
        s_qkv[n].total(put(f_qkv.at[:, low:high]))
        places = [
            (third_at(i, t), third_of(i, t, c, depth)) for i in range(low // 384, high // 384) for t in range(3)
        ]
        parts_out(f_qkv, qkv_o, places, 10 + n)

    def end_vec():
        s_vec.total(put(f_vec))
        pair.copy(f_vec, n_vec, 9).start()
        stores.append(load(f_vec, vec_o.at[0]))

    sums[...] = jnp.zeros_like(sums)
    b_vec[...] = jnp.zeros_like(b_vec)
    for copy in first:
        copy.wait()
    ours, yours = span(c, length), span(1 - c, length)

    def contract(rows, cols):
        w = area[:, :, cols].reshape(2, depth, 256)
        return mm(part[rows, :], w[0]) + mm(gmixed[rows, :], w[1])

    def out_theirs(i):
        cols = span(i, 256)
        xhat[length:tokens, cols] = contract(yours, cols).astype(BF)

    loop(depth // 256, out_theirs)
    rest = pair.copy(xhat.at[length:tokens], xhat.at[0:length], 3)
    rest.start()

    def out_ours(i):
        cols = span(i, 256)
        gmid[:, cols] = gmid[:, cols] + contract(ours, cols) + vecs[DB : DB + 1, cols]

    loop(depth // 256, out_ours)
    for copy in second:
        copy.wait()

    def hidden_grad(i):
        cols = span(i, 256)
        w = area[span(i, 2)].reshape(256, depth)
        grad = mm(cot[...].reshape(tokens, depth), w, NT) * wide[:, cols].astype(F32)
        low = grad.astype(BF)
        wide[:, cols] = low
        total = jnp.sum(low.astype(F32), 0, keepdims=True)
        b_vec[2 * i, 8:9, :] = total[:, 0:128]
        b_vec[2 * i + 1, 8:9, :] = total[:, 128:256]

    loop(units // 256, hidden_grad)

    def in_grad(i):
        cols = span(i, 256)
        b_in[span(i, 4)] = mm(norm2[:, cols], wide[...], TN).astype(BF).reshape(4, 64, units)

    loop(depth // 256, in_grad)
    line = s_line.steps()
    run(s_down.acrosses(), s_in.begin, line[0])
    rest.wait_recv()
    gmid[...] = gmid[...] + xhat[0:length, :].astype(F32)
    layer = load(gmid, layer_o)
    rest.wait_send()
    third.append(load(xhat_ref, xhat))

    def send_part(i):
        rows = span(i, 256)
        return pair.copy(part.at[rows], part_in.at[rows], 4 + i)

    def norm_grad(i):
        rows = span(i, 256)
        part[rows, :] = mm(wide[rows, :], area2[...].reshape(depth, units), NT).astype(BF)
        send_part(i).start()

    loop(4, norm_grad)
    run(s_down.alongs(), line[1])
    norm1_in = load(norm1_ref, area.at[0:8])
    tok_in = load(tok_ref, area.at[8:12])
    triple_in = load(triple_ref, area2.at[:, :, 0 : 3 * half])
    for copy in third:
        copy.wait()

    def middle_rows(i, ours):
        s = c if ours else 1 - c
        inside = span(i, 128)
        rows = pl.ds(pl.multiple_of(s * length + i * 128, 128), 128)
        grad = part[rows, :].astype(F32) + part_in[rows, :].astype(F32)
        normed = xhat[rows, :].astype(F32)
        scaled = grad * vecs[G2 : G2 + 1, :]
        top = cot[s, inside, :].astype(F32)
        middle = top + lse[s, inside, INV_AT : INV_AT + 1] * (
            scaled
            - jnp.mean(scaled, -1, keepdims=True)
            - normed * jnp.mean(scaled * normed, -1, keepdims=True)
        )
        low = middle.astype(BF)
        gmixed[rows, :] = low
        if ours:
            gmid[inside, :] = middle
            sums[G2 : G2 + 1, :] += jnp.sum(grad * normed, 0, keepdims=True)
            sums[B2 : B2 + 1, :] += jnp.sum(grad, 0, keepdims=True)
            sums[OB : OB + 1, :] += jnp.sum(low.astype(F32), 0, keepdims=True)
            sums[DB : DB + 1, :] += jnp.sum(top, 0, keepdims=True)

    for i in range(4):
        send_part(i).wait_recv()
    layer.wait()
    loop(length // 128, functools.partial(middle_rows, ours=True))
    loop(length // 128, functools.partial(middle_rows, ours=False))

    def out_grad(i):
        cols = span(i, 256)
        gout[span(i, 4)] = mm(att[:, cols], gmixed[...], TN).astype(BF).reshape(4, 64, depth)

    loop(half // 256, out_grad)
    keep = load(gout.at[:, mine], b_out.at[pl.ds(8 * c, 8)])
    mate = pair.copy(gout.at[:, theirs], b_out.at[pl.ds(8 * c, 8)], 0)
    mate.start()

    def att_grad(i):
        rows = span(i, 512)
        gatt[rows, :] = mm(gmixed[rows, :], w_out[...].reshape(half, depth), NT).astype(BF)

    loop(2, att_grad)
    keep.wait()
    mate.wait_recv()
    run(s_in.acrosses(3, 2), s_out.begin, line[2])
    triple_in.wait()
    for copy in fourth:
        copy.wait()
    attend_back = functools.partial(
        attend_pair_back, triple=area2, mask=mask, lse=lse, gatt=gatt, gtriple=wide, sums=sums, c=c
    )
    norm1_in.wait()

    def qkv_grad(i, cut):
        cols = span(i, 256)
        normed = area[0:8, :, cols].reshape(tokens, 256)
        grad = mm(normed, wide[:, 768 * cut : 768 * (cut + 1)], TN).astype(BF)
        b_qkv[span(i, 4), :, 768 * cut : 768 * (cut + 1)] = grad.reshape(4, 64, 768)

    loop(4, attend_back, {0: s_in.acrosses(1), 1: s_in.acrosses(0)})
    loop(depth // 256, functools.partial(qkv_grad, cut=0))
    run(s_qkv[0].begin)
    loop(4, lambda i: attend_back(i + 4), {0: s_in.alongs(3), 1: s_in.alongs(2), 2: s_in.alongs(1), 3: s_in.alongs(0)})
    run(s_out.acrosses())
    for i in range(4):
        send_part(i).wait_send()

    def input_grad(i, s):
        rows = pl.ds(pl.multiple_of(s * length + i * 128, 128), 128)
        return mm(wide[rows, 0 : 3 * half], w_qkv[...].reshape(depth, 3 * half), NT)

    def first_theirs(i):
        part[span(i, 128), :] = input_grad(i, 1 - c).astype(BF)

    loop(length // 128, first_theirs)
    last = pair.copy(part.at[0:length], part_in.at[0:length], 8)
    last.start()
    loop(depth // 256, functools.partial(qkv_grad, cut=1))
    run(s_qkv[1].begin)
    tok_in.wait()

    def first_ours(i):
        inside = span(i, 128)
        grad = input_grad(i, c) + part_in[inside, :].astype(F32)
        normed, inverse = stats(area[8 + i, :, :].astype(F32))
        scaled = grad * vecs[G1 : G1 + 1, :]
        gmid[inside, :] = gmid[inside, :] + inverse * (
            scaled
            - jnp.mean(scaled, -1, keepdims=True)
            - normed * jnp.mean(scaled * normed, -1, keepdims=True)
        )
        sums[G1 : G1 + 1, :] += jnp.sum(grad * normed, 0, keepdims=True)
        sums[B1 : B1 + 1, :] += jnp.sum(grad, 0, keepdims=True)

    last.wait_recv()
    loop(length // 128, first_ours)
    stores.append(load(gmid, input_o))
    for w in range(8):
        for k in range(2):
            b_vec[2 * w + k, 0:8, :] = sums[:, 128 * w : 128 * (w + 1)]
    run(
        s_vec.begin, s_qkv[2].begin, s_qkv[0].acrosses(), end_down, s_out.alongs(), end_in, s_qkv[0].alongs(),
        s_qkv[1].acrosses(), s_vec.acrosses(), s_qkv[2].acrosses(), end_out, s_qkv[1].alongs(), s_vec.alongs(),
        s_qkv[2].alongs(), functools.partial(end_qkv, 0), functools.partial(end_qkv, 1), end_vec,
        functools.partial(end_qkv, 2),
    )
    pair.copy(f_vec, n_vec, 9).wait_recv()
    stores.append(load(n_vec, vec_o.at[1]))
    for s in every:
        s.drain()
    mate.wait_send()
    last.wait_send()
    pair.copy(f_vec, n_vec, 9).wait_send()
    for store in stores:
        store.wait()


def backward_all(saved, inputs):
    (
        qkv, w_out, w_in, w_down, vecs, norm1, triple, att, lse, xhat, norm2, slope, cot, mask, gdown, hidden, mid,
    ) = saved
    length, depth = inputs.shape
    tokens = 2 * length
    dq, do, di = qkv.shape[2], w_out.shape[2], w_in.shape[2]
    down, dd = w_down.shape[1:]
    outs = [
        ((32, 2 * dq), F32), ((32, do), F32), ((32, 2 * di), F32), ((down, dd), F32), ((2, 16, 128), F32),
        ((length, depth), F32), ((length, depth), F32),
    ]
    blocks = [((64, dq), BF), ((32, do), BF), ((64, di), BF), ((down, dd), BF), ((16, 128), F32)]
    scratch = [((16,) + s, d) for s, d in blocks] + [((15,) + s, d) for s, d in blocks] + [(s, F32) for s, d in blocks]
    scratch += [
        ((16, 128), F32), (qkv.shape, BF), (w_out.shape, BF), (w_down.shape, BF), (w_in.shape, BF), (slope.shape, BF),
        (vecs.shape, F32), (att.shape, BF), (lse.shape, F32), (xhat.shape, BF), (norm2.shape, BF),
        (cot.shape, BF), (mask.shape, mask.dtype), ((tokens, depth), BF), ((tokens, depth), BF),
        ((length, depth), F32), ((tokens, depth), BF), ((tokens, depth // 2), BF), (w_out.shape, BF), ((8, depth), F32),
    ]
    args = (
        qkv, w_out, w_in, w_down, vecs, norm1.reshape(8, 128, depth), triple.reshape(16, 64, dq), att, lse, xhat,
        norm2, slope, cot, mask, gdown, hidden, mid, inputs.reshape(4, 128, depth),
    )
    return pl.pallas_call(
        backward_kernel,
        out_shape=[jax.ShapeDtypeStruct(s, d) for s, d in outs],
        in_specs=[pl.BlockSpec(memory_space=pl.ANY)] * len(args),
        out_specs=[pl.BlockSpec(memory_space=pl.ANY)] * len(outs),
        scratch_shapes=[pltpu.VMEM(s, d) for s, d in scratch]
        + [
            pltpu.SemaphoreType.DMA((8, 15)),
            pltpu.SemaphoreType.DMA((8, 15)),
            pltpu.SemaphoreType.DMA((13,)),
            pltpu.SemaphoreType.DMA((13,)),
            pltpu.SemaphoreType.DMA((32,)),
        ],
        compiler_params=pltpu.CompilerParams(
            collective_id=1, has_side_effects=True, vmem_limit_bytes=67043328
        ),
        name="backward_scatter",
    )(*args)

def local_split(
    inputs, segment_ids, cotangent, ln1_gain, ln1_shift, w_qkv, query_bias, value_bias, w_out, out_bias,
    ln2_gain, ln2_shift, w_in, in_bias, w_down, down_bias,
):
    c = lax.axis_index("c")
    narrow = lax.axis_index("x") * 2 + c
    length, d_model = inputs.shape
    small = jnp.stack(
        [ln1_gain, ln1_shift, query_bias, value_bias, out_bias, ln2_gain, ln2_shift, down_bias]
    ).astype(F32)
    quarter = jnp.arange(4)[None, :, None] == narrow
    tile = jnp.where(quarter, small[:, None, :], 0.0).reshape(8, 128)
    tile = jnp.concatenate([tile, in_bias.astype(F32)[None], jnp.zeros((7, 128), F32)])
    col = jnp.broadcast_to(segment_ids[:, None], (length, 128))
    row = jnp.broadcast_to(segment_ids[None, :], (8, length))
    saved = forward_all(w_qkv, w_out, w_in, w_down, tile, inputs, cotangent, col, row)
    d_qkv, d_out, d_in, d_down, d_vec, grad_input, layer_out = backward_all(saved, inputs)
    eight = (d_vec[0, :8] + d_vec[1, :8]).reshape(8, 4, 32)
    eight = lax.dynamic_index_in_dim(eight, narrow, 1, False)
    return (
        layer_out, grad_input, eight[0], eight[1], d_qkv, eight[2], eight[3], d_out, eight[4],
        eight[5], eight[6], d_in, d_vec[0, 8], d_down, eight[7],
    )


def solution(mesh):
    sizes = tuple(mesh.shape.values())
    step, names = local, (("wide", "narrow"),)
    if sizes == (8, 4):
        mesh = Mesh(mesh.devices.reshape(4, 2, 2, 2), ("z", "y", "x", "c"))
        step, names = local_split, (("z", "y", "x", "c"),)
    line, plane = P(names[0]), P(names[0], None)
    return jax.shard_map(
        step,
        mesh=mesh,
        in_specs=(plane, line, plane, line, line, plane, line, line, plane, line, line, line, plane, line, plane, line),
        out_specs=(plane, plane, line, line, plane, line, line, plane, line, line, line, plane, line, plane, line),
        check_vma=False,
    )
```
